256 devices in a mesh: row: 8 (over y, z_hi), col: 4 (over x), layer: 8 (over z_lo, core).
Axes of the slice: x: 4, y: 4, z: 8 (z_hi: 2, z_lo: 4; z = z_hi * 4 + z_lo), core: 2. Of those that a mesh axis runs over, the one named last changes fastest.
Arguments:
- coeffs: float32 [4096, 4096], P(('row', 'col'), 'layer'), may hold values from -6 to 6
- hblocks: float32 [256, 128, 128], P('layer'), may hold values from -0.1875 to 0.1875
- hcount: int32 [32], replicated, may hold values from 1 to 16, 256 in all
- hcols: int32 [256], P('layer'), may hold values from 0 to 31
Outputs:
- sigma: float32 [4096, 4096], P(('row', 'col'), 'layer')
The draws below stay inside these ranges and needn't reach their ends.
Inputs may be any that keep to these rules, and one draw needn't show every extreme that they name: `hcount`: the blocks of a row stand together in hcols and hblocks, rows in order; the counts sum to 256 and some row holds 16. `hcols`: a row may name a column more than once; such blocks add.
All inputs are finite; a program needn't handle non-finite values.
Results may differ from the reference program's by a relative error of at most 0.00007.
Values sent between devices are 32-bit elements; how exact they have to be, the bound alone decides.
No kernel may reach another device: no remote copies, remote signals or barrier semaphores. Data moves between devices by JAX's collectives and lax.ppermute only.
A program may use at most 64 MiB of HBM per device.

```python
import math
import jax
import jax.numpy as jnp
import numpy as np
from jax import lax

NSTR = 4096
BLK = 128
NBLK = 32
NZ = 256
MOST = 16


def set_ends(entries, own_key, least, top_value):
    spot = [jax.random.randint(jax.random.fold_in(own_key, axis), (), 0, length) for axis, length in enumerate(entries.shape)]
    main_axis = entries.shape.index(max(entries.shape))
    beside = spot[:main_axis] + [(spot[main_axis] + 1) % entries.shape[main_axis]] + spot[main_axis + 1:]
    return entries.at[tuple(spot)].set(least).at[tuple(beside)].set(top_value)


def shard_levels(own_key, shape, split, low, top_value):
    loudness = 1.0
    for axis_at, parts in split:
        draws = jax.random.uniform(jax.random.fold_in(jax.random.fold_in(own_key, 6), axis_at), (parts,), jnp.float32, low / len(split), top_value / len(split))
        loudness = loudness * jnp.repeat(jnp.exp(draws), shape[axis_at] // parts).reshape((-1,) + (1,) * (len(shape) - 1 - axis_at))
    return loudness


def profile(number_of, total, reach, lean):
    weights = [(1 << 20) // math.isqrt(rank ** lean) + 1 for rank in range(2, number_of + 1)]
    surplus, given = total - reach - (number_of - 1), [1] * (number_of - 1)
    while surplus > 0:
        movable = [i for i in range(number_of - 1) if given[i] < reach]
        whole, remaining = sum([weights[i] for i in movable]), surplus
        for i in movable:
            more = min(reach - given[i], max(1, remaining * weights[i] // whole), surplus)
            given[i] = given[i] + more
            surplus = surplus - more
    return np.array([reach] + given)


def ragged(own_key, number_of, total, reach, skew):
    if number_of == 2:
        one = jax.random.randint(own_key, (), max(1, total - reach), min(reach, total - 1) + 1)
        return jnp.stack([one, total - one])
    lengths = jnp.asarray(profile(number_of, total, reach, skew), jnp.int32)
    pairs = (number_of - 1) // 2
    donor, sink = lengths[1:1 + 2 * pairs:2], lengths[2:2 + 2 * pairs:2]
    margin = jnp.minimum(donor - 1, reach - sink)
    moved = jax.random.randint(jax.random.fold_in(own_key, 1), (pairs,), 0, 1 << 20) % (margin + 1)
    lengths = lengths.at[1:1 + 2 * pairs:2].set(donor - moved).at[2:2 + 2 * pairs:2].set(sink + moved)
    return lengths[jax.random.permutation(jax.random.fold_in(own_key, 2), number_of)]


def centred(rng, dims, scale, bound, shards=(), kind=jnp.bfloat16):
    entries = jax.random.normal(rng, dims, jnp.float32) * scale
    if len(shards) > 0:
        entries = shard_levels(rng, dims, shards, -0.22, 0.18) * entries
    return jnp.clip(entries, min=-bound, max=bound).astype(kind)


def setup_inputs(seed: int = 0) -> dict:
    key_list = jax.random.split(jax.random.key(seed), 5)
    coeffs = centred(key_list[0], (NSTR, NSTR), 1.0, 6.0, ((0, 32), (1, 8)), jnp.float32)
    hblocks = centred(key_list[1], (NZ, BLK, BLK), (BLK * NZ // NBLK) ** -0.5, 0.1875, ((0, 8),), jnp.float32)
    hcount = ragged(key_list[2], NBLK, NZ, MOST, 2).astype(jnp.int32)
    hcols = set_ends(jax.random.randint(key_list[3], (NZ,), 0, NBLK), jax.random.fold_in(key_list[3], 1), 0, NBLK - 1).astype(jnp.int32)
    return dict(coeffs=coeffs, hblocks=hblocks, hcount=hcount, hcols=hcols)


def reference(coeffs, hblocks, hcount, hcols):
    row_end = jnp.cumsum(hcount).astype(jnp.int32)
    stored = jnp.arange(NZ, dtype=jnp.int32)
    owners = jnp.sum((row_end[None, :] <= stored[:, None]).astype(jnp.int32), axis=1).astype(jnp.int32)
    tiled = jnp.zeros((NBLK, NBLK, BLK, BLK), jnp.float32).at[owners, hcols].add(hblocks)
    hamiltonian = tiled.transpose(0, 2, 1, 3).reshape(NSTR, NSTR)
    beta_side = jnp.dot(coeffs, hamiltonian.T, precision=lax.Precision.HIGHEST, preferred_element_type=jnp.float32)
    alpha_side = jnp.dot(hamiltonian, coeffs, precision=lax.Precision.HIGHEST, preferred_element_type=jnp.float32)
    return beta_side + alpha_side
```

```python
import functools

import jax
import jax.numpy as jnp
from jax import lax
from jax.experimental import pallas as pl
from jax.experimental.pallas import tpu as pltpu
from jax.sharding import Mesh
from jax.sharding import PartitionSpec as P

ROWS = ("y", "h", "x")
ANY = pl.BlockSpec(memory_space=pl.ANY)
VMEM = pl.BlockSpec(memory_space=pltpu.VMEM)
SMEM = pl.BlockSpec(memory_space=pltpu.SMEM)
F32 = jnp.float32
BF16 = jnp.bfloat16


def params(mib):
    return pltpu.CompilerParams(vmem_limit_bytes=mib << 20)


def cost(flops, moved):
    return pl.CostEstimate(flops=flops, bytes_accessed=moved, transcendentals=0)


def shape(*dims):
    return jax.ShapeDtypeStruct(dims, F32)


def prep_kernel(where, c_ref, at_ref, keep_ref, send_ref):
    core = where[3]
    for t in range(4):
        turned = jnp.transpose(c_ref[:, 128 * t : 128 * (t + 1)]).reshape(8, 16, 128)
        at_ref[8 * t : 8 * (t + 1), 0] = turned
        at_ref[8 * t : 8 * (t + 1), 1] = turned
    for q in range(2):
        for t in range(4):
            span = slice(128 * t, 128 * (t + 1))
            mine = pl.multiple_of(64 * q + 32 * core, 32)
            other = pl.multiple_of(64 * q + 32 * (1 - core), 32)
            keep_ref[q, t] = c_ref[pl.ds(mine, 32), span]
            send_ref[q, t] = c_ref[pl.ds(other, 32), span]


def product_kernel(
    where, cols, owners, b0, b1, b2, b3, at_ref, h0, h1, h2, h3, oa_ref, ob0, ob1, ob2, ob3,
    beta, alpha, stack, hbuf, acc, sem_a, sem_h,
):
    y, x, z = where[0], where[1], where[2]
    parts = (b0, b1, b2, b3)
    loads = []
    for k in range(4):
        home = jnp.bitwise_and(z - k + 4, 3)
        loads.append(
            pltpu.make_async_copy(parts[k], beta.at[pl.ds(8 * home, 8)], sem_a.at[k])
        )
    loads.append(pltpu.make_async_copy(at_ref, alpha, sem_a.at[4]))
    for load in loads:
        load.start()
    chunks = []
    for g, h in enumerate((h0, h1, h2, h3)):
        for half in range(2):
            chunks.append(
                pltpu.make_async_copy(
                    h.at[pl.ds(16 * half, 16)],
                    hbuf.at[pl.ds(32 * g + 16 * half, 16)],
                    sem_h.at[2 * g + half],
                )
            )
    for chunk in chunks:
        chunk.start()
    acc[...] = jnp.zeros_like(acc)
    for load in loads:
        load.wait()

    @pl.loop(0, 32)
    def _(j):
        for row, source in ((0, beta), (32, alpha)):
            value = source[j]
            high = value.astype(BF16)
            stack[j, row : row + 32] = high
            stack[j, 64 + row : 96 + row] = (value - high.astype(F32)).astype(BF16)

    def place(g, i):
        if g < 2:
            return 32 * g + i
        ys, xs, b = i // 8, (i // 2) % 4, i % 2
        dy = jnp.where(ys == 1, 3, jnp.where(ys == 0, 0, ys - 1))
        dx = jnp.where(xs == 1, 3, jnp.where(xs == 0, 0, xs - 1))
        return (
            32 * g
            + 8 * jnp.bitwise_and(y + dy, 3)
            + 2 * jnp.bitwise_and(x + dx, 3)
            + b
        )

    contract = (((1,), (1,)), ((), ()))
    for n, chunk in enumerate(chunks):
        chunk.wait()
        g, first = n // 2, 16 * (n % 2)

        @pl.loop(0, 4)
        def _(step, g=g, first=first):
            terms = []
            for u in range(4):
                i = first + 4 * step + u
                at = place(g, i)
                block = hbuf[32 * g + i]
                high = block.astype(BF16)
                low = (block - high.astype(F32)).astype(BF16)
                left = stack[cols[at]]
                one = lax.dot_general(left, high, contract, preferred_element_type=F32)
                two = lax.dot_general(left[:64], low, contract, preferred_element_type=F32)
                terms.append((owners[at], one[:64] + (one[64:] + two)))
            for owner, term in terms:
                acc[owner] += term

    for i in range(32):
        oa_ref[i] = acc[i, 32:]
    for k, out in enumerate((ob0, ob1, ob2, ob3)):
        home = 8 * jnp.bitwise_and(z + k, 3)
        for j in range(8):
            out[j] = acc[home + j, :32]


def middle_kernel(where, r0, r1, r2, r3, keep_ref, send_ref):
    core = where[3]
    for slot, (one, two) in enumerate(((r0, r2), (r1, r3))):
        for t in range(4):
            mine, other = 4 * core + t, 4 * (1 - core) + t
            keep_ref[slot, t] = one[mine] + two[mine]
            send_ref[slot, t] = one[other] + two[other]


def final_kernel(where, ar_ref, keep_ref, got_ref, out_ref):
    q, core = jnp.bitwise_and(where[2], 1), where[3]
    for t in range(4):
        span = slice(128 * t, 128 * (t + 1))
        total = ar_ref[8 * t : 8 * (t + 1), 0] + ar_ref[8 * t : 8 * (t + 1), 1]
        out_ref[:, span] = jnp.transpose(total.reshape(128, 128))
        for slot in range(2):
            base = 64 * jnp.bitwise_xor(q, slot)
            mine = pl.ds(pl.multiple_of(base + 32 * core, 32), 32)
            other = pl.ds(pl.multiple_of(base + 32 * (1 - core), 32), 32)
            out_ref[mine, span] += keep_ref[slot, t]
            out_ref[other, span] += got_ref[slot, t]


def shift(value, axis, by):
    return lax.ppermute(value, axis, [(i, (i + by) % 4) for i in range(4)])


def swap(value):
    return lax.ppermute(value, "c", [(0, 1), (1, 0)])


def pair(value):
    return lax.ppermute(value, "z", [(0, 1), (1, 0), (2, 3), (3, 2)])


def ring(value, axis):
    half = value.shape[0] // 2
    down, up = shift(value, axis, 1), shift(value, axis, -1)
    far = shift(down[:half], axis, 1), shift(up[half:], axis, -1)
    return jnp.concatenate((value, down, up) + far, axis=0)


def local(coeffs, hblocks, hcount, hcols):
    y, x, z, c = (lax.axis_index(n) for n in ("y", "x", "z", "c"))
    where = jnp.stack([y, x, z, c]).astype(jnp.int32)

    at, keep, send = pl.pallas_call(
        prep_kernel,
        out_shape=(shape(32, 2, 16, 128), shape(2, 4, 32, 128), shape(2, 4, 32, 128)),
        in_specs=[SMEM, VMEM],
        out_specs=(VMEM, VMEM, VMEM),
        compiler_params=params(16),
        cost_estimate=cost(0, 1 << 20),
        name="prep",
    )(where, coeffs)

    moved = lax.all_to_all(at.reshape(1024, 128), ROWS + ("z",), 0, 0, tiled=True)
    moved = moved.reshape(32, 32, 128)

    piece = lax.dynamic_slice_in_dim(hblocks, 2 * (4 * y + x), 2, axis=0)
    far = ring(ring(pair(piece), "x"), "y")
    near_swapped = swap(hblocks)
    far_swapped = swap(far)
    near_cols = jnp.concatenate([hcols, swap(hcols)])
    cols = jnp.concatenate([near_cols, pair(near_cols)])
    marks = jnp.arange(32, dtype=jnp.int32)
    row_end = jnp.sum(jnp.where(marks[:, None] <= marks[None, :], hcount[:, None], 0), axis=0)
    shard = jnp.stack([2 * z + c, 2 * z + 1 - c, 2 * (z ^ 1) + c, 2 * (z ^ 1) + 1 - c])
    index = (32 * shard[:, None].astype(jnp.int32) + marks[None, :]).reshape(128)
    owners = jnp.sum((row_end[None, :] <= index[:, None]).astype(jnp.int32), axis=1)

    rows = jnp.where(c == 0, jnp.stack([keep, swap(send)]), jnp.stack([swap(send), keep]))
    rows = rows.transpose(1, 0, 2, 3, 4).reshape(2, 8, 32, 128)
    same = lax.dynamic_index_in_dim(rows, z & 1, 0, keepdims=False)
    differ = lax.dynamic_index_in_dim(rows, 1 - (z & 1), 0, keepdims=False)
    beta = [same, shift(differ, "z", 1), shift(same, "z", 2), shift(differ, "z", 3)]

    oa, *ob = pl.pallas_call(
        product_kernel,
        out_shape=(shape(32, 32, 128),) + (shape(8, 32, 128),) * 4,
        in_specs=[SMEM] * 3 + [ANY] * 9,
        out_specs=(VMEM,) * 5,
        scratch_shapes=[
            pltpu.VMEM((32, 32, 128), F32),
            pltpu.VMEM((32, 32, 128), F32),
            pltpu.VMEM((32, 128, 128), BF16),
            pltpu.VMEM((128, 128, 128), F32),
            pltpu.VMEM((32, 64, 128), F32),
            pltpu.SemaphoreType.DMA((5,)),
            pltpu.SemaphoreType.DMA((8,)),
        ],
        compiler_params=params(40),
        cost_estimate=cost(6 * 128 * 64 * 128 * 128, 10 << 20),
        name="product",
    )(where, cols, owners, *beta, moved, hblocks, near_swapped, far, far_swapped)

    back = lax.all_to_all(oa.reshape(1024, 128), ROWS + ("z",), 0, 0, tiled=True)
    back = back.reshape(32, 2, 16, 128)
    got = [ob[0]] + [shift(ob[k], "z", k) for k in (1, 2, 3)]
    keep, send = pl.pallas_call(
        middle_kernel,
        out_shape=(shape(2, 4, 32, 128), shape(2, 4, 32, 128)),
        in_specs=[SMEM] + [VMEM] * 4,
        out_specs=(VMEM, VMEM),
        compiler_params=params(16),
        cost_estimate=cost(0, 1 << 20),
        name="middle",
    )(where, *got)
    return pl.pallas_call(
        final_kernel,
        out_shape=shape(128, 512),
        in_specs=[SMEM] + [VMEM] * 3,
        out_specs=VMEM,
        compiler_params=params(16),
        cost_estimate=cost(0, 1 << 20),
        name="final",
    )(where, back, keep, swap(send))


def solution(mesh):
    fine = Mesh(mesh.devices.reshape(4, 2, 4, 4, 2), ("y", "h", "x", "z", "c"))
    in_specs = (P(ROWS, ("z", "c")), P(("z", "c"), None, None), P(), P(("z", "c")))
    out_specs = P(ROWS, ("z", "c"))
    return jax.shard_map(local, mesh=fine, in_specs=in_specs, out_specs=out_specs, check_vma=False)
```

```python
import jax
import jax.numpy as jnp
from jax import lax
from jax.experimental import pallas as pl
from jax.experimental.pallas import tpu as pltpu
from jax.sharding import Mesh
from jax.sharding import PartitionSpec as P

ROWS = ("y", "h", "x")
ANY = pl.BlockSpec(memory_space=pl.ANY)
VMEM = pl.BlockSpec(memory_space=pltpu.VMEM)
SMEM = pl.BlockSpec(memory_space=pltpu.SMEM)
F32 = jnp.float32
BF16 = jnp.bfloat16


def params(mib):
    return pltpu.CompilerParams(vmem_limit_bytes=mib << 20)


def cost(flops, moved):
    return pl.CostEstimate(flops=flops, bytes_accessed=moved, transcendentals=0)


def shape(*dims, kind=F32):
    return jax.ShapeDtypeStruct(dims, kind)


def small(kernel, outs, where, *args):
    return pl.pallas_call(
        kernel,
        out_shape=outs,
        in_specs=[SMEM] + [VMEM] * len(args),
        out_specs=(VMEM,) * len(outs),
        compiler_params=params(16),
        cost_estimate=cost(0, 1 << 20),
        name=kernel.__name__,
    )(where, *args)


def prep_kernel(where, h_ref, c_ref, at_ref, keep_ref, send_ref, piece_ref, sem):
    y, x, core = where[0], where[1], where[3]
    copy = pltpu.make_async_copy(h_ref.at[pl.ds(2 * (4 * y + x), 2)], piece_ref, sem)
    copy.start()
    for t in range(4):
        turned = jnp.transpose(c_ref[:, 128 * t : 128 * (t + 1)])
        at_ref[8 * t : 8 * (t + 1)] = turned.reshape(8, 16, 128)
    for q in range(2):
        for t in range(4):
            span = slice(128 * t, 128 * (t + 1))
            mine = pl.multiple_of(64 * q + 32 * core, 32)
            other = pl.multiple_of(64 * q + 32 * (1 - core), 32)
            keep_ref[q, t] = c_ref[pl.ds(mine, 32), span]
            send_ref[q, t] = c_ref[pl.ds(other, 32), span]
    copy.wait()


def rows_kernel(where, keep_ref, got_ref, same_ref, differ_ref):
    q, core = jnp.bitwise_and(where[2], 1), where[3]
    for t in range(4):
        same_ref[4 * core + t] = keep_ref[q, t]
        same_ref[4 * (1 - core) + t] = got_ref[q, t]
        differ_ref[4 * core + t] = keep_ref[1 - q, t]
        differ_ref[4 * (1 - core) + t] = got_ref[1 - q, t]


def join_kernel(where, moved, own, down, up, far_a, far_b, same_ref, differ_ref, out_ref):
    q = jnp.bitwise_and(where[2], 1)
    same_ref[...] = moved[:, pl.ds(pl.multiple_of(8 * q, 8), 8), :]
    differ_ref[...] = moved[:, pl.ds(pl.multiple_of(8 * (1 - q), 8), 8), :]
    at = 0
    for part in (own, down, up, far_a, far_b):
        out_ref[at : at + part.shape[0]] = part[...]
        at += part.shape[0]


def accumulate(blocks, cols, owners, stack, acc):
    contract = (((1,), (1,)), ((), ()))
    terms = []
    for block, at in blocks:
        high = block.astype(BF16)
        low = (block - high.astype(F32)).astype(BF16)
        left = stack[cols[at]]
        one = lax.dot_general(left, high, contract, preferred_element_type=F32)
        two = lax.dot_general(left[:64], low, contract, preferred_element_type=F32)
        terms.append((owners[at], one[:64] + (one[64:] + two)))
    for owner, term in terms:
        acc[owner] += term


def near_kernel(
    where, cols, owners, b0, b1, b2, b3, a0, a1, a2, a3, h0, h1, acc, stack,
    beta, alpha, hbuf, sem_a, sem_h,
):
    z = where[2]
    loads = []
    for k, part in enumerate((b0, b1, b2, b3)):
        home = jnp.bitwise_and(z - k + 4, 3)
        loads.append(pltpu.make_async_copy(part, beta.at[pl.ds(8 * home, 8)], sem_a.at[k]))
    for k, part in enumerate((a0, a1, a2, a3)):
        loads.append(
            pltpu.make_async_copy(part, alpha.at[:, pl.ds(8 * k, 8)], sem_a.at[4 + k])
        )
    for load in loads:
        load.start()
    chunks = []
    for n in range(4):
        source = (h0, h1)[n // 2].at[pl.ds(16 * (n % 2), 16)]
        chunks.append(pltpu.make_async_copy(source, hbuf.at[pl.ds(16 * n, 16)], sem_h.at[n]))
    for chunk in chunks:
        chunk.start()
    acc[...] = jnp.zeros_like(acc)
    for load in loads:
        load.wait()

    @pl.loop(0, 32)
    def _(j):
        for row, source in ((0, beta), (32, alpha)):
            value = source[j]
            high = value.astype(BF16)
            stack[j, row : row + 32] = high
            stack[j, 64 + row : 96 + row] = (value - high.astype(F32)).astype(BF16)

    for n, chunk in enumerate(chunks):
        chunk.wait()

        @pl.loop(0, 4)
        def _(step, n=n):
            first = 16 * n + 4 * step
            accumulate([(hbuf[first + u], first + u) for u in range(4)], cols, owners, stack, acc)


FAR = (8, 8, 8, 4, 4)


def far_kernel(where, cols, owners, acc_in, stack_in, *refs):
    sources, outs = refs[:10], refs[10:18]
    acc, stack, hbuf, sem_a, sem_h = refs[18:]
    y, x, z = where[0], where[1], where[2]
    loads = [
        pltpu.make_async_copy(acc_in, acc, sem_a.at[0]),
        pltpu.make_async_copy(stack_in, stack, sem_a.at[1]),
    ]
    for load in loads:
        load.start()
    chunks = []
    for core in range(2):
        at = 0
        for n, size in enumerate(FAR):
            ref = sources[5 * core + n]
            copy = pltpu.make_async_copy(
                ref, hbuf.at[pl.ds(32 * core + at, size)], sem_h.at[5 * core + n]
            )
            chunks.append((copy, core, at, size))
            at += size
    for chunk, *_ in chunks:
        chunk.start()
    for load in loads:
        load.wait()

    def home(core, i):
        ys, xs, b = i // 8, (i // 2) % 4, i % 2
        dy = jnp.where(ys == 1, 3, jnp.where(ys == 0, 0, ys - 1))
        dx = jnp.where(xs == 1, 3, jnp.where(xs == 0, 0, xs - 1))
        spot = 8 * jnp.bitwise_and(y + dy, 3) + 2 * jnp.bitwise_and(x + dx, 3) + b
        return 64 + 32 * core + spot

    for chunk, core, at, size in chunks:
        chunk.wait()

        @pl.loop(0, size // 4)
        def _(step, core=core, at=at):
            first = at + 4 * step
            blocks = [(hbuf[32 * core + first + u], home(core, first + u)) for u in range(4)]
            accumulate(blocks, cols, owners, stack, acc)

    for k in range(4):
        span = slice(32 + 8 * k, 40 + 8 * k)
        outs[k][...] = acc[:, span]
        outs[4 + k][...] = acc[pl.ds(8 * jnp.bitwise_and(z + k, 3), 8), :32]


def gather_kernel(where, r0, r1, r2, r3, out_ref):
    q = jnp.bitwise_and(where[2], 1)
    out_ref[:, pl.ds(pl.multiple_of(8 * q, 8), 8), :] = r0[...] + r2[...]
    out_ref[:, pl.ds(pl.multiple_of(8 * (1 - q), 8), 8), :] = r1[...] + r3[...]


def middle_kernel(where, r0, r1, r2, r3, keep_ref, send_ref):
    core = where[3]
    for slot, (one, two) in enumerate(((r0, r2), (r1, r3))):
        for t in range(4):
            mine, other = 4 * core + t, 4 * (1 - core) + t
            keep_ref[slot, t] = one[mine] + two[mine]
            send_ref[slot, t] = one[other] + two[other]


def final_kernel(where, back_ref, keep_ref, got_ref, out_ref):
    q, core = jnp.bitwise_and(where[2], 1), where[3]
    for t in range(4):
        span = slice(128 * t, 128 * (t + 1))
        out_ref[:, span] = jnp.transpose(back_ref[8 * t : 8 * (t + 1)].reshape(128, 128))
        for slot in range(2):
            base = 64 * jnp.bitwise_xor(q, slot)
            mine = pl.ds(pl.multiple_of(base + 32 * core, 32), 32)
            other = pl.ds(pl.multiple_of(base + 32 * (1 - core), 32), 32)
            out_ref[mine, span] += keep_ref[slot, t]
            out_ref[other, span] += got_ref[slot, t]


def shift(value, axis, by):
    return lax.ppermute(value, axis, [(i, (i + by) % 4) for i in range(4)])


def swap(value):
    return lax.ppermute(value, "c", [(0, 1), (1, 0)])


def pair(value):
    return lax.ppermute(value, "z", [(0, 1), (1, 0), (2, 3), (3, 2)])


def ring(value, axis):
    half = value.shape[0] // 2
    down, up = shift(value, axis, 1), shift(value, axis, -1)
    return value, down, up, shift(down[:half], axis, 1), shift(up[half:], axis, -1)


def spread(same, differ):
    return same, shift(differ, "z", 1), shift(same, "z", 2), shift(differ, "z", 3)


def tables(hcount, hcols, z, c):
    near_cols = jnp.concatenate([hcols, swap(hcols)])
    cols = jnp.concatenate([near_cols, pair(near_cols)])
    marks = jnp.arange(32, dtype=jnp.int32)
    row_end = jnp.sum(jnp.where(marks[:, None] <= marks[None, :], hcount[:, None], 0), axis=0)
    shard = jnp.stack([2 * z + c, 2 * z + 1 - c, 2 * (z ^ 1) + c, 2 * (z ^ 1) + 1 - c])
    index = (32 * shard[:, None].astype(jnp.int32) + marks[None, :]).reshape(128)
    return cols, jnp.sum((row_end[None, :] <= index[:, None]).astype(jnp.int32), axis=1)


def local(coeffs, hblocks, hcount, hcols):
    y, x, z, c = (lax.axis_index(n) for n in ("y", "x", "z", "c"))
    where = jnp.stack([y, x, z, c]).astype(jnp.int32)
    cols, owners = tables(hcount, hcols, z, c)

    at, keep, send, piece = pl.pallas_call(
        prep_kernel,
        out_shape=(shape(32, 16, 128), shape(2, 4, 32, 128), shape(2, 4, 32, 128), shape(2, 128, 128)),
        in_specs=[SMEM, ANY, VMEM],
        out_specs=(VMEM, VMEM, VMEM, ANY),
        scratch_shapes=[pltpu.SemaphoreType.DMA],
        compiler_params=params(16),
        cost_estimate=cost(0, 1 << 20),
        name="prep",
    )(where, hblocks, coeffs)

    moved = lax.all_to_all(at, ROWS, 0, 0, tiled=True)
    near_swapped = swap(hblocks)
    same, differ = small(rows_kernel, (shape(8, 32, 128),) * 2, where, keep, swap(send))
    beta = spread(same, differ)
    same, differ, joined = small(
        join_kernel,
        (shape(32, 8, 128), shape(32, 8, 128), shape(8, 128, 128)),
        where, moved, *ring(pair(piece), "x"),
    )
    alpha = spread(same, differ)
    far = ring(joined, "y")
    far_swapped = [swap(part) for part in far]

    acc, stack = pl.pallas_call(
        near_kernel,
        out_shape=(shape(32, 64, 128), shape(32, 128, 128, kind=BF16)),
        in_specs=[SMEM] * 3 + [ANY] * 10,
        out_specs=(VMEM,) * 2,
        scratch_shapes=[
            pltpu.VMEM((32, 32, 128), F32),
            pltpu.VMEM((32, 32, 128), F32),
            pltpu.VMEM((64, 128, 128), F32),
            pltpu.SemaphoreType.DMA((8,)),
            pltpu.SemaphoreType.DMA((4,)),
        ],
        compiler_params=params(32),
        cost_estimate=cost(6 * 64 * 64 * 128 * 128, 7 << 20),
        name="near",
    )(where, cols, owners, *beta, *alpha, hblocks, near_swapped)
    outs = pl.pallas_call(
        far_kernel,
        out_shape=(shape(32, 8, 128),) * 4 + (shape(8, 32, 128),) * 4,
        in_specs=[SMEM] * 3 + [ANY] * 12,
        out_specs=(VMEM,) * 8,
        scratch_shapes=[
            pltpu.VMEM((32, 64, 128), F32),
            pltpu.VMEM((32, 128, 128), BF16),
            pltpu.VMEM((64, 128, 128), F32),
            pltpu.SemaphoreType.DMA((2,)),
            pltpu.SemaphoreType.DMA((10,)),
        ],
        compiler_params=params(32),
        cost_estimate=cost(6 * 64 * 64 * 128 * 128, 7 << 20),
        name="far",
    )(where, cols, owners, acc, stack, *far, *far_swapped)

    got = [outs[0]] + [shift(outs[k], "z", -k) for k in (1, 2, 3)]
    (total,) = small(gather_kernel, (shape(32, 16, 128),), where, *got)
    back = lax.all_to_all(total, ROWS, 0, 0, tiled=True)
    got = [outs[4]] + [shift(outs[4 + k], "z", k) for k in (1, 2, 3)]
    keep, send = small(middle_kernel, (shape(2, 4, 32, 128),) * 2, where, *got)
    (out,) = small(final_kernel, (shape(128, 512),), where, back, keep, swap(send))
    return out


def solution(mesh):
    fine = Mesh(mesh.devices.reshape(4, 2, 4, 4, 2), ("y", "h", "x", "z", "c"))
    in_specs = (P(ROWS, ("z", "c")), P(("z", "c"), None, None), P(), P(("z", "c")))
    out_specs = P(ROWS, ("z", "c"))
    return jax.shard_map(local, mesh=fine, in_specs=in_specs, out_specs=out_specs, check_vma=False)
```

```python
import jax
import jax.numpy as jnp
from jax import lax
from jax.experimental import pallas as pl
from jax.experimental.pallas import tpu as pltpu
from jax.sharding import Mesh
from jax.sharding import PartitionSpec as P

ROWS = ("y", "h", "x")
ANY = pl.BlockSpec(memory_space=pl.ANY)
VMEM = pl.BlockSpec(memory_space=pltpu.VMEM)
SMEM = pl.BlockSpec(memory_space=pltpu.SMEM)
F32 = jnp.float32
BF16 = jnp.bfloat16
CONTRACT = (((1,), (1,)), ((), ()))
OFFSETS = (0, -1, 1, 2)


def params(mib):
    return pltpu.CompilerParams(vmem_limit_bytes=mib << 20)


def cost(flops, moved):
    return pl.CostEstimate(flops=flops, bytes_accessed=moved, transcendentals=0)


def shape(*dims, kind=F32):
    return jax.ShapeDtypeStruct(dims, kind)


def join_kernel(where, c_ref, own, down, up, far, at_ref, out_ref):
    x = where[1]
    for t in range(4):
        turned = jnp.transpose(c_ref[:, 128 * t : 128 * (t + 1)]).reshape(8, 16, 128)
        at_ref[8 * t : 8 * (t + 1), 0] = turned
        at_ref[8 * t : 8 * (t + 1), 1] = turned
    for by, part in zip(OFFSETS, (own, down, up, far)):
        out_ref[pl.ds(2 * jnp.bitwise_and(x + by + 4, 3), 2)] = part[...]


def halves(value):
    high = value.astype(BF16)
    return high, (value - high.astype(F32)).astype(BF16)


def product(left, block):
    high, low = halves(block)
    rows = left.shape[0] // 2
    one = lax.dot_general(left, high, CONTRACT, preferred_element_type=F32)
    two = lax.dot_general(left[:rows], low, CONTRACT, preferred_element_type=F32)
    return one[:rows] + (one[rows:] + two)


def alpha_pass(first, count, hbuf, cols, owners, table, stack, acc):
    @pl.loop(0, count // 4)
    def _(step):
        at = first + 4 * step
        terms = []
        for u in range(4):
            spot = table + at + u
            terms.append((owners[spot], product(stack[cols[spot]], hbuf[at + u])))
        for owner, term in terms:
            acc[owner] += term


def beta_pass(where, row_end, shard, group, table, hbuf, cols, owners, stack, acc):
    z, core = where[2], where[3]
    inner = jnp.logical_or(z == 1, z == 2)
    for side in range(2):
        base = 8 * (z if side == 0 else 3 - z) + 4 * core
        start = jnp.where(base == 0, 0, row_end[jnp.maximum(base - 1, 0)])
        stop = row_end[base + 3]
        if side == 1:
            stop = jnp.where(inner, stop, start)
        low = jnp.clip(start - 32 * shard, 0, 32)
        high = jnp.clip(stop - 32 * shard, 0, 32)

        @pl.loop(0, lax.shift_right_logical(high - low + 1, 1))
        def _(step, side=side, base=base, low=low, high=high):
            terms = []
            for u in range(2):
                i = low + 2 * step + u
                spot = 32 * group + jnp.minimum(i, 31)
                owner = 4 * side + owners[table + spot] - base
                term = product(stack[cols[table + spot]], hbuf[spot])
                terms.append((jnp.where(i < high, owner, 8), term))
            for owner, term in terms:
                acc[owner] += term


def near_kernel(
    where, cols, owners, row_end, gathered, a_ref, h0, h1, acc_a, acc_b, stack_a, stack_b,
    wide, hbuf, total, sem_g, sem_h,
):
    z, core = where[2], where[3]
    gather = pltpu.make_async_copy(gathered, wide, sem_g)
    chunks = [
        pltpu.make_async_copy(h, hbuf.at[pl.ds(32 * n, 32)], sem_h.at[n])
        for n, h in enumerate((h0, h1))
    ]
    for copy in chunks + [gather]:
        copy.start()
    acc_a[...] = jnp.zeros_like(acc_a)
    total[...] = jnp.zeros_like(total)

    @pl.loop(0, 32)
    def _(j):
        high, low = halves(a_ref[j])
        stack_a[j, :32] = high
        stack_a[j, 32:] = low

    for n in range(2):
        chunks[n].wait()
        alpha_pass(32 * n, 32, hbuf, cols, owners, 0, stack_a, acc_a)

    gather.wait()

    @pl.loop(0, 8)
    def _(slab):
        for t in range(4):
            high, low = halves(wide[slab, :, 128 * t : 128 * (t + 1)])
            stack_b[4 * slab + t, :128] = high
            stack_b[4 * slab + t, 128:] = low

    for n in range(2):
        shard = 2 * z + (core if n == 0 else 1 - core)
        beta_pass(where, row_end, shard, n, 0, hbuf, cols, owners, stack_b, total)
    acc_b[...] = total[:8]


FAR = ((0, 0, 8), (-1, 0, 8), (1, 0, 8), (2, 0, 4), (2, 4, 4))


def far_kernel(where, cols, owners, row_end, in_a, in_b, in_stack_a, in_stack_b, *refs):
    sources, (out_a, own_b, other_b) = refs[:10], refs[10:13]
    acc_b, stack_a, stack_b, hbuf, sem_a, sem_h = refs[13:]
    y, z, core = where[0], where[2], where[3]
    loads = [
        pltpu.make_async_copy(in_a, out_a, sem_a.at[0]),
        pltpu.make_async_copy(in_stack_a, stack_a, sem_a.at[1]),
        pltpu.make_async_copy(in_b, acc_b.at[pl.ds(0, 8)], sem_a.at[2]),
        pltpu.make_async_copy(in_stack_b, stack_b, sem_a.at[3]),
    ]
    chunks = []
    for side in range(2):
        for n, (by, extra, size) in enumerate(FAR):
            home = 32 * side + 8 * jnp.bitwise_and(y + by + 4, 3) + extra
            copy = pltpu.make_async_copy(
                sources[5 * side + n], hbuf.at[pl.ds(home, size)], sem_h.at[5 * side + n]
            )
            chunks.append((copy, home, size))
    for load in loads[:2]:
        load.start()
    for chunk, *_ in chunks:
        chunk.start()
    for load in loads[2:]:
        load.start()
    for load in loads[:2]:
        load.wait()
    for chunk, home, size in chunks:
        chunk.wait()
        alpha_pass(home, size, hbuf, cols, owners, 64, stack_a, out_a)
    for load in loads[2:]:
        load.wait()
    for side in range(2):
        shard = 2 * jnp.bitwise_xor(z, 1) + (core if side == 0 else 1 - core)
        beta_pass(where, row_end, shard, side, 64, hbuf, cols, owners, stack_b, acc_b)
    own_b[...] = acc_b[:4]
    other_b[...] = acc_b[4:8]


def final_kernel(back_ref, own_ref, got_ref, out_ref):
    for t in range(4):
        span = slice(128 * t, 128 * (t + 1))
        total = back_ref[8 * t : 8 * (t + 1), 0] + back_ref[8 * t : 8 * (t + 1), 1]
        out_ref[:, span] = jnp.transpose(total.reshape(128, 128)) + (own_ref[t] + got_ref[t])


def shift(value, axis, by):
    return lax.ppermute(value, axis, [(i, (i + by) % 4) for i in range(4)])


def swap(value):
    return lax.ppermute(value, "c", [(0, 1), (1, 0)])


def pair(value):
    return lax.ppermute(value, "z", [(0, 1), (1, 0), (2, 3), (3, 2)])


def ring(value, axis):
    half = value.shape[0] // 2
    down, up = shift(value, axis, 1), shift(value, axis, -1)
    return value, down, up, shift(down[:half], axis, 1), shift(up[half:], axis, -1)


def tables(hcount, hcols, z, c):
    near_cols = jnp.concatenate([hcols, swap(hcols)])
    cols = jnp.concatenate([near_cols, pair(near_cols)])
    marks = jnp.arange(32, dtype=jnp.int32)
    row_end = jnp.sum(jnp.where(marks[:, None] <= marks[None, :], hcount[:, None], 0), axis=0)
    shard = jnp.stack([2 * z + c, 2 * z + 1 - c, 2 * (z ^ 1) + c, 2 * (z ^ 1) + 1 - c])
    index = (32 * shard[:, None].astype(jnp.int32) + marks[None, :]).reshape(128)
    owners = jnp.sum((row_end[None, :] <= index[:, None]).astype(jnp.int32), axis=1)
    return cols, owners, row_end


def local(coeffs, hblocks, hcount, hcols):
    y, x, z, c = (lax.axis_index(n) for n in ("y", "x", "z", "c"))
    where = jnp.stack([y, x, z, c]).astype(jnp.int32)
    info = (where,) + tables(hcount, hcols, z, c)

    wide = lax.all_gather(coeffs, ("z", "c"), axis=0)
    near_swapped = swap(hblocks)
    piece = pair(lax.dynamic_slice_in_dim(hblocks, 2 * (4 * y + x), 2, axis=0))
    at, joined = pl.pallas_call(
        join_kernel,
        out_shape=(shape(32, 2, 16, 128), shape(8, 128, 128)),
        in_specs=[SMEM] + [VMEM] * 5,
        out_specs=(VMEM, VMEM),
        compiler_params=params(16),
        cost_estimate=cost(0, 2 << 20),
        name="join",
    )(where, coeffs, piece, *(shift(piece, "x", by) for by in (1, -1, 2)))

    moved = lax.all_to_all(at.reshape(1024, 128), ROWS + ("z",), 0, 0, tiled=True)
    far = ring(joined, "y")
    far_swapped = [swap(part) for part in far]
    state = pl.pallas_call(
        near_kernel,
        out_shape=(
            shape(32, 32, 128),
            shape(8, 128, 128),
            shape(32, 64, 128, kind=BF16),
            shape(32, 256, 128, kind=BF16),
        ),
        in_specs=[SMEM] * 4 + [ANY, VMEM, ANY, ANY],
        out_specs=(VMEM,) * 4,
        scratch_shapes=[
            pltpu.VMEM((8, 128, 512), F32),
            pltpu.VMEM((64, 128, 128), F32),
            pltpu.VMEM((9, 128, 128), F32),
            pltpu.SemaphoreType.DMA,
            pltpu.SemaphoreType.DMA((2,)),
        ],
        compiler_params=params(32),
        cost_estimate=cost(6 * 64 * 128 * 128 * 128, 9 << 20),
        name="near",
    )(*info, wide, moved.reshape(32, 32, 128), hblocks, near_swapped)
    out_a, own_b, other_b = pl.pallas_call(
        far_kernel,
        out_shape=(shape(32, 32, 128), shape(4, 128, 128), shape(4, 128, 128)),
        in_specs=[SMEM] * 4 + [ANY] * 14,
        out_specs=(VMEM,) * 3,
        scratch_shapes=[
            pltpu.VMEM((9, 128, 128), F32),
            pltpu.VMEM((32, 64, 128), BF16),
            pltpu.VMEM((32, 256, 128), BF16),
            pltpu.VMEM((64, 128, 128), F32),
            pltpu.SemaphoreType.DMA((4,)),
            pltpu.SemaphoreType.DMA((10,)),
        ],
        compiler_params=params(32),
        cost_estimate=cost(6 * 64 * 64 * 128 * 128, 8 << 20),
        name="far",
    )(*info, *state, *far, *far_swapped)

    back = lax.all_to_all(out_a.reshape(1024, 128), ROWS + ("z",), 0, 0, tiled=True)
    got = lax.ppermute(other_b, "z", [(1, 2), (2, 1)])
    return pl.pallas_call(
        final_kernel,
        out_shape=shape(128, 512),
        in_specs=[VMEM] * 3,
        out_specs=VMEM,
        compiler_params=params(16),
        cost_estimate=cost(0, 1 << 20),
        name="final",
    )(back.reshape(32, 2, 16, 128), own_b, got)


def solution(mesh):
    fine = Mesh(mesh.devices.reshape(4, 2, 4, 4, 2), ("y", "h", "x", "z", "c"))
    in_specs = (P(ROWS, ("z", "c")), P(("z", "c"), None, None), P(), P(("z", "c")))
    out_specs = P(ROWS, ("z", "c"))
    return jax.shard_map(local, mesh=fine, in_specs=in_specs, out_specs=out_specs, check_vma=False)
```

```python
import jax
import jax.numpy as jnp
from jax import lax
from jax.experimental import pallas as pl
from jax.experimental.pallas import tpu as pltpu
from jax.sharding import Mesh
from jax.sharding import PartitionSpec as P

ROWS = ("y", "h", "x")
ANY = pl.BlockSpec(memory_space=pl.ANY)
VMEM = pl.BlockSpec(memory_space=pltpu.VMEM)
SMEM = pl.BlockSpec(memory_space=pltpu.SMEM)
F32 = jnp.float32
BF16 = jnp.bfloat16
CONTRACT = (((1,), (1,)), ((), ()))
OFFSETS = (0, -1, 1, 2)


def params(mib):
    return pltpu.CompilerParams(vmem_limit_bytes=mib << 20)


def cost(flops, moved):
    return pl.CostEstimate(flops=flops, bytes_accessed=moved, transcendentals=0)


def shape(*dims, kind=F32):
    return jax.ShapeDtypeStruct(dims, kind)


def turn_kernel(c_ref, after, at_ref):
    for t in range(4):
        turned = jnp.transpose(c_ref[:, 128 * t : 128 * (t + 1)]).reshape(8, 16, 128)
        at_ref[8 * t : 8 * (t + 1), 0] = turned
        at_ref[8 * t : 8 * (t + 1), 1] = turned


def join_kernel(where, cols, own, down, up, far, out_ref):
    x = where[1]
    for by, part in zip(OFFSETS, (own, down, up, far)):
        out_ref[pl.ds(2 * jnp.bitwise_and(x + by + 4, 3), 2)] = part[...]


def halves(value):
    high = value.astype(BF16)
    return high, (value - high.astype(F32)).astype(BF16)


def product(left, block):
    high, low = halves(block)
    rows = left.shape[0] // 2
    one = lax.dot_general(left, high, CONTRACT, preferred_element_type=F32)
    two = lax.dot_general(left[:rows], low, CONTRACT, preferred_element_type=F32)
    return one[:rows] + (one[rows:] + two)


def alpha_pass(first, count, hbuf, cols, owners, table, stack, acc):
    @pl.loop(0, count // 4)
    def _(step):
        at = first + 4 * step
        terms = []
        for u in range(4):
            spot = table + at + u
            terms.append((owners[spot], product(stack[cols[spot]], hbuf[at + u])))
        for owner, term in terms:
            acc[owner] += term


def beta_pass(table, hbuf, cols, slots, stack, acc, list_ref):
    def note(n, count):
        list_ref[count] = n
        return count + jnp.where(slots[table + n] < 16, 1, 0)

    count = lax.fori_loop(0, 64, note, 0)
    list_ref[count] = 0

    @pl.loop(0, lax.shift_right_logical(count + 1, 1))
    def _(step):
        terms = []
        for u in range(2):
            n = list_ref[2 * step + u]
            column = cols[table + n]
            left = stack[4 * lax.shift_right_logical(column, 3) + jnp.bitwise_and(column, 3)]
            slot = jnp.where(2 * step + u < count, slots[table + n], 16)
            terms.append((slot, product(left, hbuf[n])))
        for slot, term in terms:
            acc[slot] += term


def beta_near_kernel(
    where, cols, slots, w0, w1, w2, w3, h0, h1, out_b, stack_b,
    wide, hbuf, acc, list_ref, sem_w, sem_h,
):
    z = where[2]
    loads = [
        pltpu.make_async_copy(w, wide.at[k], sem_w.at[k]) for k, w in enumerate((w0, w1, w2, w3))
    ]
    for load in loads:
        load.start()
    chunks = [
        pltpu.make_async_copy(h, hbuf.at[pl.ds(32 * n, 32)], sem_h.at[n])
        for n, h in enumerate((h0, h1))
    ]
    for chunk in chunks:
        chunk.start()
    acc[...] = jnp.zeros_like(acc)
    for k, load in enumerate(loads):
        home = 4 * jnp.bitwise_and(z - k + 4, 3)
        load.wait()
        for t in range(4):
            high, low = halves(wide[k, :, 128 * t : 128 * (t + 1)])
            stack_b[home + t, :128] = high
            stack_b[home + t, 128:] = low
    for chunk in chunks:
        chunk.wait()
    beta_pass(0, hbuf, cols, slots, stack_b, acc, list_ref)
    out_b[...] = acc[:16]


def alpha_near_kernel(cols, owners, a_ref, h0, h1, acc_a, stack_a, hbuf, sem_h):
    chunks = []
    for n in range(4):
        source = (h0, h1)[n // 2].at[pl.ds(16 * (n % 2), 16)]
        chunks.append(pltpu.make_async_copy(source, hbuf.at[pl.ds(16 * n, 16)], sem_h.at[n]))
    for chunk in chunks:
        chunk.start()
    acc_a[...] = jnp.zeros_like(acc_a)

    @pl.loop(0, 32)
    def _(j):
        high, low = halves(a_ref[j])
        stack_a[j, :32] = high
        stack_a[j, 32:] = low

    for n, chunk in enumerate(chunks):
        chunk.wait()
        alpha_pass(16 * n, 16, hbuf, cols, owners, 0, stack_a, acc_a)


FAR = ((0, 0, 8), (-1, 0, 8), (1, 0, 8), (2, 0, 4), (2, 4, 4))


def far_kernel(where, cols, owners, slots, in_a, in_stack_a, in_b, in_stack_b, *refs):
    sources, (out_a, keep_b, send_b) = refs[:10], refs[10:13]
    acc_b, stack_a, stack_b, hbuf, list_ref, sem_a, sem_h = refs[13:]
    y, core = where[0], where[3]
    loads = [
        pltpu.make_async_copy(in_a, out_a, sem_a.at[0]),
        pltpu.make_async_copy(in_stack_a, stack_a, sem_a.at[1]),
        pltpu.make_async_copy(in_b, acc_b.at[pl.ds(0, 16)], sem_a.at[2]),
        pltpu.make_async_copy(in_stack_b, stack_b, sem_a.at[3]),
    ]
    chunks = []
    for side in range(2):
        for n, (by, extra, size) in enumerate(FAR):
            home = 32 * side + 8 * jnp.bitwise_and(y + by + 4, 3) + extra
            copy = pltpu.make_async_copy(
                sources[5 * side + n], hbuf.at[pl.ds(home, size)], sem_h.at[5 * side + n]
            )
            chunks.append((copy, home, size))
    for load in loads[:2]:
        load.start()
    for chunk, *_ in chunks:
        chunk.start()
    for load in loads[2:]:
        load.start()
    for load in loads[:2]:
        load.wait()
    for chunk, home, size in chunks:
        chunk.wait()
        alpha_pass(home, size, hbuf, cols, owners, 64, stack_a, out_a)
    for load in loads[2:]:
        load.wait()
    beta_pass(64, hbuf, cols, slots, stack_b, acc_b, list_ref)
    for plane in range(2):
        keep_b[4 * plane : 4 * plane + 4] = acc_b[pl.ds(8 * plane + 4 * core, 4)]
        send_b[4 * plane : 4 * plane + 4] = acc_b[pl.ds(8 * plane + 4 * (1 - core), 4)]


def cores_kernel(keep_ref, got_ref, own_ref, other_ref):
    own_ref[...] = keep_ref[:4] + got_ref[:4]
    other_ref[...] = keep_ref[4:] + got_ref[4:]


def final_kernel(back_ref, own_ref, got_ref, out_ref):
    for t in range(4):
        span = slice(128 * t, 128 * (t + 1))
        total = back_ref[8 * t : 8 * (t + 1), 0] + back_ref[8 * t : 8 * (t + 1), 1]
        out_ref[:, span] = jnp.transpose(total.reshape(128, 128)) + (own_ref[t] + got_ref[t])


def shift(value, axis, by):
    return lax.ppermute(value, axis, [(i, (i + by) % 4) for i in range(4)])


def swap(value):
    return lax.ppermute(value, "c", [(0, 1), (1, 0)])


def pair(value):
    return lax.ppermute(value, "z", [(0, 1), (1, 0), (2, 3), (3, 2)])


def ring(value, axis):
    half = value.shape[0] // 2
    down, up = shift(value, axis, 1), shift(value, axis, -1)
    return value, down, up, shift(down[:half], axis, 1), shift(up[half:], axis, -1)


def tables(hcount, hcols, z, c):
    near_cols = jnp.concatenate([hcols, swap(hcols)])
    cols = jnp.concatenate([near_cols, pair(near_cols)])
    marks = jnp.arange(32, dtype=jnp.int32)
    row_end = jnp.sum(jnp.where(marks[:, None] <= marks[None, :], hcount[:, None], 0), axis=0)
    shard = jnp.stack([2 * z + c, 2 * z + 1 - c, 2 * (z ^ 1) + c, 2 * (z ^ 1) + 1 - c])
    index = (32 * shard[:, None].astype(jnp.int32) + marks[None, :]).reshape(128)
    owners = jnp.sum((row_end[None, :] <= index[:, None]).astype(jnp.int32), axis=1)
    inner = (z == 1) | (z == 2)
    slots = jnp.where(owners // 8 == z, owners % 8, 16)
    slots = jnp.where(inner & (owners // 8 == 3 - z), 8 + owners % 8, slots)
    return cols, owners, jnp.where((cols // 4) % 2 == c, slots, 16)


def call(kernel, outs, in_specs, *args, scratch=(), mib=16, work=(0, 1 << 20)):
    single = not isinstance(outs, tuple)
    return pl.pallas_call(
        kernel,
        out_shape=outs,
        in_specs=in_specs,
        out_specs=VMEM if single else (VMEM,) * len(outs),
        scratch_shapes=scratch,
        compiler_params=params(mib),
        cost_estimate=cost(*work),
        name=kernel.__name__,
    )(*args)


def local(coeffs, hblocks, hcount, hcols):
    y, x, z, c = (lax.axis_index(n) for n in ("y", "x", "z", "c"))
    where = jnp.stack([y, x, z, c]).astype(jnp.int32)
    cols, owners, slots = tables(hcount, hcols, z, c)

    near_swapped = swap(hblocks)
    piece = pair(lax.dynamic_slice_in_dim(hblocks, 2 * (4 * y + x), 2, axis=0))
    at = call(turn_kernel, shape(32, 2, 16, 128), [VMEM, ANY], coeffs, piece)
    moved = lax.all_to_all(at.reshape(1024, 128), ROWS + ("z",), 0, 0, tiled=True)
    rows = [coeffs] + [shift(coeffs, "z", k) for k in (1, 2, 3)]
    joined = call(
        join_kernel, shape(8, 128, 128), [SMEM] * 2 + [VMEM] * 4,
        where, cols, piece, *(shift(piece, "x", by) for by in (1, -1, 2)),
    )
    far = ring(joined, "y")
    far_swapped = [swap(part) for part in far]

    out_b, stack_b = call(
        beta_near_kernel,
        (shape(16, 128, 128), shape(16, 256, 128, kind=BF16)),
        [SMEM] * 3 + [ANY] * 6,
        where, cols, slots, *rows, hblocks, near_swapped,
        scratch=[
            pltpu.VMEM((4, 128, 512), F32),
            pltpu.VMEM((64, 128, 128), F32),
            pltpu.VMEM((17, 128, 128), F32),
            pltpu.SMEM((72,), jnp.int32),
            pltpu.SemaphoreType.DMA((4,)),
            pltpu.SemaphoreType.DMA((2,)),
        ],
        mib=24,
        work=(6 * 32 * 128 * 128 * 128, 7 << 20),
    )
    acc_a, stack_a = call(
        alpha_near_kernel,
        (shape(32, 32, 128), shape(32, 64, 128, kind=BF16)),
        [SMEM] * 2 + [VMEM] + [ANY] * 2,
        cols, owners, moved.reshape(32, 32, 128), hblocks, near_swapped,
        scratch=[pltpu.VMEM((64, 128, 128), F32), pltpu.SemaphoreType.DMA((4,))],
        mib=24,
        work=(6 * 64 * 64 * 128 * 128, 7 << 20),
    )
    out_a, keep_b, send_b = call(
        far_kernel,
        (shape(32, 32, 128), shape(8, 128, 128), shape(8, 128, 128)),
        [SMEM] * 4 + [ANY] * 14,
        where, cols, owners, slots, acc_a, stack_a, out_b, stack_b, *far, *far_swapped,
        scratch=[
            pltpu.VMEM((17, 128, 128), F32),
            pltpu.VMEM((32, 64, 128), BF16),
            pltpu.VMEM((16, 256, 128), BF16),
            pltpu.VMEM((64, 128, 128), F32),
            pltpu.SMEM((72,), jnp.int32),
            pltpu.SemaphoreType.DMA((4,)),
            pltpu.SemaphoreType.DMA((10,)),
        ],
        mib=24,
        work=(6 * 64 * 64 * 128 * 128, 8 << 20),
    )

    back = lax.all_to_all(out_a.reshape(1024, 128), ROWS + ("z",), 0, 0, tiled=True)
    own, other = call(cores_kernel, (shape(4, 128, 128),) * 2, [VMEM] * 2, keep_b, swap(send_b))
    got = lax.ppermute(other, "z", [(1, 2), (2, 1)])
    return call(
        final_kernel, shape(128, 512), [VMEM] * 3, back.reshape(32, 2, 16, 128), own, got
    )


def solution(mesh):
    fine = Mesh(mesh.devices.reshape(4, 2, 4, 4, 2), ("y", "h", "x", "z", "c"))
    in_specs = (P(ROWS, ("z", "c")), P(("z", "c"), None, None), P(), P(("z", "c")))
    out_specs = P(ROWS, ("z", "c"))
    return jax.shard_map(local, mesh=fine, in_specs=in_specs, out_specs=out_specs, check_vma=False)
```

```python
import jax
import jax.numpy as jnp
from jax import lax
from jax.experimental import pallas as pl
from jax.experimental.pallas import tpu as pltpu
from jax.sharding import Mesh
from jax.sharding import PartitionSpec as P

ROWS = ("y", "h", "x")
ANY = pl.BlockSpec(memory_space=pl.ANY)
VMEM = pl.BlockSpec(memory_space=pltpu.VMEM)
SMEM = pl.BlockSpec(memory_space=pltpu.SMEM)
F32 = jnp.float32
BF16 = jnp.bfloat16
CONTRACT = (((1,), (1,)), ((), ()))
OFFSETS = (0, -1, 1, 2)


def params(mib):
    return pltpu.CompilerParams(vmem_limit_bytes=mib << 20)


def cost(flops, moved):
    return pl.CostEstimate(flops=flops, bytes_accessed=moved, transcendentals=0)


def shape(*dims, kind=F32):
    return jax.ShapeDtypeStruct(dims, kind)


def turn_kernel(c_ref, w1, w2, w3, at_ref):
    for t in range(4):
        turned = jnp.transpose(c_ref[:, 128 * t : 128 * (t + 1)]).reshape(8, 16, 128)
        at_ref[8 * t : 8 * (t + 1), 0] = turned
        at_ref[8 * t : 8 * (t + 1), 1] = turned


def join_kernel(where, cols, own, down, up, far, out_ref):
    x = where[1]
    for by, part in zip(OFFSETS, (own, down, up, far)):
        out_ref[pl.ds(2 * jnp.bitwise_and(x + by + 4, 3), 2)] = part[...]


def halves(value):
    high = value.astype(BF16)
    return high, (value - high.astype(F32)).astype(BF16)


def product(left, block):
    high, low = halves(block)
    rows = left.shape[0] // 2
    one = lax.dot_general(left, high, CONTRACT, preferred_element_type=F32)
    two = lax.dot_general(left[:rows], low, CONTRACT, preferred_element_type=F32)
    return one[:rows] + (one[rows:] + two)


def alpha_pass(first, count, hbuf, cols, owners, table, stack, acc):
    @pl.loop(0, count // 4)
    def _(step):
        at = first + 4 * step
        terms = []
        for u in range(4):
            spot = table + at + u
            terms.append((owners[spot], product(stack[cols[spot]], hbuf[at + u])))
        for owner, term in terms:
            acc[owner] += term


def beta_pass(table, hbuf, cols, slots, stack, acc, list_ref):
    def note(n, count):
        list_ref[count] = n
        return count + jnp.where(slots[table + n] < 16, 1, 0)

    count = lax.fori_loop(0, 64, note, 0)
    list_ref[count] = 0

    @pl.loop(0, lax.shift_right_logical(count + 1, 1))
    def _(step):
        terms = []
        for u in range(2):
            n = list_ref[2 * step + u]
            column = cols[table + n]
            left = stack[4 * lax.shift_right_logical(column, 3) + jnp.bitwise_and(column, 3)]
            slot = jnp.where(2 * step + u < count, slots[table + n], 16)
            terms.append((slot, product(left, hbuf[n])))
        for slot, term in terms:
            acc[slot] += term


def beta_near_kernel(
    where, cols, slots, w0, w1, w2, w3, h0, h1, out_b, stack_b,
    wide, hbuf, acc, list_ref, sem_w, sem_h,
):
    z = where[2]
    loads = [
        pltpu.make_async_copy(w, wide.at[k], sem_w.at[k]) for k, w in enumerate((w0, w1, w2, w3))
    ]
    for load in loads:
        load.start()
    chunks = [
        pltpu.make_async_copy(h, hbuf.at[pl.ds(32 * n, 32)], sem_h.at[n])
        for n, h in enumerate((h0, h1))
    ]
    for chunk in chunks:
        chunk.start()
    acc[...] = jnp.zeros_like(acc)
    for k, load in enumerate(loads):
        home = 4 * jnp.bitwise_and(z - k + 4, 3)
        load.wait()
        for t in range(4):
            high, low = halves(wide[k, :, 128 * t : 128 * (t + 1)])
            stack_b[home + t, :128] = high
            stack_b[home + t, 128:] = low
    for chunk in chunks:
        chunk.wait()
    beta_pass(0, hbuf, cols, slots, stack_b, acc, list_ref)
    out_b[...] = acc[:16]


def alpha_near_kernel(cols, owners, a_ref, h0, h1, acc_a, stack_a, hbuf, sem_h):
    chunks = []
    for n in range(4):
        source = (h0, h1)[n // 2].at[pl.ds(16 * (n % 2), 16)]
        chunks.append(pltpu.make_async_copy(source, hbuf.at[pl.ds(16 * n, 16)], sem_h.at[n]))
    for chunk in chunks:
        chunk.start()
    acc_a[...] = jnp.zeros_like(acc_a)

    @pl.loop(0, 32)
    def _(j):
        high, low = halves(a_ref[j])
        stack_a[j, :32] = high
        stack_a[j, 32:] = low

    for n, chunk in enumerate(chunks):
        chunk.wait()
        alpha_pass(16 * n, 16, hbuf, cols, owners, 0, stack_a, acc_a)


FAR = ((0, 0, 8), (-1, 0, 8), (1, 0, 8), (2, 0, 4), (2, 4, 4))


def far_kernel(where, cols, owners, slots, in_a, in_stack_a, in_b, in_stack_b, *refs):
    sources, (out_a, keep_b, send_b) = refs[:10], refs[10:13]
    acc_b, stack_a, stack_b, hbuf, list_ref, sem_a, sem_h = refs[13:]
    y, core = where[0], where[3]
    loads = [
        pltpu.make_async_copy(in_a, out_a, sem_a.at[0]),
        pltpu.make_async_copy(in_stack_a, stack_a, sem_a.at[1]),
        pltpu.make_async_copy(in_b, acc_b.at[pl.ds(0, 16)], sem_a.at[2]),
        pltpu.make_async_copy(in_stack_b, stack_b, sem_a.at[3]),
    ]
    chunks = []
    for side in range(2):
        for n, (by, extra, size) in enumerate(FAR):
            home = 32 * side + 8 * jnp.bitwise_and(y + by + 4, 3) + extra
            copy = pltpu.make_async_copy(
                sources[5 * side + n], hbuf.at[pl.ds(home, size)], sem_h.at[5 * side + n]
            )
            chunks.append((copy, home, size))
    for load in loads[:2]:
        load.start()
    for chunk, *_ in chunks:
        chunk.start()
    for load in loads[2:]:
        load.start()
    for load in loads[:2]:
        load.wait()
    for chunk, home, size in chunks:
        chunk.wait()
        alpha_pass(home, size, hbuf, cols, owners, 64, stack_a, out_a)
    for load in loads[2:]:
        load.wait()
    beta_pass(64, hbuf, cols, slots, stack_b, acc_b, list_ref)
    for plane in range(2):
        keep_b[4 * plane : 4 * plane + 4] = acc_b[pl.ds(8 * plane + 4 * core, 4)]
        send_b[4 * plane : 4 * plane + 4] = acc_b[pl.ds(8 * plane + 4 * (1 - core), 4)]


def cores_kernel(keep_ref, got_ref, own_ref, other_ref):
    own_ref[...] = keep_ref[:4] + got_ref[:4]
    other_ref[...] = keep_ref[4:] + got_ref[4:]


def final_kernel(back_ref, own_ref, got_ref, out_ref):
    for t in range(4):
        span = slice(128 * t, 128 * (t + 1))
        total = back_ref[8 * t : 8 * (t + 1), 0] + back_ref[8 * t : 8 * (t + 1), 1]
        out_ref[:, span] = jnp.transpose(total.reshape(128, 128)) + (own_ref[t] + got_ref[t])


def shift(value, axis, by):
    return lax.ppermute(value, axis, [(i, (i + by) % 4) for i in range(4)])


def swap(value):
    return lax.ppermute(value, "c", [(0, 1), (1, 0)])


def pair(value):
    return lax.ppermute(value, "z", [(0, 1), (1, 0), (2, 3), (3, 2)])


def ring(value, axis):
    half = value.shape[0] // 2
    down, up = shift(value, axis, 1), shift(value, axis, -1)
    return value, down, up, shift(down[:half], axis, 1), shift(up[half:], axis, -1)


def tables(hcount, hcols, z, c):
    near_cols = jnp.concatenate([hcols, swap(hcols)])
    cols = jnp.concatenate([near_cols, pair(near_cols)])
    marks = jnp.arange(32, dtype=jnp.int32)
    row_end = jnp.sum(jnp.where(marks[:, None] <= marks[None, :], hcount[:, None], 0), axis=0)
    shard = jnp.stack([2 * z + c, 2 * z + 1 - c, 2 * (z ^ 1) + c, 2 * (z ^ 1) + 1 - c])
    index = (32 * shard[:, None].astype(jnp.int32) + marks[None, :]).reshape(128)
    owners = jnp.sum((row_end[None, :] <= index[:, None]).astype(jnp.int32), axis=1)
    inner = (z == 1) | (z == 2)
    slots = jnp.where(owners // 8 == z, owners % 8, 16)
    slots = jnp.where(inner & (owners // 8 == 3 - z), 8 + owners % 8, slots)
    return cols, owners, jnp.where((cols // 4) % 2 == c, slots, 16)


def call(kernel, outs, in_specs, *args, scratch=(), mib=16, work=(0, 1 << 20)):
    single = not isinstance(outs, tuple)
    return pl.pallas_call(
        kernel,
        out_shape=outs,
        in_specs=in_specs,
        out_specs=VMEM if single else (VMEM,) * len(outs),
        scratch_shapes=scratch,
        compiler_params=params(mib),
        cost_estimate=cost(*work),
        name=kernel.__name__,
    )(*args)


def local(coeffs, hblocks, hcount, hcols):
    y, x, z, c = (lax.axis_index(n) for n in ("y", "x", "z", "c"))
    where = jnp.stack([y, x, z, c]).astype(jnp.int32)
    cols, owners, slots = tables(hcount, hcols, z, c)

    near_swapped = swap(hblocks)
    piece = pair(lax.dynamic_slice_in_dim(hblocks, 2 * (4 * y + x), 2, axis=0))
    rows = [coeffs] + [shift(coeffs, "z", k) for k in (1, 2, 3)]
    at = call(turn_kernel, shape(32, 2, 16, 128), [VMEM] + [ANY] * 3, *rows)
    moved = lax.all_to_all(at.reshape(1024, 128), ROWS + ("z",), 0, 0, tiled=True)
    joined = call(
        join_kernel, shape(8, 128, 128), [SMEM] * 2 + [VMEM] * 4,
        where, cols, piece, *(shift(piece, "x", by) for by in (1, -1, 2)),
    )
    far = ring(joined, "y")
    far_swapped = [swap(part) for part in far]

    out_b, stack_b = call(
        beta_near_kernel,
        (shape(16, 128, 128), shape(16, 256, 128, kind=BF16)),
        [SMEM] * 3 + [ANY] * 6,
        where, cols, slots, *rows, hblocks, near_swapped,
        scratch=[
            pltpu.VMEM((4, 128, 512), F32),
            pltpu.VMEM((64, 128, 128), F32),
            pltpu.VMEM((17, 128, 128), F32),
            pltpu.SMEM((72,), jnp.int32),
            pltpu.SemaphoreType.DMA((4,)),
            pltpu.SemaphoreType.DMA((2,)),
        ],
        mib=24,
        work=(6 * 32 * 128 * 128 * 128, 7 << 20),
    )
    acc_a, stack_a = call(
        alpha_near_kernel,
        (shape(32, 32, 128), shape(32, 64, 128, kind=BF16)),
        [SMEM] * 2 + [VMEM] + [ANY] * 2,
        cols, owners, moved.reshape(32, 32, 128), hblocks, near_swapped,
        scratch=[pltpu.VMEM((64, 128, 128), F32), pltpu.SemaphoreType.DMA((4,))],
        mib=24,
        work=(6 * 64 * 64 * 128 * 128, 7 << 20),
    )
    out_a, keep_b, send_b = call(
        far_kernel,
        (shape(32, 32, 128), shape(8, 128, 128), shape(8, 128, 128)),
        [SMEM] * 4 + [ANY] * 14,
        where, cols, owners, slots, acc_a, stack_a, out_b, stack_b, *far, *far_swapped,
        scratch=[
            pltpu.VMEM((17, 128, 128), F32),
            pltpu.VMEM((32, 64, 128), BF16),
            pltpu.VMEM((16, 256, 128), BF16),
            pltpu.VMEM((64, 128, 128), F32),
            pltpu.SMEM((72,), jnp.int32),
            pltpu.SemaphoreType.DMA((4,)),
            pltpu.SemaphoreType.DMA((10,)),
        ],
        mib=24,
        work=(6 * 64 * 64 * 128 * 128, 8 << 20),
    )

    back = lax.all_to_all(out_a.reshape(1024, 128), ROWS + ("z",), 0, 0, tiled=True)
    own, other = call(cores_kernel, (shape(4, 128, 128),) * 2, [VMEM] * 2, keep_b, swap(send_b))
    got = lax.ppermute(other, "z", [(1, 2), (2, 1)])
    return call(
        final_kernel, shape(128, 512), [VMEM] * 3, back.reshape(32, 2, 16, 128), own, got
    )


def solution(mesh):
    fine = Mesh(mesh.devices.reshape(4, 2, 4, 4, 2), ("y", "h", "x", "z", "c"))
    in_specs = (P(ROWS, ("z", "c")), P(("z", "c"), None, None), P(), P(("z", "c")))
    out_specs = P(ROWS, ("z", "c"))
    return jax.shard_map(local, mesh=fine, in_specs=in_specs, out_specs=out_specs, check_vma=False)
```

```python
import jax
import jax.numpy as jnp
from jax import lax
from jax.experimental import pallas as pl
from jax.experimental.pallas import tpu as pltpu
from jax.sharding import Mesh
from jax.sharding import PartitionSpec as P

ROWS = ("y", "h", "x")
ANY = pl.BlockSpec(memory_space=pl.ANY)
VMEM = pl.BlockSpec(memory_space=pltpu.VMEM)
SMEM = pl.BlockSpec(memory_space=pltpu.SMEM)
F32 = jnp.float32
BF16 = jnp.bfloat16
TRASH = 28
CONTRACT = (((1,), (1,)), ((), ()))

def params(mib):
    return pltpu.CompilerParams(vmem_limit_bytes=mib << 20)


def cost(flops, moved):
    return pl.CostEstimate(flops=flops, bytes_accessed=moved, transcendentals=0)


def shape(*dims, kind=F32):
    return jax.ShapeDtypeStruct(dims, kind)


def turn_kernel(c_ref, at_ref):
    for t in range(4):
        turned = jnp.transpose(c_ref[:, 128 * t : 128 * (t + 1)]).reshape(8, 16, 128)
        for plane in range(4):
            at_ref[8 * t : 8 * (t + 1), plane] = turned


def halves(value):
    high = value.astype(BF16)
    return high, (value - high.astype(F32)).astype(BF16)


def product(left, block):
    high, low = halves(block)
    rows = left.shape[0] // 2
    one = lax.dot_general(left, high, CONTRACT, preferred_element_type=F32)
    two = lax.dot_general(left[:rows], low, CONTRACT, preferred_element_type=F32)
    return one[:rows] + (one[rows:] + two)


def beta_kernel(
    where, cols, slots, w0, w1, w2, w3, h0, h1, keep_ref, send_ref, token_ref,
    wide, stack, hbuf, acc, list_ref, sem_w, sem_h,
):
    z, core = where[2], where[3]
    loads = [
        pltpu.make_async_copy(w, wide.at[k], sem_w.at[k]) for k, w in enumerate((w0, w1, w2, w3))
    ]
    chunks = [
        pltpu.make_async_copy(h, hbuf.at[pl.ds(32 * n, 32)], sem_h.at[n])
        for n, h in enumerate((h0, h1))
    ]
    for copy in loads + chunks:
        copy.start()
    acc[...] = jnp.zeros_like(acc)

    def note(n, count):
        list_ref[count] = n
        return count + jnp.where(slots[n] < TRASH, 1, 0)

    count = lax.fori_loop(0, 64, note, 0)
    list_ref[count] = 0
    for k, load in enumerate(loads):
        home = 4 * jnp.bitwise_and(z - k + 4, 3)
        load.wait()
        for t in range(4):
            high, low = halves(wide[k, :, 128 * t : 128 * (t + 1)])
            stack[home + t, :128] = high
            stack[home + t, 128:] = low
    for chunk in chunks:
        chunk.wait()

    @pl.loop(0, lax.shift_right_logical(count + 1, 1))
    def _(step):
        terms = []
        for u in range(2):
            n = list_ref[2 * step + u]
            column = cols[n]
            left = stack[4 * lax.shift_right_logical(column, 3) + jnp.bitwise_and(column, 3)]
            slot = jnp.where(2 * step + u < count, slots[n], TRASH)
            terms.append((slot, product(left, hbuf[n])))
        for slot, term in terms:
            acc[slot] += term

    for group in range(3):
        keep_ref[4 * group : 4 * group + 4] = acc[pl.ds(8 * group + 4 * core, 4)]
        send_ref[4 * group : 4 * group + 4] = acc[pl.ds(8 * group + 4 * (1 - core), 4)]
    mine = core == jnp.where(z == 0, 0, 1)
    edge = acc[24:28]
    keep_ref[12:] = jnp.where(mine, edge, 0.0)
    send_ref[12:] = jnp.where(mine, 0.0, edge)
    token_ref[...] = jnp.zeros_like(token_ref)


def alpha_kernel(cols, owners, a_ref, h0, h1, after, acc, stack, hbuf, sem_h):
    chunks = []
    for n in range(4):
        source = (h0, h1)[n // 2].at[pl.ds(16 * (n % 2), 16)]
        chunks.append(pltpu.make_async_copy(source, hbuf.at[pl.ds(16 * n, 16)], sem_h.at[n]))
    for chunk in chunks:
        chunk.start()
    acc[...] = jnp.zeros_like(acc)

    @pl.loop(0, 32)
    def _(j):
        high, low = halves(a_ref[j])
        stack[j, :64] = high
        stack[j, 64:] = low

    for n, chunk in enumerate(chunks):
        chunk.wait()

        @pl.loop(0, 4)
        def _(step, n=n):
            terms = []
            for u in range(4):
                spot = 16 * n + 4 * step + u
                terms.append((owners[spot], product(stack[cols[spot]], hbuf[spot])))
            for owner, term in terms:
                acc[owner] += term


def cores_kernel(keep_ref, got_ref, own_ref, down_ref, up_ref, edge_ref):
    for n, ref in enumerate((own_ref, down_ref, up_ref, edge_ref)):
        ref[...] = keep_ref[4 * n : 4 * n + 4] + got_ref[4 * n : 4 * n + 4]


def final_kernel(back_ref, own_ref, down_ref, up_ref, edge_ref, out_ref):
    for t in range(4):
        part = back_ref[8 * t : 8 * (t + 1)]
        total = (part[:, 0] + part[:, 1]) + (part[:, 2] + part[:, 3])
        beta = (own_ref[t] + down_ref[t]) + (up_ref[t] + edge_ref[t])
        out_ref[:, 128 * t : 128 * (t + 1)] = jnp.transpose(total.reshape(128, 128)) + beta


def swap(value):
    return lax.ppermute(value, "c", [(0, 1), (1, 0)])


def tables(hcount, hcols, z, c):
    cols = jnp.concatenate([hcols, swap(hcols)])
    marks = jnp.arange(32, dtype=jnp.int32)
    row_end = jnp.sum(jnp.where(marks[:, None] <= marks[None, :], hcount[:, None], 0), axis=0)
    shard = jnp.stack([2 * z + c, 2 * z + 1 - c])
    index = (32 * shard[:, None].astype(jnp.int32) + marks[None, :]).reshape(64)
    owners = jnp.sum((row_end[None, :] <= index[:, None]).astype(jnp.int32), axis=1)
    step = owners // 8 - z
    slots = owners % 8 + jnp.where(step == 0, 0, jnp.where(step == -1, 8, 16))
    slots = jnp.where(step == 2, 24 + owners - 16, jnp.where(step == -2, 24 + owners - 12, slots))
    return cols, owners, jnp.where((cols // 4) % 2 == c, slots, TRASH)


def call(kernel, outs, in_specs, *args, scratch=(), mib=16, work=(0, 1 << 20)):
    single = not isinstance(outs, tuple)
    return pl.pallas_call(
        kernel,
        out_shape=outs,
        in_specs=in_specs,
        out_specs=VMEM if single else (VMEM,) * len(outs),
        scratch_shapes=scratch,
        compiler_params=params(mib),
        cost_estimate=cost(*work),
        name=kernel.__name__,
    )(*args)


def local(coeffs, hblocks, hcount, hcols):
    z, c = lax.axis_index("z"), lax.axis_index("c")
    where = jnp.stack([z, z, z, c]).astype(jnp.int32)
    swapped = swap(hblocks)
    rows = [coeffs] + [
        lax.ppermute(coeffs, "z", [(i, (i + k) % 4) for i in range(4)]) for k in (1, 2, 3)
    ]
    cols, owners, slots = tables(hcount, hcols, z, c)
    at = call(turn_kernel, shape(32, 4, 16, 128), [VMEM], coeffs)
    moved = lax.all_to_all(at.reshape(2048, 128), ROWS + ("z",), 0, 0, tiled=True)

    keep, send, token = call(
        beta_kernel,
        (shape(16, 128, 128), shape(16, 128, 128), shape(8, 128)),
        [SMEM] * 3 + [ANY] * 6,
        where, cols, slots, *rows, hblocks, swapped,
        scratch=[
            pltpu.VMEM((4, 128, 512), F32),
            pltpu.VMEM((16, 256, 128), BF16),
            pltpu.VMEM((64, 128, 128), F32),
            pltpu.VMEM((TRASH + 1, 128, 128), F32),
            pltpu.SMEM((72,), jnp.int32),
            pltpu.SemaphoreType.DMA((4,)),
            pltpu.SemaphoreType.DMA((2,)),
        ],
        mib=24,
        work=(6 * 32 * 128 * 128 * 128, 7 << 20),
    )
    (out_a,) = call(
        alpha_kernel,
        (shape(32, 64, 128),),
        [SMEM] * 2 + [VMEM] + [ANY] * 2 + [VMEM],
        cols, owners, moved.reshape(32, 64, 128), hblocks, swapped, token,
        scratch=[
            pltpu.VMEM((32, 128, 128), BF16),
            pltpu.VMEM((64, 128, 128), F32),
            pltpu.SemaphoreType.DMA((4,)),
        ],
        mib=24,
        work=(6 * 64 * 64 * 128 * 128, 7 << 20),
    )

    back = lax.all_to_all(out_a.reshape(2048, 128), ROWS + ("z",), 0, 0, tiled=True)
    own, down, up, edge = call(
        cores_kernel, (shape(4, 128, 128),) * 4, [VMEM] * 2, keep, swap(send)
    )
    down = lax.ppermute(down, "z", [(1, 0), (2, 1), (3, 2)])
    up = lax.ppermute(up, "z", [(0, 1), (1, 2), (2, 3)])
    edge = lax.ppermute(edge, "z", [(0, 2), (3, 1)])
    return call(
        final_kernel, shape(128, 512), [VMEM] * 5,
        back.reshape(32, 4, 16, 128), own, down, up, edge,
    )


def solution(mesh):
    fine = Mesh(mesh.devices.reshape(4, 2, 4, 4, 2), ("y", "h", "x", "z", "c"))
    in_specs = (P(ROWS, ("z", "c")), P(("z", "c"), None, None), P(), P(("z", "c")))
    out_specs = P(ROWS, ("z", "c"))
    return jax.shard_map(local, mesh=fine, in_specs=in_specs, out_specs=out_specs, check_vma=False)
```

```python
import jax
import jax.numpy as jnp
from jax import lax
from jax.experimental import pallas as pl
from jax.experimental.pallas import tpu as pltpu
from jax.sharding import Mesh
from jax.sharding import PartitionSpec as P

ROWS = ("y", "h", "x")
ANY = pl.BlockSpec(memory_space=pl.ANY)
VMEM = pl.BlockSpec(memory_space=pltpu.VMEM)
SMEM = pl.BlockSpec(memory_space=pltpu.SMEM)
F32 = jnp.float32
BF16 = jnp.bfloat16
TRASH = 28
CONTRACT = (((1,), (1,)), ((), ()))

BUSY = 40 * 10**9


def params(mib):
    return pltpu.CompilerParams(vmem_limit_bytes=mib << 20)


def cost(flops, moved):
    return pl.CostEstimate(flops=flops, bytes_accessed=moved, transcendentals=0)


def shape(*dims, kind=F32):
    return jax.ShapeDtypeStruct(dims, kind)


def turn_kernel(c_ref, at_ref):
    for t in range(4):
        turned = jnp.transpose(c_ref[:, 128 * t : 128 * (t + 1)]).reshape(8, 16, 128)
        for plane in range(4):
            at_ref[8 * t : 8 * (t + 1), plane] = turned


def halves(value):
    high = value.astype(BF16)
    return high, (value - high.astype(F32)).astype(BF16)


def product(left, block):
    high, low = halves(block)
    rows = left.shape[0] // 2
    one = lax.dot_general(left, high, CONTRACT, preferred_element_type=F32)
    two = lax.dot_general(left[:rows], low, CONTRACT, preferred_element_type=F32)
    return one[:rows] + (one[rows:] + two)


def beta_kernel(
    where, cols, slots, w0, w1, w2, w3, h0, h1, keep_ref, send_ref,
    wide, stack, hbuf, acc, list_ref, sem_w, sem_h,
):
    z, core = where[2], where[3]
    loads = [
        pltpu.make_async_copy(w, wide.at[k], sem_w.at[k]) for k, w in enumerate((w0, w1, w2, w3))
    ]
    chunks = [
        pltpu.make_async_copy(h, hbuf.at[pl.ds(32 * n, 32)], sem_h.at[n])
        for n, h in enumerate((h0, h1))
    ]
    for copy in loads + chunks:
        copy.start()
    acc[...] = jnp.zeros_like(acc)

    def note(n, count):
        list_ref[count] = n
        return count + jnp.where(slots[n] < TRASH, 1, 0)

    count = lax.fori_loop(0, 64, note, 0)
    list_ref[count] = 0
    for k, load in enumerate(loads):
        home = 4 * jnp.bitwise_and(z - k + 4, 3)
        load.wait()
        for t in range(4):
            high, low = halves(wide[k, :, 128 * t : 128 * (t + 1)])
            stack[home + t, :128] = high
            stack[home + t, 128:] = low
    for chunk in chunks:
        chunk.wait()

    @pl.loop(0, lax.shift_right_logical(count + 1, 1))
    def _(step):
        terms = []
        for u in range(2):
            n = list_ref[2 * step + u]
            column = cols[n]
            left = stack[4 * lax.shift_right_logical(column, 3) + jnp.bitwise_and(column, 3)]
            slot = jnp.where(2 * step + u < count, slots[n], TRASH)
            terms.append((slot, product(left, hbuf[n])))
        for slot, term in terms:
            acc[slot] += term

    for group in range(3):
        keep_ref[4 * group : 4 * group + 4] = acc[pl.ds(8 * group + 4 * core, 4)]
        send_ref[4 * group : 4 * group + 4] = acc[pl.ds(8 * group + 4 * (1 - core), 4)]
    mine = core == jnp.where(z == 0, 0, 1)
    edge = acc[24:28]
    keep_ref[12:] = jnp.where(mine, edge, 0.0)
    send_ref[12:] = jnp.where(mine, 0.0, edge)


def alpha_kernel(cols, owners, a_ref, h0, h1, after, out_ref, acc, stack, hbuf, sem_h, sem_o):
    chunks = []
    for n in range(4):
        source = (h0, h1)[n // 2].at[pl.ds(16 * (n % 2), 16)]
        chunks.append(pltpu.make_async_copy(source, hbuf.at[pl.ds(16 * n, 16)], sem_h.at[n]))
    for chunk in chunks:
        chunk.start()
    acc[...] = jnp.zeros_like(acc)

    @pl.loop(0, 32)
    def _(j):
        high, low = halves(a_ref[j])
        stack[j, :64] = high
        stack[j, 64:] = low

    for n, chunk in enumerate(chunks):
        chunk.wait()

        @pl.loop(0, 4)
        def _(step, n=n):
            terms = []
            for u in range(4):
                spot = 16 * n + 4 * step + u
                terms.append((owners[spot], product(stack[cols[spot]], hbuf[spot])))
            for owner, term in terms:
                acc[owner] += term

    copy = pltpu.make_async_copy(acc, out_ref, sem_o)
    copy.start()
    copy.wait()


def cores_kernel(keep_ref, got_ref, own_ref, down_ref, up_ref, edge_ref):
    for n, ref in enumerate((own_ref, down_ref, up_ref, edge_ref)):
        ref[...] = keep_ref[4 * n : 4 * n + 4] + got_ref[4 * n : 4 * n + 4]


def planes_kernel(own_ref, down_ref, up_ref, edge_ref, out_ref, token_ref):
    out_ref[...] = (own_ref[...] + down_ref[...]) + (up_ref[...] + edge_ref[...])
    token_ref[...] = jnp.zeros_like(token_ref)


def final_kernel(back_ref, beta_ref, out_ref):
    for t in range(4):
        part = back_ref[8 * t : 8 * (t + 1)]
        total = (part[:, 0] + part[:, 1]) + (part[:, 2] + part[:, 3])
        out_ref[:, 128 * t : 128 * (t + 1)] = jnp.transpose(total.reshape(128, 128)) + beta_ref[t]


def swap(value):
    return lax.ppermute(value, "c", [(0, 1), (1, 0)])


def tables(hcount, hcols, z, c):
    cols = jnp.concatenate([hcols, swap(hcols)])
    marks = jnp.arange(32, dtype=jnp.int32)
    row_end = jnp.sum(jnp.where(marks[:, None] <= marks[None, :], hcount[:, None], 0), axis=0)
    shard = jnp.stack([2 * z + c, 2 * z + 1 - c])
    index = (32 * shard[:, None].astype(jnp.int32) + marks[None, :]).reshape(64)
    owners = jnp.sum((row_end[None, :] <= index[:, None]).astype(jnp.int32), axis=1)
    step = owners // 8 - z
    slots = owners % 8 + jnp.where(step == 0, 0, jnp.where(step == -1, 8, 16))
    slots = jnp.where(step == 2, 24 + owners - 16, jnp.where(step == -2, 24 + owners - 12, slots))
    return cols, owners, jnp.where((cols // 4) % 2 == c, slots, TRASH)


def call(kernel, outs, in_specs, *args, scratch=(), mib=16, work=(0, 1 << 20), space=VMEM):
    single = not isinstance(outs, tuple)
    return pl.pallas_call(
        kernel,
        out_shape=outs,
        in_specs=in_specs,
        out_specs=space if single else (space,) * len(outs),
        scratch_shapes=scratch,
        compiler_params=params(mib),
        cost_estimate=cost(*work),
        name=kernel.__name__,
    )(*args)


def local(coeffs, hblocks, hcount, hcols):
    z, c = lax.axis_index("z"), lax.axis_index("c")
    where = jnp.stack([z, z, z, c]).astype(jnp.int32)
    swapped = swap(hblocks)
    rows = [coeffs] + [
        lax.ppermute(coeffs, "z", [(i, (i + k) % 4) for i in range(4)]) for k in (1, 2, 3)
    ]
    cols, owners, slots = tables(hcount, hcols, z, c)
    at = call(turn_kernel, shape(32, 4, 16, 128), [VMEM], coeffs)
    moved = lax.all_to_all(at.reshape(2048, 128), ROWS + ("z",), 0, 0, tiled=True)

    keep, send = call(
        beta_kernel,
        (shape(16, 128, 128), shape(16, 128, 128)),
        [SMEM] * 3 + [ANY] * 6,
        where, cols, slots, *rows, hblocks, swapped,
        scratch=[
            pltpu.VMEM((4, 128, 512), F32),
            pltpu.VMEM((16, 256, 128), BF16),
            pltpu.VMEM((64, 128, 128), F32),
            pltpu.VMEM((TRASH + 1, 128, 128), F32),
            pltpu.SMEM((72,), jnp.int32),
            pltpu.SemaphoreType.DMA((4,)),
            pltpu.SemaphoreType.DMA((2,)),
        ],
        mib=24,
        work=(BUSY, 7 << 20),
    )
    own, down, up, edge = call(
        cores_kernel, (shape(4, 128, 128),) * 4, [VMEM] * 2, keep, swap(send)
    )
    down = lax.ppermute(down, "z", [(1, 0), (2, 1), (3, 2)])
    up = lax.ppermute(up, "z", [(0, 1), (1, 2), (2, 3)])
    edge = lax.ppermute(edge, "z", [(0, 2), (3, 1)])
    beta, token = call(
        planes_kernel, (shape(4, 128, 128), shape(8, 128)), [VMEM] * 4, own, down, up, edge
    )
    out_a = call(
        alpha_kernel,
        shape(32, 64, 128),
        [SMEM] * 2 + [VMEM] + [ANY] * 2 + [VMEM],
        cols, owners, moved.reshape(32, 64, 128), hblocks, swapped, token,
        scratch=[
            pltpu.VMEM((32, 64, 128), F32),
            pltpu.VMEM((32, 128, 128), BF16),
            pltpu.VMEM((64, 128, 128), F32),
            pltpu.SemaphoreType.DMA((4,)),
            pltpu.SemaphoreType.DMA,
        ],
        mib=24,
        space=pl.BlockSpec(memory_space=pltpu.HBM),
        work=(BUSY, 7 << 20),
    )

    back = lax.all_to_all(out_a.reshape(2048, 128), ROWS + ("z",), 0, 0, tiled=True)
    return call(
        final_kernel, shape(128, 512), [VMEM] * 2, back.reshape(32, 4, 16, 128), beta
    )


def solution(mesh):
    fine = Mesh(mesh.devices.reshape(4, 2, 4, 4, 2), ("y", "h", "x", "z", "c"))
    in_specs = (P(ROWS, ("z", "c")), P(("z", "c"), None, None), P(), P(("z", "c")))
    out_specs = P(ROWS, ("z", "c"))
    return jax.shard_map(local, mesh=fine, in_specs=in_specs, out_specs=out_specs, check_vma=False)
```

```python
import jax
import jax.numpy as jnp
from jax import lax
from jax.experimental import pallas as pl
from jax.experimental.pallas import tpu as pltpu
from jax.sharding import Mesh
from jax.sharding import PartitionSpec as P

ROWS = ("y", "h", "x")
ANY = pl.BlockSpec(memory_space=pl.ANY)
VMEM = pl.BlockSpec(memory_space=pltpu.VMEM)
SMEM = pl.BlockSpec(memory_space=pltpu.SMEM)
F32 = jnp.float32
BF16 = jnp.bfloat16
TRASH = 28
CONTRACT = (((1,), (1,)), ((), ()))

BUSY = 40 * 10**9


def params(mib):
    return pltpu.CompilerParams(vmem_limit_bytes=mib << 20)


def cost(flops, moved):
    return pl.CostEstimate(flops=flops, bytes_accessed=moved, transcendentals=0)


def shape(*dims, kind=F32):
    return jax.ShapeDtypeStruct(dims, kind)


def turn_kernel(c_ref, at_ref):
    for t in range(4):
        turned = jnp.transpose(c_ref[:, 128 * t : 128 * (t + 1)]).reshape(8, 16, 128)
        for plane in range(4):
            at_ref[8 * t : 8 * (t + 1), plane] = turned


def halves(value):
    high = value.astype(BF16)
    return high, (value - high.astype(F32)).astype(BF16)


def product(left, block):
    high, low = halves(block)
    rows = left.shape[0] // 2
    one = lax.dot_general(left, high, CONTRACT, preferred_element_type=F32)
    two = lax.dot_general(left[:rows], low, CONTRACT, preferred_element_type=F32)
    return one[:rows] + (one[rows:] + two)


def beta_kernel(
    where, cols, slots, w0, w1, w2, w3, h0, h1, keep_ref, send_ref,
    wide, stack, hbuf, acc, list_ref, sem_w, sem_h,
):
    z, core = where[2], where[3]
    loads = [
        pltpu.make_async_copy(w, wide.at[k], sem_w.at[k]) for k, w in enumerate((w0, w1, w2, w3))
    ]
    chunks = [
        pltpu.make_async_copy(h, hbuf.at[pl.ds(32 * n, 32)], sem_h.at[n])
        for n, h in enumerate((h0, h1))
    ]
    for copy in loads + chunks:
        copy.start()
    acc[...] = jnp.zeros_like(acc)

    def note(n, count):
        list_ref[count] = n
        return count + jnp.where(slots[n] < TRASH, 1, 0)

    count = lax.fori_loop(0, 64, note, 0)
    list_ref[count] = 0
    for k, load in enumerate(loads):
        home = 4 * jnp.bitwise_and(z - k + 4, 3)
        load.wait()
        for t in range(4):
            high, low = halves(wide[k, :, 128 * t : 128 * (t + 1)])
            stack[home + t, :128] = high
            stack[home + t, 128:] = low
    for chunk in chunks:
        chunk.wait()

    @pl.loop(0, lax.shift_right_logical(count + 1, 1))
    def _(step):
        terms = []
        for u in range(2):
            n = list_ref[2 * step + u]
            column = cols[n]
            left = stack[4 * lax.shift_right_logical(column, 3) + jnp.bitwise_and(column, 3)]
            slot = jnp.where(2 * step + u < count, slots[n], TRASH)
            terms.append((slot, product(left, hbuf[n])))
        for slot, term in terms:
            acc[slot] += term

    for group in range(3):
        keep_ref[4 * group : 4 * group + 4] = acc[pl.ds(8 * group + 4 * core, 4)]
        send_ref[4 * group : 4 * group + 4] = acc[pl.ds(8 * group + 4 * (1 - core), 4)]
    mine = core == jnp.where(z == 0, 0, 1)
    edge = acc[24:28]
    keep_ref[12:] = jnp.where(mine, edge, 0.0)
    send_ref[12:] = jnp.where(mine, 0.0, edge)


def alpha_kernel(
    where, cols, owners, a_ref, h0, h1, after, o0, o1, o2, o3, acc, stack, hbuf, sem_h
):
    z = where[2]
    chunks = []
    for n in range(4):
        source = (h0, h1)[n // 2].at[pl.ds(16 * (n % 2), 16)]
        chunks.append(pltpu.make_async_copy(source, hbuf.at[pl.ds(16 * n, 16)], sem_h.at[n]))
    for chunk in chunks:
        chunk.start()
    acc[...] = jnp.zeros_like(acc)

    @pl.loop(0, 32)
    def _(j):
        for k in range(4):
            home = pl.multiple_of(16 * jnp.bitwise_and(z + k, 3), 16)
            high, low = halves(a_ref[j, pl.ds(home, 16)])
            stack[j, 16 * k : 16 * k + 16] = high
            stack[j, 64 + 16 * k : 80 + 16 * k] = low

    for n, chunk in enumerate(chunks):
        chunk.wait()

        @pl.loop(0, 4)
        def _(step, n=n):
            terms = []
            for u in range(4):
                spot = 16 * n + 4 * step + u
                terms.append((owners[spot], product(stack[cols[spot]], hbuf[spot])))
            for owner, term in terms:
                acc[owner] += term

    for k, ref in enumerate((o0, o1, o2, o3)):
        ref[...] = acc[pl.ds(4 * z, 20), 16 * k : 16 * k + 16]


def strings_kernel(where, after, p0, p1, p2, p3, out_ref):
    z = where[2]
    out_ref[...] = jnp.zeros_like(out_ref)
    for k, part in enumerate((p0, p1, p2, p3)):
        out_ref[pl.ds(4 * jnp.bitwise_and(z - k + 4, 3), 20)] += part[...]


def cores_kernel(keep_ref, got_ref, own_ref, down_ref, up_ref, edge_ref, token_ref):
    token_ref[...] = jnp.zeros_like(token_ref)
    for n, ref in enumerate((own_ref, down_ref, up_ref, edge_ref)):
        ref[...] = keep_ref[4 * n : 4 * n + 4] + got_ref[4 * n : 4 * n + 4]


def planes_kernel(own_ref, down_ref, up_ref, edge_ref, out_ref, token_ref):
    token_ref[...] = jnp.zeros_like(token_ref)
    out_ref[...] = (own_ref[...] + down_ref[...]) + (up_ref[...] + edge_ref[...])


def final_kernel(back_ref, beta_ref, out_ref):
    for t in range(4):
        turned = jnp.transpose(back_ref[8 * t : 8 * (t + 1)].reshape(128, 128))
        out_ref[:, 128 * t : 128 * (t + 1)] = turned + beta_ref[t]


def swap(value):
    return lax.ppermute(value, "c", [(0, 1), (1, 0)])


def shift(value, by):
    return lax.ppermute(value, "z", [(i, (i + by) % 4) for i in range(4)])


def tables(hcount, hcols, z, c):
    cols = jnp.concatenate([hcols, swap(hcols)])
    marks = jnp.arange(32, dtype=jnp.int32)
    row_end = jnp.sum(jnp.where(marks[:, None] <= marks[None, :], hcount[:, None], 0), axis=0)
    shard = jnp.stack([2 * z + c, 2 * z + 1 - c])
    index = (32 * shard[:, None].astype(jnp.int32) + marks[None, :]).reshape(64)
    owners = jnp.sum((row_end[None, :] <= index[:, None]).astype(jnp.int32), axis=1)
    step = owners // 8 - z
    slots = owners % 8 + jnp.where(step == 0, 0, jnp.where(step == -1, 8, 16))
    slots = jnp.where(step == 2, 24 + owners - 16, jnp.where(step == -2, 24 + owners - 12, slots))
    return cols, owners, jnp.where((cols // 4) % 2 == c, slots, TRASH)


def call(kernel, outs, in_specs, *args, scratch=(), mib=16, work=(0, 1 << 20), space=VMEM):
    single = not isinstance(outs, tuple)
    return pl.pallas_call(
        kernel,
        out_shape=outs,
        in_specs=in_specs,
        out_specs=space if single else (space,) * len(outs),
        scratch_shapes=scratch,
        compiler_params=params(mib),
        cost_estimate=cost(*work),
        name=kernel.__name__,
    )(*args)


def local(coeffs, hblocks, hcount, hcols):
    z, c = lax.axis_index("z"), lax.axis_index("c")
    where = jnp.stack([z, z, z, c]).astype(jnp.int32)
    swapped = swap(hblocks)
    rows = [coeffs] + [shift(coeffs, k) for k in (1, 2, 3)]
    cols, owners, slots = tables(hcount, hcols, z, c)
    at = call(turn_kernel, shape(32, 4, 16, 128), [VMEM], coeffs)
    moved = lax.all_to_all(at.reshape(2048, 128), ROWS + ("z",), 0, 0, tiled=True)

    keep, send = call(
        beta_kernel,
        (shape(16, 128, 128), shape(16, 128, 128)),
        [SMEM] * 3 + [ANY] * 6,
        where, cols, slots, *rows, hblocks, swapped,
        scratch=[
            pltpu.VMEM((4, 128, 512), F32),
            pltpu.VMEM((16, 256, 128), BF16),
            pltpu.VMEM((64, 128, 128), F32),
            pltpu.VMEM((TRASH + 1, 128, 128), F32),
            pltpu.SMEM((72,), jnp.int32),
            pltpu.SemaphoreType.DMA((4,)),
            pltpu.SemaphoreType.DMA((2,)),
        ],
        mib=24,
        work=(BUSY, 7 << 20),
    )
    own, down, up, edge, token = call(
        cores_kernel,
        (shape(4, 128, 128),) * 4 + (shape(8, 128),),
        [VMEM] * 2,
        keep, swap(send),
    )
    down = lax.ppermute(down, "z", [(1, 0), (2, 1), (3, 2)])
    up = lax.ppermute(up, "z", [(0, 1), (1, 2), (2, 3)])
    edge = lax.ppermute(edge, "z", [(0, 2), (3, 1)])
    beta, done = call(
        planes_kernel,
        (shape(4, 128, 128), shape(8, 128)),
        [VMEM] * 4,
        own, down, up, edge,
        work=(BUSY, 1 << 20),
    )
    parts = call(
        alpha_kernel,
        (shape(20, 16, 128),) * 4,
        [SMEM] * 3 + [VMEM] + [ANY] * 2 + [VMEM],
        where, cols, owners, moved.reshape(32, 64, 128), hblocks, swapped, token,
        scratch=[
            pltpu.VMEM((32, 64, 128), F32),
            pltpu.VMEM((32, 128, 128), BF16),
            pltpu.VMEM((64, 128, 128), F32),
            pltpu.SemaphoreType.DMA((4,)),
        ],
        mib=24,
        work=(BUSY, 7 << 20),
    )
    parts = [parts[0]] + [shift(parts[k], k) for k in (1, 2, 3)]
    total = call(strings_kernel, shape(32, 16, 128), [SMEM] + [VMEM] * 5, where, done, *parts)
    back = lax.all_to_all(total, ROWS, 0, 0, tiled=True)
    return call(final_kernel, shape(128, 512), [VMEM] * 2, back, beta)


def solution(mesh):
    fine = Mesh(mesh.devices.reshape(4, 2, 4, 4, 2), ("y", "h", "x", "z", "c"))
    in_specs = (P(ROWS, ("z", "c")), P(("z", "c"), None, None), P(), P(("z", "c")))
    out_specs = P(ROWS, ("z", "c"))
    return jax.shard_map(local, mesh=fine, in_specs=in_specs, out_specs=out_specs, check_vma=False)
```

```python
import jax
import jax.numpy as jnp
from jax import lax
from jax.experimental import pallas as pl
from jax.experimental.pallas import tpu as pltpu
from jax.sharding import Mesh
from jax.sharding import PartitionSpec as P

ROWS = ("y", "h", "x")
HBM = pl.BlockSpec(memory_space=pltpu.HBM)
VMEM = pl.BlockSpec(memory_space=pltpu.VMEM)
SMEM = pl.BlockSpec(memory_space=pltpu.SMEM)
F32 = jnp.float32
BF16 = jnp.bfloat16
TRASH = 28
CONTRACT = (((1,), (1,)), ((), ()))

BUSY = 40 * 10**9


def params(mib):
    return pltpu.CompilerParams(vmem_limit_bytes=mib << 20)


def cost(flops, moved):
    return pl.CostEstimate(flops=flops, bytes_accessed=moved, transcendentals=0)


def shape(*dims, kind=F32):
    return jax.ShapeDtypeStruct(dims, kind)


def turn_kernel(c_ref, at_ref):
    for t in range(4):
        turned = jnp.transpose(c_ref[:, 128 * t : 128 * (t + 1)]).reshape(8, 16, 128)
        for plane in range(4):
            at_ref[8 * t : 8 * (t + 1), plane] = turned


def halves(value):
    high = value.astype(BF16)
    return high, (value - high.astype(F32)).astype(BF16)


def product(left, block):
    high, low = halves(block)
    rows = left.shape[0] // 2
    one = lax.dot_general(left, high, CONTRACT, preferred_element_type=F32)
    two = lax.dot_general(left[:rows], low, CONTRACT, preferred_element_type=F32)
    return one[:rows] + (one[rows:] + two)


def beta_kernel(
    where, cols, slots, w0, w1, w2, w3, h0, h1, keep_ref, send_ref,
    wide, stack, hbuf, acc, list_ref, sem_w, sem_h,
):
    z, core = where[2], where[3]
    loads = [
        pltpu.make_async_copy(w, wide.at[k], sem_w.at[k]) for k, w in enumerate((w0, w1, w2, w3))
    ]
    chunks = [
        pltpu.make_async_copy(h, hbuf.at[pl.ds(32 * n, 32)], sem_h.at[n])
        for n, h in enumerate((h0, h1))
    ]
    for copy in loads + chunks:
        copy.start()
    acc[...] = jnp.zeros_like(acc)

    def note(n, count):
        list_ref[count] = n
        return count + jnp.where(slots[n] < TRASH, 1, 0)

    count = lax.fori_loop(0, 64, note, 0)
    list_ref[count] = 0
    for k, load in enumerate(loads):
        home = 4 * jnp.bitwise_and(z - k + 4, 3)
        load.wait()
        for t in range(4):
            high, low = halves(wide[k, :, 128 * t : 128 * (t + 1)])
            stack[home + t, :128] = high
            stack[home + t, 128:] = low
    for chunk in chunks:
        chunk.wait()

    @pl.loop(0, lax.shift_right_logical(count + 1, 1))
    def _(step):
        terms = []
        for u in range(2):
            n = list_ref[2 * step + u]
            column = cols[n]
            left = stack[4 * lax.shift_right_logical(column, 3) + jnp.bitwise_and(column, 3)]
            slot = jnp.where(2 * step + u < count, slots[n], TRASH)
            terms.append((slot, product(left, hbuf[n])))
        for slot, term in terms:
            acc[slot] += term

    for group in range(3):
        keep_ref[4 * group : 4 * group + 4] = acc[pl.ds(8 * group + 4 * core, 4)]
        send_ref[4 * group : 4 * group + 4] = acc[pl.ds(8 * group + 4 * (1 - core), 4)]
    mine = core == jnp.where(z == 0, 0, 1)
    edge = acc[24:28]
    keep_ref[12:] = jnp.where(mine, edge, 0.0)
    send_ref[12:] = jnp.where(mine, 0.0, edge)


def alpha_kernel(
    where, cols, owners, a_ref, h0, h1, after, o0, o1, o2, o3, acc, stack, hbuf, sem_h
):
    z = where[2]
    chunks = []
    for n in range(4):
        source = (h0, h1)[n // 2].at[pl.ds(16 * (n % 2), 16)]
        chunks.append(pltpu.make_async_copy(source, hbuf.at[pl.ds(16 * n, 16)], sem_h.at[n]))
    for chunk in chunks:
        chunk.start()
    acc[...] = jnp.zeros_like(acc)

    @pl.loop(0, 32)
    def _(j):
        for k in range(4):
            home = pl.multiple_of(16 * jnp.bitwise_and(z + k, 3), 16)
            high, low = halves(a_ref[j, pl.ds(home, 16)])
            stack[j, 16 * k : 16 * k + 16] = high
            stack[j, 64 + 16 * k : 80 + 16 * k] = low

    for n, chunk in enumerate(chunks):
        chunk.wait()

        @pl.loop(0, 4)
        def _(step, n=n):
            terms = []
            for u in range(4):
                spot = 16 * n + 4 * step + u
                terms.append((owners[spot], product(stack[cols[spot]], hbuf[spot])))
            for owner, term in terms:
                acc[owner] += term

    for k, ref in enumerate((o0, o1, o2, o3)):
        ref[...] = acc[pl.ds(4 * z, 20), 16 * k : 16 * k + 16]


def strings_kernel(where, after, p0, p1, p2, p3, out_ref):
    z = where[2]
    out_ref[...] = jnp.zeros_like(out_ref)
    for k, part in enumerate((p0, p1, p2, p3)):
        out_ref[pl.ds(4 * jnp.bitwise_and(z - k + 4, 3), 20)] += part[...]


def cores_kernel(keep_ref, got_ref, after, own_ref, down_ref, up_ref, edge_ref, token_ref):
    token_ref[...] = jnp.zeros_like(token_ref)
    for n, ref in enumerate((own_ref, down_ref, up_ref, edge_ref)):
        ref[...] = keep_ref[4 * n : 4 * n + 4] + got_ref[4 * n : 4 * n + 4]


def planes_kernel(own_ref, down_ref, up_ref, edge_ref, out_ref, token_ref):
    token_ref[...] = jnp.zeros_like(token_ref)
    out_ref[...] = (own_ref[...] + down_ref[...]) + (up_ref[...] + edge_ref[...])


def final_kernel(back_ref, beta_ref, out_ref):
    for t in range(4):
        turned = jnp.transpose(back_ref[8 * t : 8 * (t + 1)].reshape(128, 128))
        out_ref[:, 128 * t : 128 * (t + 1)] = turned + beta_ref[t]


def swap(value):
    return lax.ppermute(value, "c", [(0, 1), (1, 0)])


def shift(value, by):
    return lax.ppermute(value, "z", [(i, (i + by) % 4) for i in range(4)])


def tables(hcount, hcols, z, c):
    cols = jnp.concatenate([hcols, swap(hcols)])
    marks = jnp.arange(32, dtype=jnp.int32)
    row_end = jnp.sum(jnp.where(marks[:, None] <= marks[None, :], hcount[:, None], 0), axis=0)
    shard = jnp.stack([2 * z + c, 2 * z + 1 - c])
    index = (32 * shard[:, None].astype(jnp.int32) + marks[None, :]).reshape(64)
    owners = jnp.sum((row_end[None, :] <= index[:, None]).astype(jnp.int32), axis=1)
    step = owners // 8 - z
    slots = owners % 8 + jnp.where(step == 0, 0, jnp.where(step == -1, 8, 16))
    slots = jnp.where(step == 2, 24 + owners - 16, jnp.where(step == -2, 24 + owners - 12, slots))
    return cols, owners, jnp.where((cols // 4) % 2 == c, slots, TRASH)


def call(kernel, outs, in_specs, *args, scratch=(), mib=16, work=(0, 1 << 20), space=VMEM):
    single = not isinstance(outs, tuple)
    return pl.pallas_call(
        kernel,
        out_shape=outs,
        in_specs=in_specs,
        out_specs=space if single else (space,) * len(outs),
        scratch_shapes=scratch,
        compiler_params=params(mib),
        cost_estimate=cost(*work),
        name=kernel.__name__,
    )(*args)


def local(coeffs, hblocks, hcount, hcols):
    z, c = lax.axis_index("z"), lax.axis_index("c")
    where = jnp.stack([z, z, z, c]).astype(jnp.int32)
    swapped = swap(hblocks)
    rows = [coeffs] + [shift(coeffs, k) for k in (1, 2, 3)]
    cols, owners, slots = tables(hcount, hcols, z, c)
    at = call(turn_kernel, shape(32, 4, 16, 128), [VMEM], coeffs)
    moved = lax.all_to_all(at.reshape(2048, 128), ROWS + ("z",), 0, 0, tiled=True)

    keep, send = call(
        beta_kernel,
        (shape(16, 128, 128), shape(16, 128, 128)),
        [SMEM] * 3 + [HBM] * 6,
        where, cols, slots, *rows, hblocks, swapped,
        scratch=[
            pltpu.VMEM((4, 128, 512), F32),
            pltpu.VMEM((16, 256, 128), BF16),
            pltpu.VMEM((64, 128, 128), F32),
            pltpu.VMEM((TRASH + 1, 128, 128), F32),
            pltpu.SMEM((72,), jnp.int32),
            pltpu.SemaphoreType.DMA((4,)),
            pltpu.SemaphoreType.DMA((2,)),
        ],
        mib=24,
        work=(BUSY, 7 << 20),
    )
    own, down, up, edge, token = call(
        cores_kernel,
        (shape(4, 128, 128),) * 4 + (shape(8, 128),),
        [VMEM] * 2 + [HBM],
        keep, swap(send), moved,
    )
    down = lax.ppermute(down, "z", [(1, 0), (2, 1), (3, 2)])
    up = lax.ppermute(up, "z", [(0, 1), (1, 2), (2, 3)])
    edge = lax.ppermute(edge, "z", [(0, 2), (3, 1)])
    beta, done = call(
        planes_kernel,
        (shape(4, 128, 128), shape(8, 128)),
        [VMEM] * 4,
        own, down, up, edge,
        work=(BUSY, 1 << 20),
    )
    parts = call(
        alpha_kernel,
        (shape(20, 16, 128),) * 4,
        [SMEM] * 3 + [VMEM] + [HBM] * 2 + [VMEM],
        where, cols, owners, moved.reshape(32, 64, 128), hblocks, swapped, token,
        scratch=[
            pltpu.VMEM((32, 64, 128), F32),
            pltpu.VMEM((32, 128, 128), BF16),
            pltpu.VMEM((64, 128, 128), F32),
            pltpu.SemaphoreType.DMA((4,)),
        ],
        mib=24,
        work=(BUSY, 7 << 20),
    )
    parts = [parts[0]] + [shift(parts[k], k) for k in (1, 2, 3)]
    total = call(strings_kernel, shape(32, 16, 128), [SMEM] + [VMEM] * 5, where, done, *parts)
    back = lax.all_to_all(total, ROWS, 0, 0, tiled=True)
    return call(final_kernel, shape(128, 512), [VMEM] * 2, back, beta)


def solution(mesh):
    fine = Mesh(mesh.devices.reshape(4, 2, 4, 4, 2), ("y", "h", "x", "z", "c"))
    in_specs = (P(ROWS, ("z", "c")), P(("z", "c"), None, None), P(), P(("z", "c")))
    out_specs = P(ROWS, ("z", "c"))
    return jax.shard_map(local, mesh=fine, in_specs=in_specs, out_specs=out_specs, check_vma=False)
```

```python
import jax
import jax.numpy as jnp
from jax import lax
from jax.experimental import pallas as pl
from jax.experimental.pallas import tpu as pltpu
from jax.sharding import Mesh
from jax.sharding import PartitionSpec as P

ROWS = ("y", "h", "x")
HBM = pl.BlockSpec(memory_space=pltpu.HBM)
VMEM = pl.BlockSpec(memory_space=pltpu.VMEM)
SMEM = pl.BlockSpec(memory_space=pltpu.SMEM)
F32 = jnp.float32
BF16 = jnp.bfloat16
TRASH = 28

BUSY = 40 * 10**9


def params(mib):
    return pltpu.CompilerParams(vmem_limit_bytes=mib << 20)


def cost(flops, moved):
    return pl.CostEstimate(flops=flops, bytes_accessed=moved, transcendentals=0)


def shape(*dims, kind=F32):
    return jax.ShapeDtypeStruct(dims, kind)


def turn_kernel(c_ref, at_ref):
    for t in range(4):
        turned = jnp.transpose(c_ref[:, 128 * t : 128 * (t + 1)]).reshape(8, 16, 128)
        for plane in range(4):
            at_ref[8 * t : 8 * (t + 1), plane] = turned


def halves(value):
    high = value.astype(BF16)
    return high, (value - high.astype(F32)).astype(BF16)


def blocks_kernel(h0, h1, out_ref, hbuf, sem):
    chunks = []
    for n in range(8):
        source = (h0, h1)[n // 4].at[pl.ds(8 * (n % 4), 8)]
        chunks.append(pltpu.make_async_copy(source, hbuf.at[pl.ds(8 * n, 8)], sem.at[n]))
    for chunk in chunks:
        chunk.start()
    for n, chunk in enumerate(chunks):
        chunk.wait()

        @pl.loop(0, 4)
        def _(step, n=n):
            for u in range(2):
                at = 8 * n + 2 * step + u
                high, low = halves(jnp.transpose(hbuf[at]))
                out_ref[at, :, :128] = high
                out_ref[at, :, 128:] = low


def product(left, block):
    rows = left.shape[0] // 2
    both = jnp.dot(left, block, preferred_element_type=F32)
    return both[:rows, :128] + (both[rows:, :128] + both[:rows, 128:])


def beta_kernel(
    where, cols, slots, w0, w1, w2, w3, blocks, keep_ref, send_ref,
    wide, stack, acc, list_ref, sem_w,
):
    z, core = where[2], where[3]
    loads = [
        pltpu.make_async_copy(w, wide.at[k], sem_w.at[k]) for k, w in enumerate((w0, w1, w2, w3))
    ]
    for load in loads:
        load.start()
    acc[...] = jnp.zeros_like(acc)

    def note(n, count):
        list_ref[count] = n
        return count + jnp.where(slots[n] < TRASH, 1, 0)

    count = lax.fori_loop(0, 64, note, 0)
    list_ref[count] = 0
    for k, load in enumerate(loads):
        home = 4 * jnp.bitwise_and(z - k + 4, 3)
        load.wait()
        for t in range(4):
            high, low = halves(wide[k, :, 128 * t : 128 * (t + 1)])
            stack[home + t, :128] = high
            stack[home + t, 128:] = low

    @pl.loop(0, lax.shift_right_logical(count + 1, 1))
    def _(step):
        terms = []
        for u in range(2):
            n = list_ref[2 * step + u]
            column = cols[n]
            left = stack[4 * lax.shift_right_logical(column, 3) + jnp.bitwise_and(column, 3)]
            slot = jnp.where(2 * step + u < count, slots[n], TRASH)
            terms.append((slot, product(left, blocks[n])))
        for slot, term in terms:
            acc[slot] += term

    for group in range(3):
        keep_ref[4 * group : 4 * group + 4] = acc[pl.ds(8 * group + 4 * core, 4)]
        send_ref[4 * group : 4 * group + 4] = acc[pl.ds(8 * group + 4 * (1 - core), 4)]
    mine = core == jnp.where(z == 0, 0, 1)
    edge = acc[24:28]
    keep_ref[12:] = jnp.where(mine, edge, 0.0)
    send_ref[12:] = jnp.where(mine, 0.0, edge)


def alpha_kernel(
    where, cols, owners, a_ref, source, after, o0, o1, o2, o3, acc, stack, blocks, sem
):
    z = where[2]
    chunks = []
    for n in range(8):
        span = pl.ds(8 * n, 8)
        chunks.append(pltpu.make_async_copy(source.at[span], blocks.at[span], sem.at[n]))
    for chunk in chunks:
        chunk.start()
    acc[...] = jnp.zeros_like(acc)

    @pl.loop(0, 32)
    def _(j):
        for k in range(4):
            home = pl.multiple_of(16 * jnp.bitwise_and(z + k, 3), 16)
            high, low = halves(a_ref[j, pl.ds(home, 16)])
            stack[j, 16 * k : 16 * k + 16] = high
            stack[j, 64 + 16 * k : 80 + 16 * k] = low

    for n, chunk in enumerate(chunks):
        chunk.wait()

        @pl.loop(0, 2)
        def _(step, n=n):
            terms = []
            for u in range(4):
                spot = 8 * n + 4 * step + u
                terms.append((owners[spot], product(stack[cols[spot]], blocks[spot])))
            for owner, term in terms:
                acc[owner] += term

    for k, ref in enumerate((o0, o1, o2, o3)):
        ref[...] = acc[pl.ds(4 * z, 20), 16 * k : 16 * k + 16]


def strings_kernel(where, after, p0, p1, p2, p3, out_ref):
    z = where[2]
    out_ref[...] = jnp.zeros_like(out_ref)
    for k, part in enumerate((p0, p1, p2, p3)):
        out_ref[pl.ds(4 * jnp.bitwise_and(z - k + 4, 3), 20)] += part[...]


def cores_kernel(keep_ref, got_ref, own_ref, down_ref, up_ref, edge_ref, token_ref):
    token_ref[...] = jnp.zeros_like(token_ref)
    for n, ref in enumerate((own_ref, down_ref, up_ref, edge_ref)):
        ref[...] = keep_ref[4 * n : 4 * n + 4] + got_ref[4 * n : 4 * n + 4]


def planes_kernel(own_ref, down_ref, up_ref, edge_ref, out_ref, token_ref):
    token_ref[...] = jnp.zeros_like(token_ref)
    out_ref[...] = (own_ref[...] + down_ref[...]) + (up_ref[...] + edge_ref[...])


def final_kernel(back_ref, beta_ref, out_ref):
    for t in range(4):
        turned = jnp.transpose(back_ref[8 * t : 8 * (t + 1)].reshape(128, 128))
        out_ref[:, 128 * t : 128 * (t + 1)] = turned + beta_ref[t]


def swap(value):
    return lax.ppermute(value, "c", [(0, 1), (1, 0)])


def shift(value, by):
    return lax.ppermute(value, "z", [(i, (i + by) % 4) for i in range(4)])


def tables(hcount, hcols, z, c):
    cols = jnp.concatenate([hcols, swap(hcols)])
    marks = jnp.arange(32, dtype=jnp.int32)
    row_end = jnp.sum(jnp.where(marks[:, None] <= marks[None, :], hcount[:, None], 0), axis=0)
    shard = jnp.stack([2 * z + c, 2 * z + 1 - c])
    index = (32 * shard[:, None].astype(jnp.int32) + marks[None, :]).reshape(64)
    owners = jnp.sum((row_end[None, :] <= index[:, None]).astype(jnp.int32), axis=1)
    step = owners // 8 - z
    slots = owners % 8 + jnp.where(step == 0, 0, jnp.where(step == -1, 8, 16))
    slots = jnp.where(step == 2, 24 + owners - 16, jnp.where(step == -2, 24 + owners - 12, slots))
    return cols, owners, jnp.where((cols // 4) % 2 == c, slots, TRASH)


def call(kernel, outs, in_specs, *args, scratch=(), mib=16, work=(0, 1 << 20), space=VMEM):
    single = not isinstance(outs, tuple)
    return pl.pallas_call(
        kernel,
        out_shape=outs,
        in_specs=in_specs,
        out_specs=space if single else (space,) * len(outs),
        scratch_shapes=scratch,
        compiler_params=params(mib),
        cost_estimate=cost(*work),
        name=kernel.__name__,
    )(*args)


def local(coeffs, hblocks, hcount, hcols):
    z, c = lax.axis_index("z"), lax.axis_index("c")
    where = jnp.stack([z, z, z, c]).astype(jnp.int32)
    rows = [coeffs] + [shift(coeffs, k) for k in (1, 2, 3)]
    cols, owners, slots = tables(hcount, hcols, z, c)
    at = call(turn_kernel, shape(32, 4, 16, 128), [VMEM], coeffs)
    moved = lax.all_to_all(at.reshape(2048, 128), ROWS + ("z",), 0, 0, tiled=True)

    blocks = call(
        blocks_kernel,
        shape(64, 128, 256, kind=BF16),
        [HBM] * 2,
        hblocks, swap(hblocks),
        scratch=[pltpu.VMEM((64, 128, 128), F32), pltpu.SemaphoreType.DMA((8,))],
        mib=24,
        work=(0, 8 << 20),
    )
    keep, send = call(
        beta_kernel,
        (shape(16, 128, 128), shape(16, 128, 128)),
        [SMEM] * 3 + [HBM] * 4 + [VMEM],
        where, cols, slots, *rows, blocks,
        scratch=[
            pltpu.VMEM((4, 128, 512), F32),
            pltpu.VMEM((16, 256, 128), BF16),
            pltpu.VMEM((TRASH + 1, 128, 128), F32),
            pltpu.SMEM((72,), jnp.int32),
            pltpu.SemaphoreType.DMA((4,)),
        ],
        mib=24,
        work=(BUSY, 7 << 20),
    )
    own, down, up, edge, token = call(
        cores_kernel,
        (shape(4, 128, 128),) * 4 + (shape(8, 128),),
        [VMEM] * 2,
        keep, swap(send),
    )
    down = lax.ppermute(down, ("z", "c"), [(3, 1), (4, 2), (5, 3), (6, 4), (7, 5)])
    up = lax.ppermute(up, ("z", "c"), [(0, 2), (1, 3), (2, 4), (3, 5), (4, 6)])
    edge = lax.ppermute(edge, ("z", "c"), [(0, 4), (7, 3)])
    beta, done = call(
        planes_kernel,
        (shape(4, 128, 128), shape(8, 128)),
        [VMEM] * 4,
        own, down, up, edge,
        work=(BUSY, 1 << 20),
    )
    parts = call(
        alpha_kernel,
        (shape(20, 16, 128),) * 4,
        [SMEM] * 3 + [VMEM, HBM, VMEM],
        where, cols, owners, moved.reshape(32, 64, 128), blocks, token,
        scratch=[
            pltpu.VMEM((32, 64, 128), F32),
            pltpu.VMEM((32, 128, 128), BF16),
            pltpu.VMEM((64, 128, 256), BF16),
            pltpu.SemaphoreType.DMA((8,)),
        ],
        mib=24,
        work=(BUSY, 7 << 20),
    )
    parts = [parts[0]] + [shift(parts[k], k) for k in (1, 2, 3)]
    total = call(strings_kernel, shape(32, 16, 128), [SMEM] + [VMEM] * 5, where, done, *parts)
    back = lax.all_to_all(total, ROWS, 0, 0, tiled=True)
    return call(final_kernel, shape(128, 512), [VMEM] * 2, back, beta)


def solution(mesh):
    fine = Mesh(mesh.devices.reshape(4, 2, 4, 4, 2), ("y", "h", "x", "z", "c"))
    in_specs = (P(ROWS, ("z", "c")), P(("z", "c"), None, None), P(), P(("z", "c")))
    out_specs = P(ROWS, ("z", "c"))
    return jax.shard_map(local, mesh=fine, in_specs=in_specs, out_specs=out_specs, check_vma=False)
```

```python
import jax
import jax.numpy as jnp
from jax import lax
from jax.experimental import pallas as pl
from jax.experimental.pallas import tpu as pltpu
from jax.sharding import Mesh
from jax.sharding import PartitionSpec as P

ROWS = ("y", "h", "x")
HBM = pl.BlockSpec(memory_space=pltpu.HBM)
VMEM = pl.BlockSpec(memory_space=pltpu.VMEM)
SMEM = pl.BlockSpec(memory_space=pltpu.SMEM)
F32 = jnp.float32
BF16 = jnp.bfloat16
TRASH = 28

BUSY = 40 * 10**9


def params(mib):
    return pltpu.CompilerParams(vmem_limit_bytes=mib << 20)


def cost(flops, moved):
    return pl.CostEstimate(flops=flops, bytes_accessed=moved, transcendentals=0)


def shape(*dims, kind=F32):
    return jax.ShapeDtypeStruct(dims, kind)


def turn_kernel(c_ref, at_ref, buf, sem):
    loads = []
    for t in range(4):
        span = pl.ds(128 * t, 128)
        loads.append(pltpu.make_async_copy(c_ref.at[:, span], buf.at[t], sem.at[t]))
    for load in loads:
        load.start()
    for t, load in enumerate(loads):
        load.wait()
        turned = jnp.transpose(buf[t]).reshape(8, 16, 128)
        for plane in range(4):
            at_ref[8 * t : 8 * (t + 1), plane] = turned


def halves(value):
    high = value.astype(BF16)
    return high, (value - high.astype(F32)).astype(BF16)


def blocks_kernel(h0, h1, out_ref, hbuf, sem):
    chunks = []
    for n in range(8):
        source = (h0, h1)[n // 4].at[pl.ds(8 * (n % 4), 8)]
        chunks.append(pltpu.make_async_copy(source, hbuf.at[pl.ds(8 * n, 8)], sem.at[n]))
    for chunk in chunks:
        chunk.start()
    for n, chunk in enumerate(chunks):
        chunk.wait()

        @pl.loop(0, 4)
        def _(step, n=n):
            for u in range(2):
                at = 8 * n + 2 * step + u
                high, low = halves(jnp.transpose(hbuf[at]))
                out_ref[at, :, :128] = high
                out_ref[at, :, 128:] = low


def product(left, block):
    rows = left.shape[0] // 2
    both = jnp.dot(left, block, preferred_element_type=F32)
    return both[:rows, :128] + (both[rows:, :128] + both[:rows, 128:])


def beta_kernel(
    where, cols, slots, w0, w1, w2, w3, blocks, keep_ref, send_ref,
    wide, stack, acc, list_ref, sem_w,
):
    z, core = where[2], where[3]
    loads = [
        pltpu.make_async_copy(w, wide.at[k], sem_w.at[k]) for k, w in enumerate((w0, w1, w2, w3))
    ]
    for load in loads:
        load.start()
    acc[...] = jnp.zeros_like(acc)

    def note(n, count):
        list_ref[count] = n
        return count + jnp.where(slots[n] < TRASH, 1, 0)

    count = lax.fori_loop(0, 64, note, 0)
    list_ref[count] = 0
    for k, load in enumerate(loads):
        home = 4 * jnp.bitwise_and(z - k + 4, 3)
        load.wait()
        for t in range(4):
            high, low = halves(wide[k, :, 128 * t : 128 * (t + 1)])
            stack[home + t, :128] = high
            stack[home + t, 128:] = low

    @pl.loop(0, lax.shift_right_logical(count + 1, 1))
    def _(step):
        terms = []
        for u in range(2):
            n = list_ref[2 * step + u]
            column = cols[n]
            left = stack[4 * lax.shift_right_logical(column, 3) + jnp.bitwise_and(column, 3)]
            slot = jnp.where(2 * step + u < count, slots[n], TRASH)
            terms.append((slot, product(left, blocks[n])))
        for slot, term in terms:
            acc[slot] += term

    for group in range(3):
        keep_ref[4 * group : 4 * group + 4] = acc[pl.ds(8 * group + 4 * core, 4)]
        send_ref[4 * group : 4 * group + 4] = acc[pl.ds(8 * group + 4 * (1 - core), 4)]
    mine = core == jnp.where(z == 0, 0, 1)
    edge = acc[24:28]
    keep_ref[12:] = jnp.where(mine, edge, 0.0)
    send_ref[12:] = jnp.where(mine, 0.0, edge)


def alpha_kernel(
    where, cols, owners, a_ref, source, after, o0, o1, o2, o3, acc, stack, blocks, sem
):
    z = where[2]
    chunks = []
    for n in range(8):
        span = pl.ds(8 * n, 8)
        chunks.append(pltpu.make_async_copy(source.at[span], blocks.at[span], sem.at[n]))
    for chunk in chunks:
        chunk.start()
    acc[...] = jnp.zeros_like(acc)

    @pl.loop(0, 32)
    def _(j):
        for k in range(4):
            home = pl.multiple_of(16 * jnp.bitwise_and(z + k, 3), 16)
            high, low = halves(a_ref[j, pl.ds(home, 16)])
            stack[j, 16 * k : 16 * k + 16] = high
            stack[j, 64 + 16 * k : 80 + 16 * k] = low

    for n, chunk in enumerate(chunks):
        chunk.wait()

        @pl.loop(0, 2)
        def _(step, n=n):
            terms = []
            for u in range(4):
                spot = 8 * n + 4 * step + u
                terms.append((owners[spot], product(stack[cols[spot]], blocks[spot])))
            for owner, term in terms:
                acc[owner] += term

    for k, ref in enumerate((o0, o1, o2, o3)):
        ref[...] = acc[pl.ds(4 * z, 20), 16 * k : 16 * k + 16]


def strings_kernel(where, after, p0, p1, p2, p3, out_ref):
    z = where[2]
    out_ref[...] = jnp.zeros_like(out_ref)
    for k, part in enumerate((p0, p1, p2, p3)):
        out_ref[pl.ds(4 * jnp.bitwise_and(z - k + 4, 3), 20)] += part[...]


def cores_kernel(keep_ref, got_ref, own_ref, down_ref, up_ref, edge_ref, token_ref):
    token_ref[...] = jnp.zeros_like(token_ref)
    for n, ref in enumerate((own_ref, down_ref, up_ref, edge_ref)):
        ref[...] = keep_ref[4 * n : 4 * n + 4] + got_ref[4 * n : 4 * n + 4]


def planes_kernel(own_ref, down_ref, up_ref, edge_ref, out_ref, token_ref):
    token_ref[...] = jnp.zeros_like(token_ref)
    out_ref[...] = (own_ref[...] + down_ref[...]) + (up_ref[...] + edge_ref[...])


def final_kernel(back_ref, beta_ref, out_ref):
    for t in range(4):
        turned = jnp.transpose(back_ref[8 * t : 8 * (t + 1)].reshape(128, 128))
        out_ref[:, 128 * t : 128 * (t + 1)] = turned + beta_ref[t]


def swap(value):
    return lax.ppermute(value, "c", [(0, 1), (1, 0)])


def shift(value, by):
    return lax.ppermute(value, "z", [(i, (i + by) % 4) for i in range(4)])


def tables(hcount, hcols, z, c):
    cols = jnp.concatenate([hcols, swap(hcols)])
    marks = jnp.arange(32, dtype=jnp.int32)
    row_end = jnp.sum(jnp.where(marks[:, None] <= marks[None, :], hcount[:, None], 0), axis=0)
    shard = jnp.stack([2 * z + c, 2 * z + 1 - c])
    index = (32 * shard[:, None].astype(jnp.int32) + marks[None, :]).reshape(64)
    owners = jnp.sum((row_end[None, :] <= index[:, None]).astype(jnp.int32), axis=1)
    step = owners // 8 - z
    slots = owners % 8 + jnp.where(step == 0, 0, jnp.where(step == -1, 8, 16))
    slots = jnp.where(step == 2, 24 + owners - 16, jnp.where(step == -2, 24 + owners - 12, slots))
    return cols, owners, jnp.where((cols // 4) % 2 == c, slots, TRASH)


def call(kernel, outs, in_specs, *args, scratch=(), mib=16, work=(0, 1 << 20), space=VMEM):
    single = not isinstance(outs, tuple)
    return pl.pallas_call(
        kernel,
        out_shape=outs,
        in_specs=in_specs,
        out_specs=space if single else (space,) * len(outs),
        scratch_shapes=scratch,
        compiler_params=params(mib),
        cost_estimate=cost(*work),
        name=kernel.__name__,
    )(*args)


def local(coeffs, hblocks, hcount, hcols):
    z, c = lax.axis_index("z"), lax.axis_index("c")
    where = jnp.stack([z, z, z, c]).astype(jnp.int32)
    rows = [coeffs] + [shift(coeffs, k) for k in (1, 2, 3)]
    cols, owners, slots = tables(hcount, hcols, z, c)
    at = call(
        turn_kernel,
        shape(32, 4, 16, 128),
        [HBM],
        pltpu.with_memory_space_constraint(coeffs, pltpu.HBM),
        scratch=[pltpu.VMEM((4, 128, 128), F32), pltpu.SemaphoreType.DMA((4,))],
    )
    moved = lax.all_to_all(at.reshape(2048, 128), ROWS + ("z",), 0, 0, tiled=True)

    blocks = call(
        blocks_kernel,
        shape(64, 128, 256, kind=BF16),
        [HBM] * 2,
        hblocks, swap(hblocks),
        scratch=[pltpu.VMEM((64, 128, 128), F32), pltpu.SemaphoreType.DMA((8,))],
        mib=24,
        work=(0, 8 << 20),
    )
    keep, send = call(
        beta_kernel,
        (shape(16, 128, 128), shape(16, 128, 128)),
        [SMEM] * 3 + [HBM] * 4 + [VMEM],
        where, cols, slots, *rows, blocks,
        scratch=[
            pltpu.VMEM((4, 128, 512), F32),
            pltpu.VMEM((16, 256, 128), BF16),
            pltpu.VMEM((TRASH + 1, 128, 128), F32),
            pltpu.SMEM((72,), jnp.int32),
            pltpu.SemaphoreType.DMA((4,)),
        ],
        mib=24,
        work=(BUSY, 7 << 20),
    )
    own, down, up, edge, token = call(
        cores_kernel,
        (shape(4, 128, 128),) * 4 + (shape(8, 128),),
        [VMEM] * 2,
        keep, swap(send),
    )
    down = lax.ppermute(down, ("z", "c"), [(3, 1), (4, 2), (5, 3), (6, 4), (7, 5)])
    up = lax.ppermute(up, ("z", "c"), [(0, 2), (1, 3), (2, 4), (3, 5), (4, 6)])
    edge = lax.ppermute(edge, ("z", "c"), [(0, 4), (7, 3)])
    beta, done = call(
        planes_kernel,
        (shape(4, 128, 128), shape(8, 128)),
        [VMEM] * 4,
        own, down, up, edge,
        work=(BUSY, 1 << 20),
    )
    parts = call(
        alpha_kernel,
        (shape(20, 16, 128),) * 4,
        [SMEM] * 3 + [VMEM, HBM, VMEM],
        where, cols, owners, moved.reshape(32, 64, 128),
        pltpu.with_memory_space_constraint(blocks, pltpu.HBM), token,
        scratch=[
            pltpu.VMEM((32, 64, 128), F32),
            pltpu.VMEM((32, 128, 128), BF16),
            pltpu.VMEM((64, 128, 256), BF16),
            pltpu.SemaphoreType.DMA((8,)),
        ],
        mib=24,
        work=(BUSY, 7 << 20),
    )
    parts = [parts[0]] + [shift(parts[k], k) for k in (1, 2, 3)]
    total = call(strings_kernel, shape(32, 16, 128), [SMEM] + [VMEM] * 5, where, done, *parts)
    back = lax.all_to_all(total, ROWS, 0, 0, tiled=True)
    return call(final_kernel, shape(128, 512), [VMEM] * 2, back, beta)


def solution(mesh):
    fine = Mesh(mesh.devices.reshape(4, 2, 4, 4, 2), ("y", "h", "x", "z", "c"))
    in_specs = (P(ROWS, ("z", "c")), P(("z", "c"), None, None), P(), P(("z", "c")))
    out_specs = P(ROWS, ("z", "c"))
    return jax.shard_map(local, mesh=fine, in_specs=in_specs, out_specs=out_specs, check_vma=False)
```

```python
import jax
import jax.numpy as jnp
from jax import lax
from jax.experimental import pallas as pl
from jax.experimental.pallas import tpu as pltpu
from jax.sharding import Mesh
from jax.sharding import PartitionSpec as P

ROWS = ("y", "h", "x")
HBM = pl.BlockSpec(memory_space=pltpu.HBM)
VMEM = pl.BlockSpec(memory_space=pltpu.VMEM)
SMEM = pl.BlockSpec(memory_space=pltpu.SMEM)
F32 = jnp.float32
BF16 = jnp.bfloat16
TRASH = 28

BUSY = 40 * 10**9


def params(mib):
    return pltpu.CompilerParams(vmem_limit_bytes=mib << 20)


def cost(flops, moved):
    return pl.CostEstimate(flops=flops, bytes_accessed=moved, transcendentals=0)


def shape(*dims, kind=F32):
    return jax.ShapeDtypeStruct(dims, kind)


def turn_kernel(c_ref, at_ref, buf, sem):
    loads = []
    for t in range(4):
        span = pl.ds(128 * t, 128)
        loads.append(pltpu.make_async_copy(c_ref.at[:, span], buf.at[t], sem.at[t]))
    for load in loads:
        load.start()
    for t, load in enumerate(loads):
        load.wait()
        turned = jnp.transpose(buf[t]).reshape(8, 16, 128)
        for plane in range(4):
            at_ref[8 * t : 8 * (t + 1), plane] = turned


def halves(value):
    high = value.astype(BF16)
    return high, (value - high.astype(F32)).astype(BF16)


def blocks_kernel(h0, h1, out_ref, hbuf, sem):
    chunks = []
    for n in range(8):
        source = (h0, h1)[n // 4].at[pl.ds(8 * (n % 4), 8)]
        chunks.append(pltpu.make_async_copy(source, hbuf.at[pl.ds(8 * n, 8)], sem.at[n]))
    for chunk in chunks:
        chunk.start()
    for n, chunk in enumerate(chunks):
        chunk.wait()

        @pl.loop(0, 4)
        def _(step, n=n):
            for u in range(2):
                at = 8 * n + 2 * step + u
                high, low = halves(jnp.transpose(hbuf[at]))
                out_ref[at, :, :128] = high
                out_ref[at, :, 128:] = low


def product(left, block):
    rows = left.shape[0] // 2
    both = jnp.dot(left, block, preferred_element_type=F32)
    return both[:rows, :128] + (both[rows:, :128] + both[:rows, 128:])


def beta_kernel(
    where, cols, slots, w0, w1, w2, w3, w4, blocks, keep_ref, send_ref,
    wide, stack, acc, list_ref, sem_w,
):
    z, core = where[2], where[3]
    homes = (
        z,
        jnp.where(z > 0, z - 1, 4),
        jnp.bitwise_xor(z, 2),
        jnp.where(z < 3, z + 1, 4),
        jnp.where(z == 0, 3, jnp.where(z == 3, 0, 4)),
    )
    loads = [
        pltpu.make_async_copy(w, wide.at[k], sem_w.at[k])
        for k, w in enumerate((w0, w1, w2, w3, w4))
    ]
    for load in loads:
        load.start()
    acc[...] = jnp.zeros_like(acc)

    def note(n, count):
        list_ref[count] = n
        return count + jnp.where(slots[n] < TRASH, 1, 0)

    count = lax.fori_loop(0, 64, note, 0)
    list_ref[count] = 0
    for k, load in enumerate(loads):
        home = 4 * homes[k]
        load.wait()
        for t in range(4):
            high, low = halves(wide[k, :, 128 * t : 128 * (t + 1)])
            stack[home + t, :128] = high
            stack[home + t, 128:] = low

    @pl.loop(0, lax.shift_right_logical(count + 1, 1))
    def _(step):
        terms = []
        for u in range(2):
            n = list_ref[2 * step + u]
            column = cols[n]
            left = stack[4 * lax.shift_right_logical(column, 3) + jnp.bitwise_and(column, 3)]
            slot = jnp.where(2 * step + u < count, slots[n], TRASH)
            terms.append((slot, product(left, blocks[n])))
        for slot, term in terms:
            acc[slot] += term

    for group in range(3):
        keep_ref[4 * group : 4 * group + 4] = acc[pl.ds(8 * group + 4 * core, 4)]
        send_ref[4 * group : 4 * group + 4] = acc[pl.ds(8 * group + 4 * (1 - core), 4)]
    mine = core == jnp.where(z == 0, 0, 1)
    edge = acc[24:28]
    keep_ref[12:] = jnp.where(mine, edge, 0.0)
    send_ref[12:] = jnp.where(mine, 0.0, edge)


def alpha_kernel(
    where, cols, owners, a_ref, source, after, o0, o1, o2, o3, acc, stack, blocks, sem
):
    z = where[2]
    chunks = []
    for n in range(8):
        span = pl.ds(8 * n, 8)
        chunks.append(pltpu.make_async_copy(source.at[span], blocks.at[span], sem.at[n]))
    for chunk in chunks:
        chunk.start()
    acc[...] = jnp.zeros_like(acc)

    @pl.loop(0, 32)
    def _(j):
        for k in range(4):
            home = pl.multiple_of(16 * jnp.bitwise_and(z + k, 3), 16)
            high, low = halves(a_ref[j, pl.ds(home, 16)])
            stack[j, 16 * k : 16 * k + 16] = high
            stack[j, 64 + 16 * k : 80 + 16 * k] = low

    for n, chunk in enumerate(chunks):
        chunk.wait()

        for first in (8 * n, 8 * n + 4):
            terms = []
            for spot in range(first, first + 4):
                terms.append((owners[spot], product(stack[cols[spot]], blocks[spot])))
            for owner, term in terms:
                acc[owner] += term

    for k, ref in enumerate((o0, o1, o2, o3)):
        ref[...] = acc[pl.ds(4 * z, 20), 16 * k : 16 * k + 16]


def strings_kernel(where, after, p0, p1, p2, p3, out_ref):
    z = where[2]
    out_ref[...] = jnp.zeros_like(out_ref)
    for k, part in enumerate((p0, p1, p2, p3)):
        out_ref[pl.ds(4 * jnp.bitwise_and(z - k + 4, 3), 20)] += part[...]


def cores_kernel(keep_ref, got_ref, own_ref, down_ref, up_ref, edge_ref, token_ref):
    token_ref[...] = jnp.zeros_like(token_ref)
    for n, ref in enumerate((own_ref, down_ref, up_ref, edge_ref)):
        ref[...] = keep_ref[4 * n : 4 * n + 4] + got_ref[4 * n : 4 * n + 4]


def planes_kernel(own_ref, down_ref, up_ref, edge_ref, out_ref, token_ref):
    token_ref[...] = jnp.zeros_like(token_ref)
    out_ref[...] = (own_ref[...] + down_ref[...]) + (up_ref[...] + edge_ref[...])


def final_kernel(back_ref, beta_ref, out_ref):
    for t in range(4):
        turned = jnp.transpose(back_ref[8 * t : 8 * (t + 1)].reshape(128, 128))
        out_ref[:, 128 * t : 128 * (t + 1)] = turned + beta_ref[t]


def swap(value):
    return lax.ppermute(value, "c", [(0, 1), (1, 0)])


def shift(value, by):
    return lax.ppermute(value, "z", [(i, (i + by) % 4) for i in range(4)])


def tables(hcount, hcols, z, c):
    cols = jnp.concatenate([hcols, swap(hcols)])
    marks = jnp.arange(32, dtype=jnp.int32)
    row_end = jnp.sum(jnp.where(marks[:, None] <= marks[None, :], hcount[:, None], 0), axis=0)
    shard = jnp.stack([2 * z + c, 2 * z + 1 - c])
    index = (32 * shard[:, None].astype(jnp.int32) + marks[None, :]).reshape(64)
    owners = jnp.sum((row_end[None, :] <= index[:, None]).astype(jnp.int32), axis=1)
    step = owners // 8 - z
    slots = owners % 8 + jnp.where(step == 0, 0, jnp.where(step == -1, 8, 16))
    slots = jnp.where(step == 2, 24 + owners - 16, jnp.where(step == -2, 24 + owners - 12, slots))
    return cols, owners, jnp.where((cols // 4) % 2 == c, slots, TRASH)


def call(kernel, outs, in_specs, *args, scratch=(), mib=16, work=(0, 1 << 20), space=VMEM):
    single = not isinstance(outs, tuple)
    return pl.pallas_call(
        kernel,
        out_shape=outs,
        in_specs=in_specs,
        out_specs=space if single else (space,) * len(outs),
        scratch_shapes=scratch,
        compiler_params=params(mib),
        cost_estimate=cost(*work),
        name=kernel.__name__,
    )(*args)


def local(coeffs, hblocks, hcount, hcols):
    z, c = lax.axis_index("z"), lax.axis_index("c")
    where = jnp.stack([z, z, z, c]).astype(jnp.int32)
    below = lax.ppermute(coeffs, "z", [(0, 1), (1, 2), (2, 3)])
    across = shift(coeffs, 2)
    above = lax.ppermute(coeffs, "z", [(1, 0), (2, 1), (3, 2)])
    rows = [coeffs, below, across, above, lax.ppermute(across, "z", [(1, 0), (2, 3)])]
    cols, owners, slots = tables(hcount, hcols, z, c)
    at = call(
        turn_kernel,
        shape(32, 4, 16, 128),
        [HBM],
        pltpu.with_memory_space_constraint(coeffs, pltpu.HBM),
        scratch=[pltpu.VMEM((4, 128, 128), F32), pltpu.SemaphoreType.DMA((4,))],
    )
    moved = lax.all_to_all(at.reshape(2048, 128), ROWS + ("z",), 0, 0, tiled=True)

    blocks = call(
        blocks_kernel,
        shape(64, 128, 256, kind=BF16),
        [HBM] * 2,
        hblocks, swap(hblocks),
        scratch=[pltpu.VMEM((64, 128, 128), F32), pltpu.SemaphoreType.DMA((8,))],
        mib=24,
        work=(0, 8 << 20),
    )
    keep, send = call(
        beta_kernel,
        (shape(16, 128, 128), shape(16, 128, 128)),
        [SMEM] * 3 + [HBM] * 5 + [VMEM],
        where, cols, slots, *rows, blocks,
        scratch=[
            pltpu.VMEM((5, 128, 512), F32),
            pltpu.VMEM((20, 256, 128), BF16),
            pltpu.VMEM((TRASH + 1, 128, 128), F32),
            pltpu.SMEM((72,), jnp.int32),
            pltpu.SemaphoreType.DMA((5,)),
        ],
        mib=24,
        work=(BUSY, 7 << 20),
    )
    own, down, up, edge, token = call(
        cores_kernel,
        (shape(4, 128, 128),) * 4 + (shape(8, 128),),
        [VMEM] * 2,
        keep, swap(send),
    )
    down = lax.ppermute(down, ("z", "c"), [(3, 1), (4, 2), (5, 3), (6, 4), (7, 5)])
    up = lax.ppermute(up, ("z", "c"), [(0, 2), (1, 3), (2, 4), (3, 5), (4, 6)])
    edge = lax.ppermute(edge, ("z", "c"), [(0, 4), (7, 3)])
    beta, done = call(
        planes_kernel,
        (shape(4, 128, 128), shape(8, 128)),
        [VMEM] * 4,
        own, down, up, edge,
        work=(BUSY, 1 << 20),
    )
    parts = call(
        alpha_kernel,
        (shape(20, 16, 128),) * 4,
        [SMEM] * 3 + [VMEM, HBM, VMEM],
        where, cols, owners, moved.reshape(32, 64, 128),
        pltpu.with_memory_space_constraint(blocks, pltpu.HBM), token,
        scratch=[
            pltpu.VMEM((32, 64, 128), F32),
            pltpu.VMEM((32, 128, 128), BF16),
            pltpu.VMEM((64, 128, 256), BF16),
            pltpu.SemaphoreType.DMA((8,)),
        ],
        mib=24,
        work=(BUSY, 7 << 20),
    )
    parts = [parts[0]] + [shift(parts[k], k) for k in (1, 2, 3)]
    total = call(strings_kernel, shape(32, 16, 128), [SMEM] + [VMEM] * 5, where, done, *parts)
    back = lax.all_to_all(total, ROWS, 0, 0, tiled=True)
    return call(final_kernel, shape(128, 512), [VMEM] * 2, back, beta)


def solution(mesh):
    fine = Mesh(mesh.devices.reshape(4, 2, 4, 4, 2), ("y", "h", "x", "z", "c"))
    in_specs = (P(ROWS, ("z", "c")), P(("z", "c"), None, None), P(), P(("z", "c")))
    out_specs = P(ROWS, ("z", "c"))
    return jax.shard_map(local, mesh=fine, in_specs=in_specs, out_specs=out_specs, check_vma=False)
```

```python
import jax
import jax.numpy as jnp
from jax import lax
from jax.experimental import pallas as pl
from jax.experimental.pallas import tpu as pltpu
from jax.sharding import Mesh
from jax.sharding import PartitionSpec as P

ROWS = ("y", "h", "x")
HBM = pl.BlockSpec(memory_space=pltpu.HBM)
VMEM = pl.BlockSpec(memory_space=pltpu.VMEM)
SMEM = pl.BlockSpec(memory_space=pltpu.SMEM)
F32 = jnp.float32
BF16 = jnp.bfloat16
TRASH = 28

BUSY = 40 * 10**9


def params(mib):
    return pltpu.CompilerParams(vmem_limit_bytes=mib << 20)


def cost(flops, moved):
    return pl.CostEstimate(flops=flops, bytes_accessed=moved, transcendentals=0)


def shape(*dims, kind=F32):
    return jax.ShapeDtypeStruct(dims, kind)


def turn_kernel(c_ref, at_ref, buf, turned, sem, out_sem):
    loads, stores = [], []
    for t in range(4):
        span = pl.ds(128 * t, 128)
        loads.append(pltpu.make_async_copy(c_ref.at[:, span], buf.at[t], sem.at[t]))
        for plane in range(4):
            home = at_ref.at[pl.ds(8 * t, 8), plane]
            stores.append(pltpu.make_async_copy(turned.at[t], home, out_sem.at[t, plane]))
    for load in loads:
        load.start()
    for t, load in enumerate(loads):
        load.wait()
        turned[t] = jnp.transpose(buf[t]).reshape(8, 16, 128)
        for store in stores[4 * t : 4 * t + 4]:
            store.start()
    for store in stores:
        store.wait()


def halves(value):
    high = value.astype(BF16)
    return high, (value - high.astype(F32)).astype(BF16)


def blocks_kernel(h0, h1, out_ref, hbuf, sem):
    chunks = []
    for n in range(8):
        source = (h0, h1)[n // 4].at[pl.ds(8 * (n % 4), 8)]
        chunks.append(pltpu.make_async_copy(source, hbuf.at[pl.ds(8 * n, 8)], sem.at[n]))
    for chunk in chunks:
        chunk.start()
    for n, chunk in enumerate(chunks):
        chunk.wait()

        @pl.loop(0, 4)
        def _(step, n=n):
            for u in range(2):
                at = 8 * n + 2 * step + u
                high, low = halves(jnp.transpose(hbuf[at]))
                out_ref[at, :, :128] = high
                out_ref[at, :, 128:] = low


def product(left, block):
    rows = left.shape[0] // 2
    both = jnp.dot(left, block, preferred_element_type=F32)
    return both[:rows, :128] + (both[rows:, :128] + both[:rows, 128:])


def beta_kernel(
    where, cols, slots, w0, w1, w2, w3, blocks, keep_ref, send_ref,
    wide, stack, acc, list_ref, sem_w,
):
    z, core = where[2], where[3]
    loads = [
        pltpu.make_async_copy(w, wide.at[k], sem_w.at[k]) for k, w in enumerate((w0, w1, w2, w3))
    ]
    for load in loads:
        load.start()
    acc[...] = jnp.zeros_like(acc)

    def note(n, count):
        list_ref[count] = n
        return count + jnp.where(slots[n] < TRASH, 1, 0)

    count = lax.fori_loop(0, 64, note, 0)
    list_ref[count] = 0
    for k, load in enumerate(loads):
        home = 4 * jnp.bitwise_and(z - k + 4, 3)
        load.wait()
        for t in range(4):
            high, low = halves(wide[k, :, 128 * t : 128 * (t + 1)])
            stack[home + t, :128] = high
            stack[home + t, 128:] = low

    @pl.loop(0, lax.shift_right_logical(count + 1, 1))
    def _(step):
        terms = []
        for u in range(2):
            n = list_ref[2 * step + u]
            column = cols[n]
            left = stack[4 * lax.shift_right_logical(column, 3) + jnp.bitwise_and(column, 3)]
            slot = jnp.where(2 * step + u < count, slots[n], TRASH)
            terms.append((slot, product(left, blocks[n])))
        for slot, term in terms:
            acc[slot] += term

    for group in range(3):
        keep_ref[4 * group : 4 * group + 4] = acc[pl.ds(8 * group + 4 * core, 4)]
        send_ref[4 * group : 4 * group + 4] = acc[pl.ds(8 * group + 4 * (1 - core), 4)]
    mine = core == jnp.where(z == 0, 0, 1)
    edge = acc[24:28]
    keep_ref[12:] = jnp.where(mine, edge, 0.0)
    send_ref[12:] = jnp.where(mine, 0.0, edge)


def alpha_kernel(
    where, cols, owners, a_ref, source, after, o0, o1, o2, o3, acc, stack, blocks, sem
):
    z = where[2]
    chunks = []
    for n in range(8):
        span = pl.ds(8 * n, 8)
        chunks.append(pltpu.make_async_copy(source.at[span], blocks.at[span], sem.at[n]))
    for chunk in chunks:
        chunk.start()
    acc[...] = jnp.zeros_like(acc)

    @pl.loop(0, 32)
    def _(j):
        for k in range(4):
            home = pl.multiple_of(16 * jnp.bitwise_and(z + k, 3), 16)
            high, low = halves(a_ref[j, pl.ds(home, 16)])
            stack[j, 16 * k : 16 * k + 16] = high
            stack[j, 64 + 16 * k : 80 + 16 * k] = low

    for n, chunk in enumerate(chunks):
        chunk.wait()

        for first in (8 * n, 8 * n + 4):
            terms = []
            for spot in range(first, first + 4):
                terms.append((owners[spot], product(stack[cols[spot]], blocks[spot])))
            for owner, term in terms:
                acc[owner] += term

    for k, ref in enumerate((o0, o1, o2, o3)):
        ref[...] = acc[pl.ds(4 * z, 20), 16 * k : 16 * k + 16]


def strings_kernel(where, after, p0, p1, p2, p3, out_ref):
    z = where[2]
    out_ref[...] = jnp.zeros_like(out_ref)
    for k, part in enumerate((p0, p1, p2, p3)):
        out_ref[pl.ds(4 * jnp.bitwise_and(z - k + 4, 3), 20)] += part[...]


def cores_kernel(keep_ref, got_ref, own_ref, down_ref, up_ref, edge_ref, token_ref):
    token_ref[...] = jnp.zeros_like(token_ref)
    for n, ref in enumerate((own_ref, down_ref, up_ref, edge_ref)):
        ref[...] = keep_ref[4 * n : 4 * n + 4] + got_ref[4 * n : 4 * n + 4]


def planes_kernel(own_ref, down_ref, up_ref, edge_ref, out_ref, token_ref):
    token_ref[...] = jnp.zeros_like(token_ref)
    out_ref[...] = (own_ref[...] + down_ref[...]) + (up_ref[...] + edge_ref[...])


def final_kernel(back_ref, beta_ref, out_ref):
    for t in range(4):
        turned = jnp.transpose(back_ref[8 * t : 8 * (t + 1)].reshape(128, 128))
        out_ref[:, 128 * t : 128 * (t + 1)] = turned + beta_ref[t]


def swap(value):
    return lax.ppermute(value, "c", [(0, 1), (1, 0)])


def shift(value, by):
    return lax.ppermute(value, "z", [(i, (i + by) % 4) for i in range(4)])


def tables(hcount, hcols, z, c):
    cols = jnp.concatenate([hcols, swap(hcols)])
    marks = jnp.arange(32, dtype=jnp.int32)
    row_end = jnp.sum(jnp.where(marks[:, None] <= marks[None, :], hcount[:, None], 0), axis=0)
    shard = jnp.stack([2 * z + c, 2 * z + 1 - c])
    index = (32 * shard[:, None].astype(jnp.int32) + marks[None, :]).reshape(64)
    owners = jnp.sum((row_end[None, :] <= index[:, None]).astype(jnp.int32), axis=1)
    step = owners // 8 - z
    slots = owners % 8 + jnp.where(step == 0, 0, jnp.where(step == -1, 8, 16))
    slots = jnp.where(step == 2, 24 + owners - 16, jnp.where(step == -2, 24 + owners - 12, slots))
    return cols, owners, jnp.where((cols // 4) % 2 == c, slots, TRASH)


def call(kernel, outs, in_specs, *args, scratch=(), mib=16, work=(0, 1 << 20), space=VMEM):
    single = not isinstance(outs, tuple)
    return pl.pallas_call(
        kernel,
        out_shape=outs,
        in_specs=in_specs,
        out_specs=space if single else (space,) * len(outs),
        scratch_shapes=scratch,
        compiler_params=params(mib),
        cost_estimate=cost(*work),
        name=kernel.__name__,
    )(*args)


def local(coeffs, hblocks, hcount, hcols):
    z, c = lax.axis_index("z"), lax.axis_index("c")
    where = jnp.stack([z, z, z, c]).astype(jnp.int32)
    rows = [coeffs] + [shift(coeffs, k) for k in (1, 2, 3)]
    cols, owners, slots = tables(hcount, hcols, z, c)
    at = call(
        turn_kernel,
        shape(32, 4, 16, 128),
        [HBM],
        pltpu.with_memory_space_constraint(coeffs, pltpu.HBM),
        scratch=[
            pltpu.VMEM((4, 128, 128), F32),
            pltpu.VMEM((4, 8, 16, 128), F32),
            pltpu.SemaphoreType.DMA((4,)),
            pltpu.SemaphoreType.DMA((4, 4)),
        ],
        space=HBM,
    )
    moved = lax.all_to_all(at.reshape(2048, 128), ROWS + ("z",), 0, 0, tiled=True)

    blocks = call(
        blocks_kernel,
        shape(64, 128, 256, kind=BF16),
        [HBM] * 2,
        hblocks, swap(hblocks),
        scratch=[pltpu.VMEM((64, 128, 128), F32), pltpu.SemaphoreType.DMA((8,))],
        mib=24,
        work=(0, 8 << 20),
    )
    keep, send = call(
        beta_kernel,
        (shape(16, 128, 128), shape(16, 128, 128)),
        [SMEM] * 3 + [HBM] * 4 + [VMEM],
        where, cols, slots, *rows, blocks,
        scratch=[
            pltpu.VMEM((4, 128, 512), F32),
            pltpu.VMEM((16, 256, 128), BF16),
            pltpu.VMEM((TRASH + 1, 128, 128), F32),
            pltpu.SMEM((72,), jnp.int32),
            pltpu.SemaphoreType.DMA((4,)),
        ],
        mib=24,
        work=(BUSY, 7 << 20),
    )
    own, down, up, edge, token = call(
        cores_kernel,
        (shape(4, 128, 128),) * 4 + (shape(8, 128),),
        [VMEM] * 2,
        keep, swap(send),
    )
    down = lax.ppermute(down, ("z", "c"), [(3, 1), (4, 2), (5, 3), (6, 4), (7, 5)])
    up = lax.ppermute(up, ("z", "c"), [(0, 2), (1, 3), (2, 4), (3, 5), (4, 6)])
    edge = lax.ppermute(edge, ("z", "c"), [(0, 4), (7, 3)])
    beta, done = call(
        planes_kernel,
        (shape(4, 128, 128), shape(8, 128)),
        [VMEM] * 4,
        own, down, up, edge,
        work=(BUSY, 1 << 20),
    )
    parts = call(
        alpha_kernel,
        (shape(20, 16, 128),) * 4,
        [SMEM] * 3 + [VMEM, HBM, VMEM],
        where, cols, owners, moved.reshape(32, 64, 128),
        pltpu.with_memory_space_constraint(blocks, pltpu.HBM), token,
        scratch=[
            pltpu.VMEM((32, 64, 128), F32),
            pltpu.VMEM((32, 128, 128), BF16),
            pltpu.VMEM((64, 128, 256), BF16),
            pltpu.SemaphoreType.DMA((8,)),
        ],
        mib=24,
        work=(BUSY, 7 << 20),
    )
    parts = [parts[0]] + [shift(parts[k], k) for k in (1, 2, 3)]
    total = call(strings_kernel, shape(32, 16, 128), [SMEM] + [VMEM] * 5, where, done, *parts)
    back = lax.all_to_all(total, ROWS, 0, 0, tiled=True)
    return call(final_kernel, shape(128, 512), [VMEM] * 2, back, beta)


def solution(mesh):
    fine = Mesh(mesh.devices.reshape(4, 2, 4, 4, 2), ("y", "h", "x", "z", "c"))
    in_specs = (P(ROWS, ("z", "c")), P(("z", "c"), None, None), P(), P(("z", "c")))
    out_specs = P(ROWS, ("z", "c"))
    return jax.shard_map(local, mesh=fine, in_specs=in_specs, out_specs=out_specs, check_vma=False)
```

```python
import jax
import jax.numpy as jnp
from jax import lax
from jax.experimental import pallas as pl
from jax.experimental.pallas import tpu as pltpu
from jax.sharding import Mesh
from jax.sharding import PartitionSpec as P

ROWS = ("y", "h", "x")
HBM = pl.BlockSpec(memory_space=pltpu.HBM)
VMEM = pl.BlockSpec(memory_space=pltpu.VMEM)
SMEM = pl.BlockSpec(memory_space=pltpu.SMEM)
F32 = jnp.float32
BF16 = jnp.bfloat16
TRASH = 28

BUSY = 40 * 10**9


def params(mib):
    return pltpu.CompilerParams(vmem_limit_bytes=mib << 20)


def cost(flops, moved):
    return pl.CostEstimate(flops=flops, bytes_accessed=moved, transcendentals=0)


def shape(*dims, kind=F32):
    return jax.ShapeDtypeStruct(dims, kind)


def turn_kernel(c_ref, at_ref, buf, turned, sem, out_sem):
    loads, stores = [], []
    for t in range(4):
        span = pl.ds(128 * t, 128)
        loads.append(pltpu.make_async_copy(c_ref.at[:, span], buf.at[t], sem.at[t]))
        for plane in range(4):
            home = at_ref.at[pl.ds(8 * t, 8), plane]
            stores.append(pltpu.make_async_copy(turned.at[t], home, out_sem.at[t, plane]))
    for load in loads:
        load.start()
    for t, load in enumerate(loads):
        load.wait()
        turned[t] = jnp.transpose(buf[t]).reshape(8, 16, 128)
        for store in stores[4 * t : 4 * t + 4]:
            store.start()
    for store in stores:
        store.wait()


def halves(value):
    high = value.astype(BF16)
    return high, (value - high.astype(F32)).astype(BF16)


def blocks_kernel(h0, h1, out_ref, hbuf, sem):
    chunks = []
    for n in range(8):
        source = (h0, h1)[n // 4].at[pl.ds(8 * (n % 4), 8)]
        chunks.append(pltpu.make_async_copy(source, hbuf.at[pl.ds(8 * n, 8)], sem.at[n]))
    for chunk in chunks:
        chunk.start()
    for n, chunk in enumerate(chunks):
        chunk.wait()

        @pl.loop(0, 4)
        def _(step, n=n):
            for u in range(2):
                at = 8 * n + 2 * step + u
                high, low = halves(jnp.transpose(hbuf[at]))
                out_ref[at, :, :128] = high
                out_ref[at, :, 128:] = low


def product(left, block):
    rows = left.shape[0] // 2
    both = jnp.dot(left, block, preferred_element_type=F32)
    return both[:rows, :128] + (both[rows:, :128] + both[:rows, 128:])


def beta_kernel(
    where, cols, slots, w0, w1, w2, w3, blocks, keep_ref, send_ref,
    wide, stack, acc, list_ref, sem_w,
):
    z, core = where[2], where[3]
    loads = [
        pltpu.make_async_copy(w, wide.at[k], sem_w.at[k]) for k, w in enumerate((w0, w1, w2, w3))
    ]
    for load in loads:
        load.start()
    acc[...] = jnp.zeros_like(acc)

    def note(n, count):
        list_ref[count] = n
        return count + jnp.where(slots[n] < TRASH, 1, 0)

    count = lax.fori_loop(0, 64, note, 0)
    list_ref[count] = 0
    for k, load in enumerate(loads):
        home = 4 * jnp.bitwise_and(z - k + 4, 3)
        load.wait()
        for t in range(4):
            high, low = halves(wide[k, :, 128 * t : 128 * (t + 1)])
            stack[home + t, :128] = high
            stack[home + t, 128:] = low

    @pl.loop(0, lax.shift_right_logical(count + 1, 1))
    def _(step):
        terms = []
        for u in range(2):
            n = list_ref[2 * step + u]
            column = cols[n]
            left = stack[4 * lax.shift_right_logical(column, 3) + jnp.bitwise_and(column, 3)]
            slot = jnp.where(2 * step + u < count, slots[n], TRASH)
            terms.append((slot, product(left, blocks[n])))
        for slot, term in terms:
            acc[slot] += term

    for group in range(3):
        keep_ref[4 * group : 4 * group + 4] = acc[pl.ds(8 * group + 4 * core, 4)]
        send_ref[4 * group : 4 * group + 4] = acc[pl.ds(8 * group + 4 * (1 - core), 4)]
    mine = core == jnp.where(z == 0, 0, 1)
    edge = acc[24:28]
    keep_ref[12:] = jnp.where(mine, edge, 0.0)
    send_ref[12:] = jnp.where(mine, 0.0, edge)


def alpha_kernel(
    where, cols, owners, a_ref, source, after, o0, o1, o2, o3, acc, stack, blocks, sem
):
    z = where[2]
    chunks = []
    for n in range(4):
        span = pl.ds(16 * n, 16)
        chunks.append(pltpu.make_async_copy(source.at[span], blocks.at[span], sem.at[n]))
    for chunk in chunks:
        chunk.start()
    acc[...] = jnp.zeros_like(acc)

    @pl.loop(0, 32)
    def _(j):
        for k in range(4):
            home = pl.multiple_of(16 * jnp.bitwise_and(z + k, 3), 16)
            high, low = halves(a_ref[j, pl.ds(home, 16)])
            stack[j, 16 * k : 16 * k + 16] = high
            stack[j, 64 + 16 * k : 80 + 16 * k] = low

    for n, chunk in enumerate(chunks):
        chunk.wait()

        for first in range(16 * n, 16 * n + 16, 4):
            terms = []
            for spot in range(first, first + 4):
                terms.append((owners[spot], product(stack[cols[spot]], blocks[spot])))
            for owner, term in terms:
                acc[owner] += term

    for k, ref in enumerate((o0, o1, o2, o3)):
        ref[...] = acc[pl.ds(4 * z, 20), 16 * k : 16 * k + 16]


def strings_kernel(where, after, p0, p1, p2, p3, out_ref):
    z = where[2]
    out_ref[...] = jnp.zeros_like(out_ref)
    for k, part in enumerate((p0, p1, p2, p3)):
        out_ref[pl.ds(4 * jnp.bitwise_and(z - k + 4, 3), 20)] += part[...]


def cores_kernel(keep_ref, got_ref, own_ref, down_ref, up_ref, edge_ref, token_ref):
    token_ref[...] = jnp.zeros_like(token_ref)
    for n, ref in enumerate((own_ref, down_ref, up_ref, edge_ref)):
        ref[...] = keep_ref[4 * n : 4 * n + 4] + got_ref[4 * n : 4 * n + 4]


def planes_kernel(own_ref, down_ref, up_ref, edge_ref, out_ref, token_ref):
    token_ref[...] = jnp.zeros_like(token_ref)
    out_ref[...] = (own_ref[...] + down_ref[...]) + (up_ref[...] + edge_ref[...])


def final_kernel(back_ref, beta_ref, out_ref):
    for t in range(4):
        turned = jnp.transpose(back_ref[8 * t : 8 * (t + 1)].reshape(128, 128))
        out_ref[:, 128 * t : 128 * (t + 1)] = turned + beta_ref[t]


def swap(value):
    return lax.ppermute(value, "c", [(0, 1), (1, 0)])


def shift(value, by):
    return lax.ppermute(value, "z", [(i, (i + by) % 4) for i in range(4)])


def tables(hcount, hcols, z, c):
    cols = jnp.concatenate([hcols, swap(hcols)])
    marks = jnp.arange(32, dtype=jnp.int32)
    row_end = jnp.sum(jnp.where(marks[:, None] <= marks[None, :], hcount[:, None], 0), axis=0)
    shard = jnp.stack([2 * z + c, 2 * z + 1 - c])
    index = (32 * shard[:, None].astype(jnp.int32) + marks[None, :]).reshape(64)
    owners = jnp.sum((row_end[None, :] <= index[:, None]).astype(jnp.int32), axis=1)
    step = owners // 8 - z
    slots = owners % 8 + jnp.where(step == 0, 0, jnp.where(step == -1, 8, 16))
    slots = jnp.where(step == 2, 24 + owners - 16, jnp.where(step == -2, 24 + owners - 12, slots))
    return cols, owners, jnp.where((cols // 4) % 2 == c, slots, TRASH)


def call(kernel, outs, in_specs, *args, scratch=(), mib=16, work=(0, 1 << 20), space=VMEM):
    single = not isinstance(outs, tuple)
    return pl.pallas_call(
        kernel,
        out_shape=outs,
        in_specs=in_specs,
        out_specs=space if single else (space,) * len(outs),
        scratch_shapes=scratch,
        compiler_params=params(mib),
        cost_estimate=cost(*work),
        name=kernel.__name__,
    )(*args)


def local(coeffs, hblocks, hcount, hcols):
    z, c = lax.axis_index("z"), lax.axis_index("c")
    where = jnp.stack([z, z, z, c]).astype(jnp.int32)
    rows = [coeffs] + [shift(coeffs, k) for k in (1, 2, 3)]
    cols, owners, slots = tables(hcount, hcols, z, c)
    at = call(
        turn_kernel,
        shape(32, 4, 16, 128),
        [HBM],
        pltpu.with_memory_space_constraint(coeffs, pltpu.HBM),
        scratch=[
            pltpu.VMEM((4, 128, 128), F32),
            pltpu.VMEM((4, 8, 16, 128), F32),
            pltpu.SemaphoreType.DMA((4,)),
            pltpu.SemaphoreType.DMA((4, 4)),
        ],
        space=HBM,
    )
    moved = lax.all_to_all(at.reshape(2048, 128), ROWS + ("z",), 0, 0, tiled=True)

    blocks = call(
        blocks_kernel,
        shape(64, 128, 256, kind=BF16),
        [HBM] * 2,
        hblocks, swap(hblocks),
        scratch=[pltpu.VMEM((64, 128, 128), F32), pltpu.SemaphoreType.DMA((8,))],
        mib=24,
        work=(0, 8 << 20),
    )
    keep, send = call(
        beta_kernel,
        (shape(16, 128, 128), shape(16, 128, 128)),
        [SMEM] * 3 + [HBM] * 4 + [VMEM],
        where, cols, slots, *rows, blocks,
        scratch=[
            pltpu.VMEM((4, 128, 512), F32),
            pltpu.VMEM((16, 256, 128), BF16),
            pltpu.VMEM((TRASH + 1, 128, 128), F32),
            pltpu.SMEM((72,), jnp.int32),
            pltpu.SemaphoreType.DMA((4,)),
        ],
        mib=24,
        work=(BUSY, 7 << 20),
    )
    own, down, up, edge, token = call(
        cores_kernel,
        (shape(4, 128, 128),) * 4 + (shape(8, 128),),
        [VMEM] * 2,
        keep, swap(send),
    )
    down = lax.ppermute(down, ("z", "c"), [(3, 1), (4, 2), (5, 3), (6, 4), (7, 5)])
    up = lax.ppermute(up, ("z", "c"), [(0, 2), (1, 3), (2, 4), (3, 5), (4, 6)])
    edge = lax.ppermute(edge, ("z", "c"), [(0, 4), (7, 3)])
    beta, done = call(
        planes_kernel,
        (shape(4, 128, 128), shape(8, 128)),
        [VMEM] * 4,
        own, down, up, edge,
        work=(BUSY, 1 << 20),
    )
    parts = call(
        alpha_kernel,
        (shape(20, 16, 128),) * 4,
        [SMEM] * 3 + [VMEM, HBM, VMEM],
        where, cols, owners, moved.reshape(32, 64, 128),
        pltpu.with_memory_space_constraint(blocks, pltpu.HBM), token,
        scratch=[
            pltpu.VMEM((32, 64, 128), F32),
            pltpu.VMEM((32, 128, 128), BF16),
            pltpu.VMEM((64, 128, 256), BF16),
            pltpu.SemaphoreType.DMA((4,)),
        ],
        mib=24,
        work=(BUSY, 7 << 20),
    )
    far = shift(parts[2], 2)
    parts = [parts[0], shift(parts[1], 1), far, shift(parts[3], 3)]
    total = call(strings_kernel, shape(32, 16, 128), [SMEM] + [VMEM] * 5, where, done, *parts)
    back = lax.all_to_all(total, ROWS, 0, 0, tiled=True)
    return call(final_kernel, shape(128, 512), [VMEM] * 2, back, beta)


def solution(mesh):
    fine = Mesh(mesh.devices.reshape(4, 2, 4, 4, 2), ("y", "h", "x", "z", "c"))
    in_specs = (P(ROWS, ("z", "c")), P(("z", "c"), None, None), P(), P(("z", "c")))
    out_specs = P(ROWS, ("z", "c"))
    return jax.shard_map(local, mesh=fine, in_specs=in_specs, out_specs=out_specs, check_vma=False)
```

```python
import jax
import jax.numpy as jnp
from jax import lax
from jax.experimental import pallas as pl
from jax.experimental.pallas import tpu as pltpu
from jax.sharding import Mesh
from jax.sharding import PartitionSpec as P

ROWS = ("y", "h", "x")
HBM = pl.BlockSpec(memory_space=pltpu.HBM)
VMEM = pl.BlockSpec(memory_space=pltpu.VMEM)
SMEM = pl.BlockSpec(memory_space=pltpu.SMEM)
F32 = jnp.float32
BF16 = jnp.bfloat16
TRASH = 28

BUSY = 40 * 10**9


def params(mib):
    return pltpu.CompilerParams(vmem_limit_bytes=mib << 20)


def cost(flops, moved):
    return pl.CostEstimate(flops=flops, bytes_accessed=moved, transcendentals=0)


def shape(*dims, kind=F32):
    return jax.ShapeDtypeStruct(dims, kind)


def turn_kernel(c_ref, at_ref, buf, turned, sem, out_sem):
    loads, stores = [], []
    for t in range(4):
        span = pl.ds(128 * t, 128)
        loads.append(pltpu.make_async_copy(c_ref.at[:, span], buf.at[t], sem.at[t]))
        for plane in range(4):
            home = at_ref.at[pl.ds(8 * t, 8), plane]
            stores.append(pltpu.make_async_copy(turned.at[t], home, out_sem.at[t, plane]))
    for load in loads:
        load.start()
    for t, load in enumerate(loads):
        load.wait()
        turned[t] = jnp.transpose(buf[t]).reshape(8, 16, 128)
        for store in stores[4 * t : 4 * t + 4]:
            store.start()
    for store in stores:
        store.wait()


def halves(value):
    high = value.astype(BF16)
    return high, (value - high.astype(F32)).astype(BF16)


def blocks_kernel(h0, h1, out_ref, hbuf, sem):
    chunks = []
    for n in range(8):
        source = (h0, h1)[n // 4].at[pl.ds(8 * (n % 4), 8)]
        chunks.append(pltpu.make_async_copy(source, hbuf.at[pl.ds(8 * n, 8)], sem.at[n]))
    for chunk in chunks:
        chunk.start()
    for n, chunk in enumerate(chunks):
        chunk.wait()

        @pl.loop(0, 4)
        def _(step, n=n):
            for u in range(2):
                at = 8 * n + 2 * step + u
                high, low = halves(jnp.transpose(hbuf[at]))
                out_ref[at, :, :128] = high
                out_ref[at, :, 128:] = low


def product(left, block):
    rows = left.shape[0] // 2
    both = jnp.dot(left, block, preferred_element_type=F32)
    return both[:rows, :128] + (both[rows:, :128] + both[:rows, 128:])


def beta_kernel(
    where, cols, slots, w0, w1, w2, w3, blocks, keep_ref, send_ref,
    wide, stack, acc, list_ref, sem_w,
):
    z, core = where[2], where[3]
    loads = [
        pltpu.make_async_copy(w, wide.at[k], sem_w.at[k]) for k, w in enumerate((w0, w1, w2, w3))
    ]
    for load in loads:
        load.start()
    acc[...] = jnp.zeros_like(acc)

    def note(n, count):
        list_ref[count] = n
        return count + jnp.where(slots[n] < TRASH, 1, 0)

    count = lax.fori_loop(0, 64, note, 0)
    for u in range(3):
        list_ref[count + u] = 0
    for k, load in enumerate(loads):
        home = 4 * jnp.bitwise_and(z - k + 4, 3)
        load.wait()
        for t in range(4):
            high, low = halves(wide[k, :, 128 * t : 128 * (t + 1)])
            stack[home + t, :128] = high
            stack[home + t, 128:] = low

    @pl.loop(0, lax.shift_right_logical(count + 3, 2))
    def _(step):
        terms = []
        for u in range(4):
            n = list_ref[4 * step + u]
            column = cols[n]
            left = stack[4 * lax.shift_right_logical(column, 3) + jnp.bitwise_and(column, 3)]
            slot = jnp.where(4 * step + u < count, slots[n], TRASH)
            terms.append((slot, product(left, blocks[n])))
        for slot, term in terms:
            acc[slot] += term

    for group in range(3):
        keep_ref[4 * group : 4 * group + 4] = acc[pl.ds(8 * group + 4 * core, 4)]
        send_ref[4 * group : 4 * group + 4] = acc[pl.ds(8 * group + 4 * (1 - core), 4)]
    mine = core == jnp.where(z == 0, 0, 1)
    edge = acc[24:28]
    keep_ref[12:] = jnp.where(mine, edge, 0.0)
    send_ref[12:] = jnp.where(mine, 0.0, edge)


def alpha_kernel(
    where, cols, owners, a_ref, source, after, o0, o1, o2, o3, acc, stack, blocks, sem
):
    z = where[2]
    chunks = []
    for n in range(4):
        span = pl.ds(16 * n, 16)
        chunks.append(pltpu.make_async_copy(source.at[span], blocks.at[span], sem.at[n]))
    for chunk in chunks:
        chunk.start()
    acc[...] = jnp.zeros_like(acc)

    @pl.loop(0, 8)
    def _(step):
        for k in range(4):
            home = pl.multiple_of(16 * jnp.bitwise_and(z + k, 3), 16)
            for j in range(4):
                high, low = halves(a_ref[4 * step + j, pl.ds(home, 16)])
                stack[4 * step + j, 16 * k : 16 * k + 16] = high
                stack[4 * step + j, 64 + 16 * k : 80 + 16 * k] = low

    for n, chunk in enumerate(chunks):
        chunk.wait()

        for first in range(16 * n, 16 * n + 16, 4):
            terms = []
            for spot in range(first, first + 4):
                terms.append((owners[spot], product(stack[cols[spot]], blocks[spot])))
            for owner, term in terms:
                acc[owner] += term

    for k, ref in enumerate((o0, o1, o2, o3)):
        ref[...] = acc[pl.ds(4 * z, 20), 16 * k : 16 * k + 16]


def strings_kernel(where, after, p0, p1, p2, p3, out_ref):
    z = where[2]
    out_ref[...] = jnp.zeros_like(out_ref)
    for k, part in enumerate((p0, p1, p2, p3)):
        out_ref[pl.ds(4 * jnp.bitwise_and(z - k + 4, 3), 20)] += part[...]


def cores_kernel(keep_ref, got_ref, own_ref, down_ref, up_ref, edge_ref, token_ref):
    token_ref[...] = jnp.zeros_like(token_ref)
    for n, ref in enumerate((own_ref, down_ref, up_ref, edge_ref)):
        ref[...] = keep_ref[4 * n : 4 * n + 4] + got_ref[4 * n : 4 * n + 4]


def planes_kernel(own_ref, down_ref, up_ref, edge_ref, out_ref, token_ref):
    token_ref[...] = jnp.zeros_like(token_ref)
    out_ref[...] = (own_ref[...] + down_ref[...]) + (up_ref[...] + edge_ref[...])


def final_kernel(back_ref, beta_ref, out_ref):
    for t in range(4):
        turned = jnp.transpose(back_ref[8 * t : 8 * (t + 1)].reshape(128, 128))
        out_ref[:, 128 * t : 128 * (t + 1)] = turned + beta_ref[t]


def swap(value):
    return lax.ppermute(value, "c", [(0, 1), (1, 0)])


def shift(value, by):
    return lax.ppermute(value, "z", [(i, (i + by) % 4) for i in range(4)])


def tables(hcount, hcols, z, c):
    cols = jnp.concatenate([hcols, swap(hcols)])
    marks = jnp.arange(32, dtype=jnp.int32)
    row_end = jnp.sum(jnp.where(marks[:, None] <= marks[None, :], hcount[:, None], 0), axis=0)
    shard = jnp.stack([2 * z + c, 2 * z + 1 - c])
    index = (32 * shard[:, None].astype(jnp.int32) + marks[None, :]).reshape(64)
    owners = jnp.sum((row_end[None, :] <= index[:, None]).astype(jnp.int32), axis=1)
    step = owners // 8 - z
    slots = owners % 8 + jnp.where(step == 0, 0, jnp.where(step == -1, 8, 16))
    slots = jnp.where(step == 2, 24 + owners - 16, jnp.where(step == -2, 24 + owners - 12, slots))
    return cols, owners, jnp.where((cols // 4) % 2 == c, slots, TRASH)


def call(kernel, outs, in_specs, *args, scratch=(), mib=16, work=(0, 1 << 20), space=VMEM):
    single = not isinstance(outs, tuple)
    return pl.pallas_call(
        kernel,
        out_shape=outs,
        in_specs=in_specs,
        out_specs=space if single else (space,) * len(outs),
        scratch_shapes=scratch,
        compiler_params=params(mib),
        cost_estimate=cost(*work),
        name=kernel.__name__,
    )(*args)


def local(coeffs, hblocks, hcount, hcols):
    z, c = lax.axis_index("z"), lax.axis_index("c")
    where = jnp.stack([z, z, z, c]).astype(jnp.int32)
    rows = [coeffs] + [shift(coeffs, k) for k in (1, 2, 3)]
    cols, owners, slots = tables(hcount, hcols, z, c)
    at = call(
        turn_kernel,
        shape(32, 4, 16, 128),
        [HBM],
        pltpu.with_memory_space_constraint(coeffs, pltpu.HBM),
        scratch=[
            pltpu.VMEM((4, 128, 128), F32),
            pltpu.VMEM((4, 8, 16, 128), F32),
            pltpu.SemaphoreType.DMA((4,)),
            pltpu.SemaphoreType.DMA((4, 4)),
        ],
        space=HBM,
    )
    moved = lax.all_to_all(at.reshape(2048, 128), ROWS + ("z",), 0, 0, tiled=True)

    blocks = call(
        blocks_kernel,
        shape(64, 128, 256, kind=BF16),
        [HBM] * 2,
        hblocks, swap(hblocks),
        scratch=[pltpu.VMEM((64, 128, 128), F32), pltpu.SemaphoreType.DMA((8,))],
        mib=24,
        work=(0, 8 << 20),
    )
    keep, send = call(
        beta_kernel,
        (shape(16, 128, 128), shape(16, 128, 128)),
        [SMEM] * 3 + [HBM] * 4 + [VMEM],
        where, cols, slots, *rows, blocks,
        scratch=[
            pltpu.VMEM((4, 128, 512), F32),
            pltpu.VMEM((16, 256, 128), BF16),
            pltpu.VMEM((TRASH + 1, 128, 128), F32),
            pltpu.SMEM((72,), jnp.int32),
            pltpu.SemaphoreType.DMA((4,)),
        ],
        mib=24,
        work=(BUSY, 7 << 20),
    )
    own, down, up, edge, token = call(
        cores_kernel,
        (shape(4, 128, 128),) * 4 + (shape(8, 128),),
        [VMEM] * 2,
        keep, swap(send),
    )
    down = lax.ppermute(down, ("z", "c"), [(3, 1), (4, 2), (5, 3), (6, 4), (7, 5)])
    up = lax.ppermute(up, ("z", "c"), [(0, 2), (1, 3), (2, 4), (3, 5), (4, 6)])
    edge = lax.ppermute(edge, ("z", "c"), [(0, 4), (7, 3)])
    beta, done = call(
        planes_kernel,
        (shape(4, 128, 128), shape(8, 128)),
        [VMEM] * 4,
        own, down, up, edge,
        work=(BUSY, 1 << 20),
    )
    parts = call(
        alpha_kernel,
        (shape(20, 16, 128),) * 4,
        [SMEM] * 3 + [VMEM, HBM, VMEM],
        where, cols, owners, moved.reshape(32, 64, 128),
        pltpu.with_memory_space_constraint(blocks, pltpu.HBM), token,
        scratch=[
            pltpu.VMEM((32, 64, 128), F32),
            pltpu.VMEM((32, 128, 128), BF16),
            pltpu.VMEM((64, 128, 256), BF16),
            pltpu.SemaphoreType.DMA((4,)),
        ],
        mib=24,
        work=(BUSY, 7 << 20),
    )
    far = shift(parts[2], 2)
    parts = [parts[0], shift(parts[1], 1), far, shift(parts[3], 3)]
    total = call(strings_kernel, shape(32, 16, 128), [SMEM] + [VMEM] * 5, where, done, *parts)
    back = lax.all_to_all(total, ROWS, 0, 0, tiled=True)
    return call(final_kernel, shape(128, 512), [VMEM] * 2, back, beta)


def solution(mesh):
    fine = Mesh(mesh.devices.reshape(4, 2, 4, 4, 2), ("y", "h", "x", "z", "c"))
    in_specs = (P(ROWS, ("z", "c")), P(("z", "c"), None, None), P(), P(("z", "c")))
    out_specs = P(ROWS, ("z", "c"))
    return jax.shard_map(local, mesh=fine, in_specs=in_specs, out_specs=out_specs, check_vma=False)
```

```python
import jax
import jax.numpy as jnp
from jax import lax
from jax.experimental import pallas as pl
from jax.experimental.pallas import tpu as pltpu
from jax.sharding import Mesh
from jax.sharding import PartitionSpec as P

ROWS = ("y", "h", "x")
HBM = pl.BlockSpec(memory_space=pltpu.HBM)
VMEM = pl.BlockSpec(memory_space=pltpu.VMEM)
SMEM = pl.BlockSpec(memory_space=pltpu.SMEM)
F32 = jnp.float32
BF16 = jnp.bfloat16
TRASH = 28

BUSY = 40 * 10**9


def params(mib):
    return pltpu.CompilerParams(vmem_limit_bytes=mib << 20)


def cost(flops, moved):
    return pl.CostEstimate(flops=flops, bytes_accessed=moved, transcendentals=0)


def shape(*dims, kind=F32):
    return jax.ShapeDtypeStruct(dims, kind)


def turn_kernel(c_ref, at_ref, buf, turned, sem, out_sem):
    loads, stores = [], []
    for t in range(4):
        span = pl.ds(32 * t, 32)
        loads.append(pltpu.make_async_copy(c_ref.at[span], buf.at[span], sem.at[t]))
        for plane in range(4):
            home = at_ref.at[pl.ds(8 * t, 8), plane]
            stores.append(pltpu.make_async_copy(turned.at[t], home, out_sem.at[t, plane]))
    for load in loads:
        load.start()
    for load in loads:
        load.wait()
    for t in range(4):
        turned[t] = jnp.transpose(buf[:, 128 * t : 128 * (t + 1)]).reshape(8, 16, 128)
        for store in stores[4 * t : 4 * t + 4]:
            store.start()
    for store in stores:
        store.wait()


def halves(value):
    high = value.astype(BF16)
    return high, (value - high.astype(F32)).astype(BF16)


def blocks_kernel(h0, h1, out_ref, hbuf, sem):
    chunks = []
    for n in range(8):
        source = (h0, h1)[n // 4].at[pl.ds(8 * (n % 4), 8)]
        chunks.append(pltpu.make_async_copy(source, hbuf.at[pl.ds(8 * n, 8)], sem.at[n]))
    for chunk in chunks:
        chunk.start()
    for n, chunk in enumerate(chunks):
        chunk.wait()

        @pl.loop(0, 4)
        def _(step, n=n):
            for u in range(2):
                at = 8 * n + 2 * step + u
                high, low = halves(jnp.transpose(hbuf[at]))
                out_ref[at, :, :128] = high
                out_ref[at, :, 128:] = low


def product(left, block):
    rows = left.shape[0] // 2
    both = jnp.dot(left, block, preferred_element_type=F32)
    return both[:rows, :128] + (both[rows:, :128] + both[:rows, 128:])


def beta_kernel(
    where, cols, slots, w0, w1, w2, w3, blocks, keep_ref, send_ref,
    wide, stack, acc, list_ref, sem_w,
):
    z, core = where[2], where[3]
    loads = [
        pltpu.make_async_copy(w, wide.at[k], sem_w.at[k]) for k, w in enumerate((w0, w1, w2, w3))
    ]
    for load in loads:
        load.start()
    acc[...] = jnp.zeros_like(acc)

    def note(n, count):
        list_ref[count] = n
        return count + jnp.where(slots[n] < TRASH, 1, 0)

    count = lax.fori_loop(0, 64, note, 0)
    list_ref[count] = 0
    for k, load in enumerate(loads):
        home = 4 * jnp.bitwise_and(z - k + 4, 3)
        load.wait()
        for t in range(4):
            high, low = halves(wide[k, :, 128 * t : 128 * (t + 1)])
            stack[home + t, :128] = high
            stack[home + t, 128:] = low

    @pl.loop(0, lax.shift_right_logical(count + 1, 1))
    def _(step):
        terms = []
        for u in range(2):
            n = list_ref[2 * step + u]
            column = cols[n]
            left = stack[4 * lax.shift_right_logical(column, 3) + jnp.bitwise_and(column, 3)]
            slot = jnp.where(2 * step + u < count, slots[n], TRASH)
            terms.append((slot, product(left, blocks[n])))
        for slot, term in terms:
            acc[slot] += term

    for group in range(3):
        keep_ref[4 * group : 4 * group + 4] = acc[pl.ds(8 * group + 4 * core, 4)]
        send_ref[4 * group : 4 * group + 4] = acc[pl.ds(8 * group + 4 * (1 - core), 4)]
    mine = core == jnp.where(z == 0, 0, 1)
    edge = acc[24:28]
    keep_ref[12:] = jnp.where(mine, edge, 0.0)
    send_ref[12:] = jnp.where(mine, 0.0, edge)


def alpha_kernel(
    where, cols, owners, a_ref, source, after, o0, o1, o2, o3, acc, stack, blocks, sem
):
    z = where[2]
    chunks = []
    for n in range(4):
        span = pl.ds(16 * n, 16)
        chunks.append(pltpu.make_async_copy(source.at[span], blocks.at[span], sem.at[n]))
    for chunk in chunks:
        chunk.start()
    acc[...] = jnp.zeros_like(acc)

    @pl.loop(0, 32)
    def _(j):
        for k in range(4):
            home = pl.multiple_of(16 * jnp.bitwise_and(z + k, 3), 16)
            high, low = halves(a_ref[j, pl.ds(home, 16)])
            stack[j, 16 * k : 16 * k + 16] = high
            stack[j, 64 + 16 * k : 80 + 16 * k] = low

    for n, chunk in enumerate(chunks):
        chunk.wait()

        for first in range(16 * n, 16 * n + 16, 4):
            terms = []
            for spot in range(first, first + 4):
                terms.append((owners[spot], product(stack[cols[spot]], blocks[spot])))
            for owner, term in terms:
                acc[owner] += term

    for k, ref in enumerate((o0, o1, o2, o3)):
        ref[...] = acc[pl.ds(4 * z, 20), 16 * k : 16 * k + 16]


def strings_kernel(where, after, p0, p1, p2, p3, out_ref):
    z = where[2]
    out_ref[...] = jnp.zeros_like(out_ref)
    for k, part in enumerate((p0, p1, p2, p3)):
        out_ref[pl.ds(4 * jnp.bitwise_and(z - k + 4, 3), 20)] += part[...]


def cores_kernel(keep_ref, got_ref, own_ref, down_ref, up_ref, edge_ref, token_ref):
    token_ref[...] = jnp.zeros_like(token_ref)
    for n, ref in enumerate((own_ref, down_ref, up_ref, edge_ref)):
        ref[...] = keep_ref[4 * n : 4 * n + 4] + got_ref[4 * n : 4 * n + 4]


def planes_kernel(own_ref, down_ref, up_ref, edge_ref, out_ref, token_ref):
    token_ref[...] = jnp.zeros_like(token_ref)
    out_ref[...] = (own_ref[...] + down_ref[...]) + (up_ref[...] + edge_ref[...])


def final_kernel(back_ref, beta_ref, out_ref):
    for t in range(4):
        turned = jnp.transpose(back_ref[8 * t : 8 * (t + 1)].reshape(128, 128))
        out_ref[:, 128 * t : 128 * (t + 1)] = turned + beta_ref[t]


def swap(value):
    return lax.ppermute(value, "c", [(0, 1), (1, 0)])


def shift(value, by):
    return lax.ppermute(value, "z", [(i, (i + by) % 4) for i in range(4)])


def tables(hcount, hcols, z, c):
    cols = jnp.concatenate([hcols, swap(hcols)])
    marks = jnp.arange(32, dtype=jnp.int32)
    row_end = jnp.sum(jnp.where(marks[:, None] <= marks[None, :], hcount[:, None], 0), axis=0)
    shard = jnp.stack([2 * z + c, 2 * z + 1 - c])
    index = (32 * shard[:, None].astype(jnp.int32) + marks[None, :]).reshape(64)
    owners = jnp.sum((row_end[None, :] <= index[:, None]).astype(jnp.int32), axis=1)
    step = owners // 8 - z
    slots = owners % 8 + jnp.where(step == 0, 0, jnp.where(step == -1, 8, 16))
    slots = jnp.where(step == 2, 24 + owners - 16, jnp.where(step == -2, 24 + owners - 12, slots))
    return cols, owners, jnp.where((cols // 4) % 2 == c, slots, TRASH)


def call(kernel, outs, in_specs, *args, scratch=(), mib=16, work=(0, 1 << 20), space=VMEM):
    single = not isinstance(outs, tuple)
    return pl.pallas_call(
        kernel,
        out_shape=outs,
        in_specs=in_specs,
        out_specs=space if single else (space,) * len(outs),
        scratch_shapes=scratch,
        compiler_params=params(mib),
        cost_estimate=cost(*work),
        name=kernel.__name__,
    )(*args)


def local(coeffs, hblocks, hcount, hcols):
    z, c = lax.axis_index("z"), lax.axis_index("c")
    where = jnp.stack([z, z, z, c]).astype(jnp.int32)
    rows = [coeffs] + [shift(coeffs, k) for k in (1, 2, 3)]
    cols, owners, slots = tables(hcount, hcols, z, c)
    at = call(
        turn_kernel,
        shape(32, 4, 16, 128),
        [HBM],
        pltpu.with_memory_space_constraint(coeffs, pltpu.HBM),
        scratch=[
            pltpu.VMEM((128, 512), F32),
            pltpu.VMEM((4, 8, 16, 128), F32),
            pltpu.SemaphoreType.DMA((4,)),
            pltpu.SemaphoreType.DMA((4, 4)),
        ],
        space=HBM,
    )
    moved = lax.all_to_all(at.reshape(2048, 128), ROWS + ("z",), 0, 0, tiled=True)

    blocks = call(
        blocks_kernel,
        shape(64, 128, 256, kind=BF16),
        [HBM] * 2,
        hblocks, swap(hblocks),
        scratch=[pltpu.VMEM((64, 128, 128), F32), pltpu.SemaphoreType.DMA((8,))],
        mib=24,
        work=(0, 8 << 20),
    )
    keep, send = call(
        beta_kernel,
        (shape(16, 128, 128), shape(16, 128, 128)),
        [SMEM] * 3 + [HBM] * 4 + [VMEM],
        where, cols, slots, *rows, blocks,
        scratch=[
            pltpu.VMEM((4, 128, 512), F32),
            pltpu.VMEM((16, 256, 128), BF16),
            pltpu.VMEM((TRASH + 1, 128, 128), F32),
            pltpu.SMEM((72,), jnp.int32),
            pltpu.SemaphoreType.DMA((4,)),
        ],
        mib=24,
        work=(BUSY, 7 << 20),
    )
    own, down, up, edge, token = call(
        cores_kernel,
        (shape(4, 128, 128),) * 4 + (shape(8, 128),),
        [VMEM] * 2,
        keep, swap(send),
    )
    down = lax.ppermute(down, ("z", "c"), [(3, 1), (4, 2), (5, 3), (6, 4), (7, 5)])
    up = lax.ppermute(up, ("z", "c"), [(0, 2), (1, 3), (2, 4), (3, 5), (4, 6)])
    edge = lax.ppermute(edge, ("z", "c"), [(0, 4), (7, 3)])
    beta, done = call(
        planes_kernel,
        (shape(4, 128, 128), shape(8, 128)),
        [VMEM] * 4,
        own, down, up, edge,
        work=(BUSY, 1 << 20),
    )
    parts = call(
        alpha_kernel,
        (shape(20, 16, 128),) * 4,
        [SMEM] * 3 + [VMEM, HBM, VMEM],
        where, cols, owners, moved.reshape(32, 64, 128),
        pltpu.with_memory_space_constraint(blocks, pltpu.HBM), token,
        scratch=[
            pltpu.VMEM((32, 64, 128), F32),
            pltpu.VMEM((32, 128, 128), BF16),
            pltpu.VMEM((64, 128, 256), BF16),
            pltpu.SemaphoreType.DMA((4,)),
        ],
        mib=24,
        work=(BUSY, 7 << 20),
    )
    far = shift(parts[2], 2)
    parts = [parts[0], shift(parts[1], 1), far, shift(parts[3], 3)]
    total = call(strings_kernel, shape(32, 16, 128), [SMEM] + [VMEM] * 5, where, done, *parts)
    back = lax.all_to_all(total, ROWS, 0, 0, tiled=True)
    return call(final_kernel, shape(128, 512), [VMEM] * 2, back, beta)


def solution(mesh):
    fine = Mesh(mesh.devices.reshape(4, 2, 4, 4, 2), ("y", "h", "x", "z", "c"))
    in_specs = (P(ROWS, ("z", "c")), P(("z", "c"), None, None), P(), P(("z", "c")))
    out_specs = P(ROWS, ("z", "c"))
    return jax.shard_map(local, mesh=fine, in_specs=in_specs, out_specs=out_specs, check_vma=False)
```

```python
import jax
import jax.numpy as jnp
from jax import lax
from jax.experimental import pallas as pl
from jax.experimental.pallas import tpu as pltpu
from jax.sharding import Mesh
from jax.sharding import PartitionSpec as P

ROWS = ("y", "h", "x")
HBM = pl.BlockSpec(memory_space=pltpu.HBM)
VMEM = pl.BlockSpec(memory_space=pltpu.VMEM)
SMEM = pl.BlockSpec(memory_space=pltpu.SMEM)
F32 = jnp.float32
BF16 = jnp.bfloat16
TRASH = 28

BUSY = 40 * 10**9


def params(mib):
    return pltpu.CompilerParams(vmem_limit_bytes=mib << 20)


def cost(flops, moved):
    return pl.CostEstimate(flops=flops, bytes_accessed=moved, transcendentals=0)


def shape(*dims, kind=F32):
    return jax.ShapeDtypeStruct(dims, kind)


def turn_kernel(c_ref, at_ref, buf, turned, sem, out_sem):
    loads, stores = [], []
    for t in range(4):
        span = pl.ds(32 * t, 32)
        loads.append(pltpu.make_async_copy(c_ref.at[span], buf.at[span], sem.at[t]))
        for plane in range(4):
            home = at_ref.at[pl.ds(8 * t, 8), plane]
            stores.append(pltpu.make_async_copy(turned.at[t], home, out_sem.at[t, plane]))
    for load in loads:
        load.start()
    for load in loads:
        load.wait()
    for t in range(4):
        turned[t] = jnp.transpose(buf[:, 128 * t : 128 * (t + 1)]).reshape(8, 16, 128)
        for store in stores[4 * t : 4 * t + 4]:
            store.start()
    for store in stores:
        store.wait()


def halves(value):
    high = value.astype(BF16)
    return high, (value - high.astype(F32)).astype(BF16)


def blocks_kernel(h0, h1, out_ref, hbuf, sem):
    chunks = []
    for n in range(8):
        source = (h0, h1)[n // 4].at[pl.ds(8 * (n % 4), 8)]
        chunks.append(pltpu.make_async_copy(source, hbuf.at[pl.ds(8 * n, 8)], sem.at[n]))
    for chunk in chunks:
        chunk.start()
    for n, chunk in enumerate(chunks):
        chunk.wait()

        @pl.loop(0, 4)
        def _(step, n=n):
            for u in range(2):
                at = 8 * n + 2 * step + u
                high, low = halves(jnp.transpose(hbuf[at]))
                out_ref[at, :, :128] = high
                out_ref[at, :, 128:] = low


def product(left, block):
    rows = left.shape[0] // 2
    both = jnp.dot(left, block, preferred_element_type=F32)
    return both[:rows, :128] + (both[rows:, :128] + both[:rows, 128:])


def beta_kernel(
    where, cols, slots, w0, w1, w2, w3, blocks, keep_ref, send_ref,
    wide, stack, acc, list_ref, sem_w,
):
    z, core = where[2], where[3]
    loads = [
        pltpu.make_async_copy(w, wide.at[k], sem_w.at[k]) for k, w in enumerate((w0, w1, w2, w3))
    ]
    for load in loads:
        load.start()
    acc[...] = jnp.zeros_like(acc)

    def note(n, count):
        list_ref[count] = n
        return count + jnp.where(slots[n] < TRASH, 1, 0)

    count = lax.fori_loop(0, 64, note, 0)
    for u in range(3):
        list_ref[count + u] = 0
    for k, load in enumerate(loads):
        home = 4 * jnp.bitwise_and(z - k + 4, 3)
        load.wait()
        for t in range(4):
            high, low = halves(wide[k, :, 128 * t : 128 * (t + 1)])
            stack[home + t, :128] = high
            stack[home + t, 128:] = low

    @pl.loop(0, lax.shift_right_logical(count + 3, 2))
    def _(step):
        terms = []
        for u in range(4):
            n = list_ref[4 * step + u]
            column = cols[n]
            left = stack[4 * lax.shift_right_logical(column, 3) + jnp.bitwise_and(column, 3)]
            slot = jnp.where(4 * step + u < count, slots[n], TRASH)
            terms.append((slot, product(left, blocks[n])))
        for slot, term in terms:
            acc[slot] += term

    for group in range(3):
        keep_ref[4 * group : 4 * group + 4] = acc[pl.ds(8 * group + 4 * core, 4)]
        send_ref[4 * group : 4 * group + 4] = acc[pl.ds(8 * group + 4 * (1 - core), 4)]
    mine = core == jnp.where(z == 0, 0, 1)
    edge = acc[24:28]
    keep_ref[12:] = jnp.where(mine, edge, 0.0)
    send_ref[12:] = jnp.where(mine, 0.0, edge)


def alpha_kernel(
    where, cols, owners, a_ref, source, after, o0, o1, o2, o3, acc, stack, blocks, sem
):
    z = where[2]
    chunks = []
    for n in range(4):
        span = pl.ds(16 * n, 16)
        chunks.append(pltpu.make_async_copy(source.at[span], blocks.at[span], sem.at[n]))
    for chunk in chunks:
        chunk.start()
    acc[...] = jnp.zeros_like(acc)

    @pl.loop(0, 32)
    def _(j):
        for k in range(4):
            home = pl.multiple_of(16 * jnp.bitwise_and(z + k, 3), 16)
            high, low = halves(a_ref[j, pl.ds(home, 16)])
            stack[j, 16 * k : 16 * k + 16] = high
            stack[j, 64 + 16 * k : 80 + 16 * k] = low

    for n, chunk in enumerate(chunks):
        chunk.wait()

        for first in range(16 * n, 16 * n + 16, 4):
            terms = []
            for spot in range(first, first + 4):
                terms.append((owners[spot], product(stack[cols[spot]], blocks[spot])))
            for owner, term in terms:
                acc[owner] += term

    for k, ref in enumerate((o0, o1, o2, o3)):
        ref[...] = acc[pl.ds(4 * z, 20), 16 * k : 16 * k + 16]


def strings_kernel(where, after, p0, p1, p2, p3, out_ref):
    z = where[2]
    out_ref[...] = jnp.zeros_like(out_ref)
    for k, part in enumerate((p0, p1, p2, p3)):
        out_ref[pl.ds(4 * jnp.bitwise_and(z - k + 4, 3), 20)] += part[...]


def cores_kernel(keep_ref, got_ref, own_ref, down_ref, up_ref, edge_ref, token_ref):
    token_ref[...] = jnp.zeros_like(token_ref)
    for n, ref in enumerate((own_ref, down_ref, up_ref, edge_ref)):
        ref[...] = keep_ref[4 * n : 4 * n + 4] + got_ref[4 * n : 4 * n + 4]


def planes_kernel(own_ref, down_ref, up_ref, edge_ref, out_ref, token_ref):
    token_ref[...] = jnp.zeros_like(token_ref)
    out_ref[...] = (own_ref[...] + down_ref[...]) + (up_ref[...] + edge_ref[...])


def final_kernel(back_ref, beta_ref, out_ref):
    for t in range(4):
        turned = jnp.transpose(back_ref[8 * t : 8 * (t + 1)].reshape(128, 128))
        out_ref[:, 128 * t : 128 * (t + 1)] = turned + beta_ref[t]


def swap(value):
    return lax.ppermute(value, "c", [(0, 1), (1, 0)])


def shift(value, by):
    return lax.ppermute(value, "z", [(i, (i + by) % 4) for i in range(4)])


def tables(hcount, hcols, z, c):
    cols = jnp.concatenate([hcols, swap(hcols)])
    marks = jnp.arange(32, dtype=jnp.int32)
    row_end = jnp.sum(jnp.where(marks[:, None] <= marks[None, :], hcount[:, None], 0), axis=0)
    shard = jnp.stack([2 * z + c, 2 * z + 1 - c])
    index = (32 * shard[:, None].astype(jnp.int32) + marks[None, :]).reshape(64)
    owners = jnp.sum((row_end[None, :] <= index[:, None]).astype(jnp.int32), axis=1)
    step = owners // 8 - z
    slots = owners % 8 + jnp.where(step == 0, 0, jnp.where(step == -1, 8, 16))
    slots = jnp.where(step == 2, 24 + owners - 16, jnp.where(step == -2, 24 + owners - 12, slots))
    return cols, owners, jnp.where((cols // 4) % 2 == c, slots, TRASH)


def call(kernel, outs, in_specs, *args, scratch=(), mib=16, work=(0, 1 << 20), space=VMEM):
    single = not isinstance(outs, tuple)
    return pl.pallas_call(
        kernel,
        out_shape=outs,
        in_specs=in_specs,
        out_specs=space if single else (space,) * len(outs),
        scratch_shapes=scratch,
        compiler_params=params(mib),
        cost_estimate=cost(*work),
        name=kernel.__name__,
    )(*args)


def local(coeffs, hblocks, hcount, hcols):
    z, c = lax.axis_index("z"), lax.axis_index("c")
    where = jnp.stack([z, z, z, c]).astype(jnp.int32)
    across = shift(coeffs, 2)
    rows = [coeffs, shift(coeffs, 1), across, shift(coeffs, 3)]
    cols, owners, slots = tables(hcount, hcols, z, c)
    at = call(
        turn_kernel,
        shape(32, 4, 16, 128),
        [HBM],
        pltpu.with_memory_space_constraint(coeffs, pltpu.HBM),
        scratch=[
            pltpu.VMEM((128, 512), F32),
            pltpu.VMEM((4, 8, 16, 128), F32),
            pltpu.SemaphoreType.DMA((4,)),
            pltpu.SemaphoreType.DMA((4, 4)),
        ],
        space=HBM,
    )
    moved = lax.all_to_all(at.reshape(2048, 128), ROWS + ("z",), 0, 0, tiled=True)

    blocks = call(
        blocks_kernel,
        shape(64, 128, 256, kind=BF16),
        [HBM] * 2,
        hblocks, swap(hblocks),
        scratch=[pltpu.VMEM((64, 128, 128), F32), pltpu.SemaphoreType.DMA((8,))],
        mib=24,
        work=(0, 8 << 20),
    )
    keep, send = call(
        beta_kernel,
        (shape(16, 128, 128), shape(16, 128, 128)),
        [SMEM] * 3 + [HBM] * 4 + [VMEM],
        where, cols, slots, *rows, blocks,
        scratch=[
            pltpu.VMEM((4, 128, 512), F32),
            pltpu.VMEM((16, 256, 128), BF16),
            pltpu.VMEM((TRASH + 1, 128, 128), F32),
            pltpu.SMEM((72,), jnp.int32),
            pltpu.SemaphoreType.DMA((4,)),
        ],
        mib=24,
        work=(BUSY, 7 << 20),
    )
    own, down, up, edge, token = call(
        cores_kernel,
        (shape(4, 128, 128),) * 4 + (shape(8, 128),),
        [VMEM] * 2,
        keep, swap(send),
    )
    down = lax.ppermute(down, ("z", "c"), [(3, 1), (4, 2), (5, 3), (6, 4), (7, 5)])
    up = lax.ppermute(up, ("z", "c"), [(0, 2), (1, 3), (2, 4), (3, 5), (4, 6)])
    edge = lax.ppermute(edge, ("z", "c"), [(0, 4), (7, 3)])
    beta, done = call(
        planes_kernel,
        (shape(4, 128, 128), shape(8, 128)),
        [VMEM] * 4,
        own, down, up, edge,
        work=(BUSY, 1 << 20),
    )
    parts = call(
        alpha_kernel,
        (shape(20, 16, 128),) * 4,
        [SMEM] * 3 + [VMEM, HBM, VMEM],
        where, cols, owners, moved.reshape(32, 64, 128),
        pltpu.with_memory_space_constraint(blocks, pltpu.HBM), token,
        scratch=[
            pltpu.VMEM((32, 64, 128), F32),
            pltpu.VMEM((32, 128, 128), BF16),
            pltpu.VMEM((64, 128, 256), BF16),
            pltpu.SemaphoreType.DMA((4,)),
        ],
        mib=24,
        work=(BUSY, 7 << 20),
    )
    far = shift(parts[2], 2)
    parts = [parts[0], shift(parts[1], 1), far, shift(parts[3], 3)]
    total = call(strings_kernel, shape(32, 16, 128), [SMEM] + [VMEM] * 5, where, done, *parts)
    back = lax.all_to_all(total, ROWS, 0, 0, tiled=True)
    return call(final_kernel, shape(128, 512), [VMEM] * 2, back, beta)


def solution(mesh):
    fine = Mesh(mesh.devices.reshape(4, 2, 4, 4, 2), ("y", "h", "x", "z", "c"))
    in_specs = (P(ROWS, ("z", "c")), P(("z", "c"), None, None), P(), P(("z", "c")))
    out_specs = P(ROWS, ("z", "c"))
    return jax.shard_map(local, mesh=fine, in_specs=in_specs, out_specs=out_specs, check_vma=False)
```

```python
import jax
import jax.numpy as jnp
from jax import lax
from jax.experimental import pallas as pl
from jax.experimental.pallas import tpu as pltpu
from jax.sharding import Mesh
from jax.sharding import PartitionSpec as P

ROWS = ("y", "h", "x")
HBM = pl.BlockSpec(memory_space=pltpu.HBM)
VMEM = pl.BlockSpec(memory_space=pltpu.VMEM)
SMEM = pl.BlockSpec(memory_space=pltpu.SMEM)
F32 = jnp.float32
BF16 = jnp.bfloat16
TRASH = 28

BUSY = 40 * 10**9


def params(mib):
    return pltpu.CompilerParams(vmem_limit_bytes=mib << 20)


def cost(flops, moved):
    return pl.CostEstimate(flops=flops, bytes_accessed=moved, transcendentals=0)


def shape(*dims, kind=F32):
    return jax.ShapeDtypeStruct(dims, kind)


def turn_kernel(c_ref, at_ref, buf, turned, sem, out_sem):
    loads, stores = [], []
    for t in range(4):
        span = pl.ds(128 * t, 128)
        loads.append(pltpu.make_async_copy(c_ref.at[:, span], buf.at[t], sem.at[t]))
        for plane in range(4):
            home = at_ref.at[pl.ds(8 * t, 8), plane]
            stores.append(pltpu.make_async_copy(turned.at[t], home, out_sem.at[t, plane]))
    for load in loads:
        load.start()
    for t, load in enumerate(loads):
        load.wait()
        turned[t] = jnp.transpose(buf[t]).reshape(8, 16, 128)
        for store in stores[4 * t : 4 * t + 4]:
            store.start()
    for store in stores:
        store.wait()


def halves(value):
    high = value.astype(BF16)
    return high, (value - high.astype(F32)).astype(BF16)


def blocks_kernel(h0, h1, out_ref, hbuf, sem):
    chunks = []
    for n in range(8):
        source = (h0, h1)[n // 4].at[pl.ds(8 * (n % 4), 8)]
        chunks.append(pltpu.make_async_copy(source, hbuf.at[pl.ds(8 * n, 8)], sem.at[n]))
    for chunk in chunks:
        chunk.start()
    for n, chunk in enumerate(chunks):
        chunk.wait()

        @pl.loop(0, 4)
        def _(step, n=n):
            for u in range(2):
                at = 8 * n + 2 * step + u
                high, low = halves(jnp.transpose(hbuf[at]))
                out_ref[at, :, :128] = high
                out_ref[at, :, 128:] = low


def product(left, block):
    rows = left.shape[0] // 2
    both = jnp.dot(left, block, preferred_element_type=F32)
    return both[:rows, :128] + (both[rows:, :128] + both[:rows, 128:])


def beta_kernel(
    where, cols, slots, w0, w1, w2, w3, blocks, keep_ref, send_ref,
    wide, stack, acc, list_ref, sem_w,
):
    z, core = where[2], where[3]
    loads = [
        pltpu.make_async_copy(w, wide.at[k], sem_w.at[k]) for k, w in enumerate((w0, w1, w2, w3))
    ]
    for load in loads:
        load.start()
    acc[...] = jnp.zeros_like(acc)

    def note(n, count):
        list_ref[count] = n
        return count + jnp.where(slots[n] < TRASH, 1, 0)

    count = lax.fori_loop(0, 64, note, 0)
    list_ref[count] = 0
    for k, load in enumerate(loads):
        home = 4 * jnp.bitwise_and(z - k + 4, 3)
        load.wait()
        for t in range(4):
            high, low = halves(wide[k, :, 128 * t : 128 * (t + 1)])
            stack[home + t, :128] = high
            stack[home + t, 128:] = low

    @pl.loop(0, lax.shift_right_logical(count + 1, 1))
    def _(step):
        terms = []
        for u in range(2):
            n = list_ref[2 * step + u]
            column = cols[n]
            left = stack[4 * lax.shift_right_logical(column, 3) + jnp.bitwise_and(column, 3)]
            slot = jnp.where(2 * step + u < count, slots[n], TRASH)
            terms.append((slot, product(left, blocks[n])))
        for slot, term in terms:
            acc[slot] += term

    for group in range(3):
        keep_ref[4 * group : 4 * group + 4] = acc[pl.ds(8 * group + 4 * core, 4)]
        send_ref[4 * group : 4 * group + 4] = acc[pl.ds(8 * group + 4 * (1 - core), 4)]
    mine = core == jnp.where(z == 0, 0, 1)
    edge = acc[24:28]
    keep_ref[12:] = jnp.where(mine, edge, 0.0)
    send_ref[12:] = jnp.where(mine, 0.0, edge)


def alpha_kernel(
    where, cols, owners, a_ref, source, after, o0, o1, o2, o3, acc, stack, blocks, sem
):
    z = where[2]
    chunks = []
    for n in range(4):
        span = pl.ds(16 * n, 16)
        chunks.append(pltpu.make_async_copy(source.at[span], blocks.at[span], sem.at[n]))
    for chunk in chunks:
        chunk.start()
    acc[...] = jnp.zeros_like(acc)

    @pl.loop(0, 32)
    def _(j):
        for k in range(4):
            home = pl.multiple_of(16 * jnp.bitwise_and(z + k, 3), 16)
            high, low = halves(a_ref[j, pl.ds(home, 16)])
            stack[j, 16 * k : 16 * k + 16] = high
            stack[j, 64 + 16 * k : 80 + 16 * k] = low

    for n, chunk in enumerate(chunks):
        chunk.wait()

        for first in range(16 * n, 16 * n + 16, 4):
            terms = []
            for spot in range(first, first + 4):
                terms.append((owners[spot], product(stack[cols[spot]], blocks[spot])))
            for owner, term in terms:
                acc[owner] += term

    for k, ref in enumerate((o0, o1, o2, o3)):
        ref[...] = acc[pl.ds(4 * z, 20), 16 * k : 16 * k + 16]


def strings_kernel(where, after, p0, p1, p2, p3, out_ref):
    z = where[2]
    out_ref[...] = jnp.zeros_like(out_ref)
    for k, part in enumerate((p0, p1, p2, p3)):
        out_ref[pl.ds(4 * jnp.bitwise_and(z - k + 4, 3), 20)] += part[...]


def cores_kernel(keep_ref, got_ref, own_ref, down_ref, up_ref, edge_ref, token_ref):
    token_ref[...] = jnp.zeros_like(token_ref)
    for n, ref in enumerate((own_ref, down_ref, up_ref, edge_ref)):
        ref[...] = keep_ref[4 * n : 4 * n + 4] + got_ref[4 * n : 4 * n + 4]


def planes_kernel(own_ref, down_ref, up_ref, edge_ref, out_ref, token_ref):
    token_ref[...] = jnp.zeros_like(token_ref)
    out_ref[...] = (own_ref[...] + down_ref[...]) + (up_ref[...] + edge_ref[...])


def final_kernel(back_ref, beta_ref, out_ref):
    for t in range(4):
        turned = jnp.transpose(back_ref[8 * t : 8 * (t + 1)].reshape(128, 128))
        out_ref[:, 128 * t : 128 * (t + 1)] = turned + beta_ref[t]


def swap(value):
    return lax.ppermute(value, "c", [(0, 1), (1, 0)])


def shift(value, by):
    return lax.ppermute(value, "z", [(i, (i + by) % 4) for i in range(4)])


def tables(hcount, hcols, z, c):
    cols = jnp.concatenate([hcols, swap(hcols)])
    marks = jnp.arange(32, dtype=jnp.int32)
    row_end = jnp.sum(jnp.where(marks[:, None] <= marks[None, :], hcount[:, None], 0), axis=0)
    shard = jnp.stack([2 * z + c, 2 * z + 1 - c])
    index = (32 * shard[:, None].astype(jnp.int32) + marks[None, :]).reshape(64)
    owners = jnp.sum((row_end[None, :] <= index[:, None]).astype(jnp.int32), axis=1)
    step = owners // 8 - z
    slots = owners % 8 + jnp.where(step == 0, 0, jnp.where(step == -1, 8, 16))
    slots = jnp.where(step == 2, 24 + owners - 16, jnp.where(step == -2, 24 + owners - 12, slots))
    return cols, owners, jnp.where((cols // 4) % 2 == c, slots, TRASH)


def call(kernel, outs, in_specs, *args, scratch=(), mib=16, work=(0, 1 << 20), space=VMEM):
    single = not isinstance(outs, tuple)
    return pl.pallas_call(
        kernel,
        out_shape=outs,
        in_specs=in_specs,
        out_specs=space if single else (space,) * len(outs),
        scratch_shapes=scratch,
        compiler_params=params(mib),
        cost_estimate=cost(*work),
        name=kernel.__name__,
    )(*args)


def local(coeffs, hblocks, hcount, hcols):
    z, c = lax.axis_index("z"), lax.axis_index("c")
    where = jnp.stack([z, z, z, c]).astype(jnp.int32)
    rows = [coeffs] + [shift(coeffs, k) for k in (1, 2, 3)]
    cols, owners, slots = tables(hcount, hcols, z, c)
    at = call(
        turn_kernel,
        shape(32, 4, 16, 128),
        [HBM],
        pltpu.with_memory_space_constraint(coeffs, pltpu.HBM),
        scratch=[
            pltpu.VMEM((4, 128, 128), F32),
            pltpu.VMEM((4, 8, 16, 128), F32),
            pltpu.SemaphoreType.DMA((4,)),
            pltpu.SemaphoreType.DMA((4, 4)),
        ],
        space=HBM,
    )
    moved = lax.all_to_all(at.reshape(2048, 128), ROWS + ("z",), 0, 0, tiled=True)

    blocks = call(
        blocks_kernel,
        shape(64, 128, 256, kind=BF16),
        [HBM] * 2,
        hblocks, swap(hblocks),
        scratch=[pltpu.VMEM((64, 128, 128), F32), pltpu.SemaphoreType.DMA((8,))],
        mib=24,
        work=(0, 8 << 20),
    )
    keep, send = call(
        beta_kernel,
        (shape(16, 128, 128), shape(16, 128, 128)),
        [SMEM] * 3 + [HBM] * 4 + [VMEM],
        where, cols, slots, *rows, blocks,
        scratch=[
            pltpu.VMEM((4, 128, 512), F32),
            pltpu.VMEM((16, 256, 128), BF16),
            pltpu.VMEM((TRASH + 1, 128, 128), F32),
            pltpu.SMEM((72,), jnp.int32),
            pltpu.SemaphoreType.DMA((4,)),
        ],
        mib=24,
        work=(BUSY, 7 << 20),
    )
    own, down, up, edge, token = call(
        cores_kernel,
        (shape(4, 128, 128),) * 4 + (shape(8, 128),),
        [VMEM] * 2,
        keep, swap(send),
    )
    edge = lax.ppermute(edge, ("z", "c"), [(0, 4), (7, 3)])
    down = lax.ppermute(down, ("z", "c"), [(3, 1), (4, 2), (5, 3), (6, 4), (7, 5)])
    up = lax.ppermute(up, ("z", "c"), [(0, 2), (1, 3), (2, 4), (3, 5), (4, 6)])
    beta, done = call(
        planes_kernel,
        (shape(4, 128, 128), shape(8, 128)),
        [VMEM] * 4,
        own, down, up, edge,
        work=(BUSY, 1 << 20),
    )
    parts = call(
        alpha_kernel,
        (shape(20, 16, 128),) * 4,
        [SMEM] * 3 + [VMEM, HBM, VMEM],
        where, cols, owners, moved.reshape(32, 64, 128),
        pltpu.with_memory_space_constraint(blocks, pltpu.HBM), token,
        scratch=[
            pltpu.VMEM((32, 64, 128), F32),
            pltpu.VMEM((32, 128, 128), BF16),
            pltpu.VMEM((64, 128, 256), BF16),
            pltpu.SemaphoreType.DMA((4,)),
        ],
        mib=24,
        work=(BUSY, 7 << 20),
    )
    far = shift(parts[2], 2)
    parts = [parts[0], shift(parts[1], 1), far, shift(parts[3], 3)]
    total = call(strings_kernel, shape(32, 16, 128), [SMEM] + [VMEM] * 5, where, done, *parts)
    back = lax.all_to_all(total, ROWS, 0, 0, tiled=True)
    return call(final_kernel, shape(128, 512), [VMEM] * 2, back, beta)


def solution(mesh):
    fine = Mesh(mesh.devices.reshape(4, 2, 4, 4, 2), ("y", "h", "x", "z", "c"))
    in_specs = (P(ROWS, ("z", "c")), P(("z", "c"), None, None), P(), P(("z", "c")))
    out_specs = P(ROWS, ("z", "c"))
    return jax.shard_map(local, mesh=fine, in_specs=in_specs, out_specs=out_specs, check_vma=False)
```
